128 devices in a mesh: mode: 2 (over x_hi), scan: 64 (over y, z, x_lo, core).
Axes of the slice: x: 4 (x_hi: 2, x_lo: 2; x = x_hi * 2 + x_lo), y: 4, z: 4, core: 2. Of those that a mesh axis runs over, the one named last changes fastest.
Arguments:
- object_field: float32 [2, 32768, 1024], P(None, 'scan'), may hold values from -4.2 to 4.2
- probe: bfloat16 [2, 12, 512, 512], P(None, 'mode'), may hold values from -1.796875 to 1.796875
- patterns: float32 [64, 512, 512], P('scan'), may hold values from 0.2 to 6
- row_shift: int32 [64], P('scan'), may hold values from 0 to 1
- col_start: int32 [64], P('scan'), may hold values from 0 to 2
- mixing: int32 [12, 12], replicated, may hold values from -5 to 20, as said below
Outputs:
- object_new: float32 [2, 32768, 1024], P(None, 'scan')
- probe_new: bfloat16 [2, 12, 512, 512], P(None, 'mode', 'scan')
The draws below stay inside these ranges and needn't reach their ends.
Inputs may be any that keep to these rules, and one draw needn't show every extreme that they name: `mixing`: diagonal entries are 12 to 20, the others -5 to 5.
All inputs are finite; a program needn't handle non-finite values.
Results may differ from the reference program's by a relative error of at most 0.0095.
The reference program's roundings to bfloat16 on the way count: a program that leaves them out, or rounds other values in their place, can miss the bound.
Values sent between devices are 32-bit elements; how exact they have to be, the bound alone decides.
No kernel may reach another device: no remote copies, remote signals or barrier semaphores. Data moves between devices by JAX's collectives and lax.ppermute only.
A program may use at most 128 MiB of HBM per device.

```python
import math
import jax
import jax.numpy as jnp
from jax import lax

TILE = 512
MODES = 12
OBJ_COLS = 1024
P_DEV = 1
HALF = 256
POS = 64
OBJ_ROWS = 32768


def draw_mixing(key, part):
    first_key, second_key = jax.random.split(jax.random.fold_in(key, 7))
    off_values = jax.random.randint(first_key, (MODES, MODES), -5, 6, dtype=jnp.int32)
    diag_values = jax.random.randint(second_key, (MODES,), 12, 21, dtype=jnp.int32)
    identity = jnp.eye(MODES, dtype=jnp.int32)
    return off_values * (1 - identity) + diag_values[:, None] * identity


def place_ends(drawn, key, least, top_value):
    extent = drawn.shape
    spot = [jax.random.randint(jax.random.fold_in(key, axis), (), 0, extent[axis]) for axis in range(len(extent))]
    drawn = drawn.at[tuple(spot)].set(least)
    longest = extent.index(max(extent))
    spot[longest] = (spot[longest] + 1) % extent[longest]
    return drawn.at[tuple(spot)].set(top_value)


def steps_of(stream_key, extent, shards, smallest, top_value):
    def one(dim, shards_of):
        heights = jax.random.uniform(jax.random.fold_in(jax.random.fold_in(stream_key, 6), dim), (shards_of,), jnp.float32, smallest / len(shards), top_value / len(shards))
        return jnp.repeat(jnp.exp(heights), extent[dim] // shards_of).reshape((-1,) + (1,) * (len(extent) - dim - 1))

    gain = one(*shards[0])
    for cut in shards[1:]:
        gain = gain * one(*cut)
    return gain


def scatter_about(own_key, dims, width, limit, pieces=(), kind=jnp.bfloat16):
    entries = jax.random.normal(own_key, dims, jnp.float32) * width
    if len(pieces) > 0:
        entries = steps_of(own_key, dims, pieces, -0.22, 0.18) * entries
    return jnp.clip(entries, min=-limit, max=limit).astype(kind)


def setup_inputs(seed: int = 0) -> dict:
    keys = jax.random.split(jax.random.key(seed), 7)
    object_field = scatter_about(keys[0], (2, OBJ_ROWS, OBJ_COLS), 0.7, 4.2, ((1, 64),), jnp.float32)
    probe = scatter_about(keys[1], (2, MODES, TILE, TILE), 0.3, 1.796875, ((1, 2),))
    patterns = jnp.clip(jnp.exp(math.log(6.0) - 3.4011974 * jax.random.uniform(keys[2], (POS, TILE, TILE), jnp.float32) ** steps_of(keys[2], (POS, TILE, TILE), ((0, 64),), -0.2, 0.2)), 0.2, 6.0)
    row_shift = place_ends(jax.random.randint(keys[3], (POS,), 0, 2), jax.random.fold_in(keys[3], 1), 0, 1).astype(jnp.int32)
    col_start = place_ends(jax.random.randint(keys[4], (POS,), 0, 2 * OBJ_COLS // TILE - 1), jax.random.fold_in(keys[4], 1), 0, (2 * OBJ_COLS // TILE - 1) - 1).astype(jnp.int32)
    mixing = draw_mixing(jax.random.fold_in(keys[6], 71), 0)
    return {"object_field": object_field, "probe": probe, "patterns": patterns, "row_shift": row_shift, "col_start": col_start, "mixing": mixing}


def tables(tile_size):
    indices = jnp.arange(tile_size, dtype=jnp.int32)
    products = indices[:, None] * indices[None, :] % tile_size
    angles = products.astype(jnp.float32) * (2.0 * math.pi / tile_size)
    factor = 1.0 / math.sqrt(tile_size)
    return ((jnp.cos(angles) * factor).astype(jnp.bfloat16), (jnp.sin(angles) * factor).astype(jnp.bfloat16))

def right_mult(first, second):
    return jnp.einsum('...ij,jk->...ik', first.astype(jnp.float32), second.astype(jnp.float32))

def left_mult(first, second):
    return jnp.einsum('ij,...jk->...ik', first.astype(jnp.float32), second.astype(jnp.float32))

def transform(real_part, imag_part, cosine, sine_table, direction):
    half_real = right_mult(real_part, cosine) - direction * right_mult(imag_part, sine_table)
    half_imag = right_mult(imag_part, cosine) + direction * right_mult(real_part, sine_table)
    half_real = half_real.astype(jnp.bfloat16)
    half_imag = half_imag.astype(jnp.bfloat16)
    out_real = left_mult(cosine, half_real) - direction * left_mult(sine_table, half_imag)
    out_imag = left_mult(cosine, half_imag) + direction * left_mult(sine_table, half_real)
    return (out_real, out_imag)

def reference(object_field, probe, patterns, row_shift, col_start, mixing):
    cosine, sine_table = tables(TILE)
    padded = jnp.pad(object_field, ((0, 0), (0, HALF), (0, 0)))
    probe_real = probe[0].astype(jnp.float32)
    probe_imag = probe[1].astype(jnp.float32)
    illumination = lax.optimization_barrier(jnp.sum(probe_real * probe_real + probe_imag * probe_imag, axis=0))

    def visit(carry, inputs):
        object_grad, probe_grad = carry
        position, pattern, shift_rows, column = inputs
        row_first = (position // P_DEV * TILE + shift_rows * HALF).astype(jnp.int32)
        col_first = (column * HALF).astype(jnp.int32)
        zero_index = jnp.zeros((), jnp.int32)
        patches = lax.dynamic_slice(padded, (zero_index, row_first, col_first), (2, TILE, TILE))
        obj_real = patches[0]
        obj_imag = patches[1]
        exit_real = (probe_real * obj_real - probe_imag * obj_imag).astype(jnp.bfloat16)
        exit_imag = (probe_real * obj_imag + probe_imag * obj_real).astype(jnp.bfloat16)
        wave_real, wave_imag = transform(exit_real, exit_imag, cosine, sine_table, -1.0)
        summed = lax.optimization_barrier(jnp.sum(wave_real * wave_real + wave_imag * wave_imag, axis=0))
        scaling = jnp.sqrt(pattern) / jnp.sqrt(jnp.maximum(summed, 1.0))
        fixed_real = (wave_real * scaling).astype(jnp.bfloat16)
        fixed_imag = (wave_imag * scaling).astype(jnp.bfloat16)
        back_real, back_imag = transform(fixed_real, fixed_imag, cosine, sine_table, 1.0)
        resid_real = back_real - exit_real.astype(jnp.float32)
        resid_imag = back_imag - exit_imag.astype(jnp.float32)
        grad_real = lax.optimization_barrier(jnp.sum(probe_real * resid_real + probe_imag * resid_imag, axis=0))
        grad_imag = lax.optimization_barrier(jnp.sum(probe_real * resid_imag - probe_imag * resid_real, axis=0))
        region = lax.dynamic_slice(object_grad, (zero_index, row_first, col_first), (2, TILE, TILE))
        region = region + jnp.stack([grad_real, grad_imag])
        object_grad = lax.dynamic_update_slice(object_grad, region, (zero_index, row_first, col_first))
        step_real = obj_real * resid_real + obj_imag * resid_imag
        step_imag = obj_real * resid_imag - obj_imag * resid_real
        probe_grad = probe_grad + jnp.stack([step_real, step_imag])
        return ((object_grad, probe_grad), None)
    start_object = jnp.zeros((2, OBJ_ROWS + HALF, OBJ_COLS), jnp.float32)
    start_probe = jnp.zeros((2, MODES, TILE, TILE), jnp.float32)
    inputs = (jnp.arange(POS, dtype=jnp.int32), patterns, row_shift, col_start)
    (object_grad, probe_grad), unused = lax.scan(visit, (start_object, start_probe), inputs)
    object_new = object_field + object_grad[:, :OBJ_ROWS, :] / jnp.max(illumination)
    updated = probe.astype(jnp.float32) + probe_grad / math.sqrt(POS)
    weights = mixing.astype(jnp.float32) / 16.0
    probe_new = jnp.einsum('kj,cjrt->ckrt', weights, updated, precision=lax.Precision.HIGHEST)
    return (object_new, probe_new.astype(jnp.bfloat16))
```

```python
import functools, math
import jax, jax.numpy as jnp, numpy as np, ml_dtypes
from jax import lax
from jax.sharding import Mesh
from jax.sharding import PartitionSpec as P
from jax.experimental import pallas as pl
from jax.experimental.pallas import tpu as pltpu
f32, bf16 = jnp.float32, jnp.bfloat16
N = 512

def tables():
    i = np.arange(N, dtype=np.int32)
    ang = (i[:, None] * i[None, :] % N).astype(np.float32) * np.float32(2.0 * math.pi / N)
    f = np.float32(1.0 / math.sqrt(N))
    c = (np.cos(ang) * f).astype(ml_dtypes.bfloat16)
    s = (np.sin(ang) * f).astype(ml_dtypes.bfloat16)
    a = np.block([[c, -s], [s, c]])
    b = np.block([[c, s], [-s, c]])
    return a, b

ROWS = 64

def chunks(fn, rows=ROWS):
    def body(i, _):
        fn(pl.ds(pl.multiple_of(i * rows, rows), rows), i)
        return 0
    lax.fori_loop(0, N // rows, body, 0)

def make_exit(p_ref, m, patch_ref, rows):
    pr = p_ref[0, m, rows, :].astype(f32)
    pi = p_ref[1, m, rows, :].astype(f32)
    o_r = patch_ref[0, rows, :]
    o_i = patch_ref[1, rows, :]
    return pr, pi, o_r, o_i, (pr * o_r - pi * o_i).astype(bf16), (pr * o_i + pi * o_r).astype(bf16)

def forward_body(sc, tl, tr, bl, br, rl, rr, p_ref, a_ref, b_ref, wave_ref, sum_ref, patch_ref, x_s, h_s, *, mb):
    @pl.when(pl.program_id(0) == 0)
    def _():
        h = N // 2
        patch_ref[:, :h, :h] = tl[...]
        patch_ref[:, :h, h:] = tr[...]
        inside = sc[0] == 0
        @pl.when(inside)
        def _():
            patch_ref[:, h:, :h] = bl[...]
            patch_ref[:, h:, h:] = br[...]
        @pl.when(jnp.logical_not(inside))
        def _():
            patch_ref[:, h:, :h] = rl[...]
            patch_ref[:, h:, h:] = rr[...]
        sum_ref[...] = jnp.zeros_like(sum_ref)
    for m in range(mb):
        def one(rows, i):
            _, _, _, _, xr, xi = make_exit(p_ref, m, patch_ref, rows)
            x_s[m, rows, :N] = xr
            x_s[m, rows, N:] = xi
        chunks(one)
    for m in range(mb):
        half = jnp.dot(x_s[m], a_ref[...], preferred_element_type=f32).astype(bf16)
        h_s[:N, m * N:(m + 1) * N] = half[:, :N]
        h_s[N:, m * N:(m + 1) * N] = half[:, N:]
    for m in range(mb):
        w = jnp.dot(b_ref[...], h_s[:, m * N:(m + 1) * N], preferred_element_type=f32)
        wave_ref[0, m] = w[:N]
        wave_ref[1, m] = w[N:]
    def two(rows, i):
        acc = sum_ref[rows, :]
        for m in range(mb):
            a = wave_ref[0, m, rows, :]
            b = wave_ref[1, m, rows, :]
            acc = acc + (a * a + b * b)
        sum_ref[rows, :] = acc
    chunks(two)

def forward(sc, obj, rim, probe, a, b, mb=1):
    nm = probe.shape[1]
    q = (2, N // 2, N // 2)
    spec = lambda f: pl.BlockSpec(q, f)
    whole = lambda shp: pl.BlockSpec(shp, lambda k, sc: (0,) * len(shp))
    return pl.pallas_call(
        functools.partial(forward_body, mb=mb),
        grid_spec=pltpu.PrefetchScalarGridSpec(
            num_scalar_prefetch=1, grid=(nm // mb,),
            in_specs=[
                spec(lambda k, sc: (0, sc[0], sc[1])), spec(lambda k, sc: (0, sc[0], sc[1] + 1)),
                spec(lambda k, sc: (0, 1, sc[1])), spec(lambda k, sc: (0, 1, sc[1] + 1)),
                spec(lambda k, sc: (0, 0, sc[1])), spec(lambda k, sc: (0, 0, sc[1] + 1)),
                pl.BlockSpec((2, mb, N, N), lambda k, sc: (0, k, 0, 0)),
                whole((2 * N, 2 * N)), whole((2 * N, 2 * N))],
            out_specs=[
                pl.BlockSpec((2, mb, N, N), lambda k, sc: (0, k, 0, 0)),
                whole((N, N)), whole((2, N, N))],
            scratch_shapes=[pltpu.VMEM((mb, N, 2 * N), bf16), pltpu.VMEM((2 * N, mb * N), bf16)]),
        out_shape=[jax.ShapeDtypeStruct((2, nm, N, N), f32), jax.ShapeDtypeStruct((N, N), f32), jax.ShapeDtypeStruct((2, N, N), f32)],
        compiler_params=pltpu.CompilerParams(dimension_semantics=("arbitrary",), vmem_limit_bytes=56 << 20),
        name="forward",
    )(sc, obj, obj, obj, obj, rim, rim, probe, a, b)

def backward_body(sc, pat, s0, s1, patch_ref, p_ref, wave_ref, a_ref, b_ref, gin_ref, keep_ref, send_ref, top_ref, bot_ref, scale_s, x_s, h_s, *, mb, first):
    h = N // 2
    @pl.when(pl.program_id(0) == 0)
    def _():
        def one(rows, i):
            scale_s[rows, :] = jnp.sqrt(pat[0, rows, :]) / jnp.sqrt(jnp.maximum(s0[rows, :] + s1[rows, :], 1.0))
        chunks(one)
        if first:
            top_ref[...] = jnp.zeros_like(top_ref)
            bot_ref[...] = jnp.zeros_like(bot_ref)
        else:
            top_ref[...] = gin_ref[0][...]
            bot_ref[...] = gin_ref[1][...]
    core = sc[0]
    for m in range(mb):
        def one(rows, i):
            sc_ = scale_s[rows, :]
            x_s[rows, :N] = (wave_ref[0, m, rows, :] * sc_).astype(bf16)
            x_s[rows, N:] = (wave_ref[1, m, rows, :] * sc_).astype(bf16)
        chunks(one)
        half = jnp.dot(x_s[...], b_ref[...], preferred_element_type=f32).astype(bf16)
        h_s[:N] = half[:, :N]
        h_s[N:] = half[:, N:]
        back = jnp.dot(a_ref[...], h_s[...], preferred_element_type=f32)
        wave_ref[0, m] = back[:N]
        wave_ref[1, m] = back[N:]
        def two(rows, i, g_ref, r_out):
            pr, pi, o_r, o_i, xr, xi = make_exit(p_ref, m, patch_ref, rows)
            rr = wave_ref[0, m, rows, :] - xr.astype(f32)
            ri = wave_ref[1, m, rows, :] - xi.astype(f32)
            g_ref[0, r_out, :] += pr * rr + pi * ri
            g_ref[1, r_out, :] += pr * ri - pi * rr
            st = (o_r * rr + o_i * ri, o_r * ri - o_i * rr)
            n16 = ROWS // 16
            for c in range(2):
                v = st[c].reshape(n16, 2, 8, N)
                lo, hi = v[:, 0], v[:, 1]
                at = pl.ds(pl.multiple_of(i * n16, n16), n16)
                keep_ref[c, m, at] = jnp.where(core == 0, lo, hi)
                send_ref[c, m, at] = jnp.where(core == 0, hi, lo)
        nc = h // ROWS
        def tb(i, _):
            two(pl.ds(pl.multiple_of(i * ROWS, ROWS), ROWS), i, top_ref, pl.ds(pl.multiple_of(i * ROWS, ROWS), ROWS))
            return 0
        lax.fori_loop(0, nc, tb, 0)
        def bb(i, _):
            two(pl.ds(pl.multiple_of((i + nc) * ROWS, ROWS), ROWS), i + nc, bot_ref, pl.ds(pl.multiple_of(i * ROWS, ROWS), ROWS))
            return 0
        lax.fori_loop(0, nc, bb, 0)

def backward(sc, pat, s0, s1, patch, probe, wave, a, b, grads, first_mode, nm, mb=1):
    whole = lambda shp: pl.BlockSpec(shp, lambda k, sc: (0,) * len(shp))
    off = first_mode // mb
    first = grads is None
    def body(sc, *refs):
        refs = list(refs)
        ins = refs[:8]; refs = refs[8:]
        gin = None
        if not first:
            gin = refs[:2]; refs = refs[2:]
        backward_body(sc, *ins, gin, *refs, mb=mb, first=first)
    kshape = (2, nm, 32, 8, N)
    modes = pl.BlockSpec((2, mb, N, N), lambda k, sc: (0, k + off, 0, 0))
    half = whole((2, N // 2, N))
    return pl.pallas_call(
        body,
        grid_spec=pltpu.PrefetchScalarGridSpec(
            num_scalar_prefetch=1, grid=(nm // mb,),
            in_specs=[whole((1, N, N)), whole((N, N)), whole((N, N)), whole((2, N, N)), modes, modes,
                      whole((2 * N, 2 * N)), whole((2 * N, 2 * N))] + ([] if first else [half, half]),
            out_specs=[pl.BlockSpec((2, mb, 32, 8, N), lambda k, sc: (0, k, 0, 0, 0))] * 2 + [half, half],
            scratch_shapes=[pltpu.VMEM((N, N), f32), pltpu.VMEM((N, 2 * N), bf16), pltpu.VMEM((2 * N, N), bf16)]),
        out_shape=[jax.ShapeDtypeStruct(kshape, f32)] * 2 + [jax.ShapeDtypeStruct((2, N // 2, N), f32)] * 2,
        compiler_params=pltpu.CompilerParams(dimension_semantics=("arbitrary",), vmem_limit_bytes=56 << 20),
        name="backward",
    )(sc, pat, s0, s1, patch, probe, wave, a, b, *([] if first else grads))


SCAN = ("y", "z", "x", "core")
GROUPS = 2
VMEM = pltpu.CompilerParams(vmem_limit_bytes=56 << 20)


def shape(*dims):
    return jax.ShapeDtypeStruct(dims, f32)


def whole_spec(dims):
    return pl.BlockSpec(dims, lambda *_: (0,) * len(dims))


def along(value, axis, steps):
    count = lax.axis_size(axis)
    lo, hi = max(0, -steps), min(count, count - steps)
    return lax.ppermute(value, axis, [(i, i + steps) for i in range(lo, hi)])


def turned(value, axis, steps):
    count = lax.axis_size(axis)
    return lax.ppermute(value, axis, [(i, (i + steps) % count) for i in range(count)])


def swapped(value, axis):
    return turned(value, axis, 1)


def quarters(parts, axis):
    return [parts[0]] + [turned(parts[r], axis, r) for r in (1, 3, 2)]


def light_body(p_ref, out_ref):
    @pl.when(pl.program_id(0) == 0)
    def _():
        out_ref[...] = jnp.zeros_like(out_ref)

    def one(rows, i):
        pr = p_ref[0, 0, rows, :].astype(f32)
        pi = p_ref[1, 0, rows, :].astype(f32)
        out_ref[rows, :] += pr * pr + pi * pi

    chunks(one)


def light(probe):
    return pl.pallas_call(
        light_body,
        grid=(probe.shape[1],),
        in_specs=[pl.BlockSpec((2, 1, N, N), lambda k: (0, k, 0, 0))],
        out_specs=whole_spec((N, N)),
        out_shape=shape(N, N),
        name="light",
    )(probe)


def core_add_body(at, keep, recv, *outs):
    y, z = at[0], at[1]
    for r in range(4):
        yy = lax.rem(y + r, 4)
        zz = lax.rem(z + r, 4)
        outs[r][0] = keep[0, 0, yy] + recv[0, 0, yy]
        outs[4 + r][0] = keep[1, 0, :, zz] + recv[1, 0, :, zz]


def core_add(at, keep, recv):
    nm = keep.shape[1]
    dims = (2, nm, 4, 4, 16, N)
    spec = pl.BlockSpec((2, 1, 4, 4, 16, N), lambda k, at: (0, k, 0, 0, 0, 0))
    out = pl.BlockSpec((1, 4, 16, N), lambda k, at: (k, 0, 0, 0))
    outs = pl.pallas_call(
        core_add_body,
        grid_spec=pltpu.PrefetchScalarGridSpec(
            num_scalar_prefetch=1, grid=(nm,), in_specs=[spec, spec], out_specs=[out] * 8
        ),
        out_shape=[shape(nm, 4, 16, N)] * 8,
        compiler_params=VMEM,
        name="core_add",
    )(at, keep.reshape(dims), recv.reshape(dims))
    return outs[:4], outs[4:]


def plane_add_body(at, *refs, groups, nm):
    ins, outs = refs[: 8 * groups], refs[8 * groups :]
    y, z = at[0], at[1]
    for r in range(4):
        for part, pos in ((0, lax.rem(z + r, 4)), (1, lax.rem(y + r, 4))):
            for g in range(groups):
                a = ins[g * 8 + part * 4 : g * 8 + part * 4 + 4]
                outs[part * 4 + r][g * nm : (g + 1) * nm] = (
                    (a[0][:, pos] + a[1][:, pos]) + (a[2][:, pos] + a[3][:, pos])
                )


def plane_add(at, groups):
    nm = groups[0][0].shape[0]
    ng = len(groups)
    ins = [a for g in groups for a in g]
    outs = pl.pallas_call(
        functools.partial(plane_add_body, groups=ng, nm=nm),
        grid_spec=pltpu.PrefetchScalarGridSpec(
            num_scalar_prefetch=1,
            grid=(1,),
            in_specs=[whole_spec(a.shape) for a in ins],
            out_specs=[whole_spec((ng * nm, 16, N))] * 8,
        ),
        out_shape=[shape(ng * nm, 16, N)] * 8,
        compiler_params=VMEM,
        name="plane_add",
    )(at, *ins)
    return outs[:4], outs[4:]


def row_add_body(at, *refs):
    ins, rows, outs = refs[:8], refs[8], refs[9:]
    x = at[2]
    nm = ins[0].shape[0]
    scale = 1.0 / math.sqrt(64)
    for part in range(2):
        a = ins[part * 4 : part * 4 + 4]

        def total(xx):
            at_rows = pl.ds(pl.multiple_of(xx * 8, 8), 8)
            return ((a[0][:, at_rows] + a[1][:, at_rows]) + (a[2][:, at_rows] + a[3][:, at_rows])) * scale

        mine = total(x) + rows[part].astype(f32)
        outs[0][part] = mine
        outs[1][part] = total(1 - x)


def row_add(at, parts, rows):
    nm = rows.shape[1]
    ins = [*parts, rows]
    return pl.pallas_call(
        row_add_body,
        grid_spec=pltpu.PrefetchScalarGridSpec(
            num_scalar_prefetch=1,
            grid=(1,),
            in_specs=[whole_spec(a.shape) for a in ins],
            out_specs=[whole_spec((2, nm, 8, N))] * 2,
        ),
        out_shape=[shape(2, nm, 8, N)] * 2,
        compiler_params=VMEM,
        name="row_add",
    )(at, *ins)


def mix_body(at, w_ref, mine, b, c, d, out_ref):
    mode = at[3]
    nm = mine.shape[1]
    for part in range(2):
        own = [mine[part, j] + b[part, j] for j in range(nm)]
        far = [c[part, j] + d[part, j] for j in range(nm)]
        for k in range(nm):
            row = mode * nm + k
            acc = jnp.zeros((8, N), f32)
            for j in range(nm):
                acc += (w_ref[row, mode * nm + j].astype(f32) / 16.0) * own[j]
                acc += (w_ref[row, (1 - mode) * nm + j].astype(f32) / 16.0) * far[j]
            out_ref[part, k] = acc.astype(bf16)


def mix(at, mixing, mine, b, c, d):
    dims = mine.shape
    return pl.pallas_call(
        mix_body,
        grid_spec=pltpu.PrefetchScalarGridSpec(
            num_scalar_prefetch=2, grid=(1,), in_specs=[whole_spec(dims)] * 4, out_specs=whole_spec(dims)
        ),
        out_shape=jax.ShapeDtypeStruct(dims, bf16),
        compiler_params=VMEM,
        name="mix",
    )(at, mixing, mine, b, c, d)


def object_body(sc, lights, obj, top, top2, bot, bot2, over, out_ref):
    i, j = pl.program_id(0), pl.program_id(1)
    own_i, own_j = i - sc[0], j - sc[1]
    over_j = j - sc[3]
    out_ref[...] = obj[...]
    inv = lights[0]
    in_cols = jnp.logical_and(own_j >= 0, own_j < 2)

    @pl.when(jnp.logical_and(in_cols, own_i == 0))
    def _():
        out_ref[...] += (top[...] + top2[...]) / inv

    @pl.when(jnp.logical_and(in_cols, own_i == 1))
    def _():
        out_ref[...] += (bot[...] + bot2[...]) / inv

    @pl.when(jnp.logical_and(jnp.logical_and(i == 0, sc[2] == 1), jnp.logical_and(over_j >= 0, over_j < 2)))
    def _():
        out_ref[...] += over[...] / inv


def object_update(sc, brightest, obj, top, top2, bot, bot2, over):
    h = N // 2
    q = (2, h, h)
    own = pl.BlockSpec(q, lambda i, j, sc, li: (0, 0, jnp.clip(j - sc[1], 0, 1)))
    return pl.pallas_call(
        object_body,
        grid_spec=pltpu.PrefetchScalarGridSpec(
            num_scalar_prefetch=2,
            grid=(2, 4),
            in_specs=[pl.BlockSpec(q, lambda i, j, sc, li: (0, i, j))]
            + [own] * 4
            + [pl.BlockSpec(q, lambda i, j, sc, li: (0, 0, jnp.clip(j - sc[3], 0, 1)))],
            out_specs=pl.BlockSpec(q, lambda i, j, sc, li: (0, i, j)),
        ),
        out_shape=shape(2, N, 1024),
        compiler_params=VMEM,
        name="object_update",
    )(sc, brightest, obj, top, top2, bot, bot2, over)


def per_device(object_field, probe, patterns, row_shift, col_start, mixing):
    h = N // 2
    nm = probe.shape[1]
    a_table, b_table = tables()
    core = lax.axis_index("core")
    at = jnp.stack([lax.axis_index("y"), lax.axis_index("z"), lax.axis_index("x"), lax.axis_index("mode")])
    place = jnp.concatenate([row_shift, col_start])
    before = along(place, SCAN, 1)
    rim = along(object_field[:, :h, :], SCAN, -1)
    own_light = light(probe)
    wave, own_sum, patch = forward(place, object_field, rim, probe, a_table, b_table)
    far_sum = swapped(own_sum, "mode")
    far_light = swapped(own_light, "mode")
    brightest = jnp.max(own_light + far_light)[None]
    grads = None
    planes = []
    group = nm // GROUPS
    for g in range(GROUPS):
        keep, send, *grads = backward(
            core[None], patterns, own_sum, far_sum, patch, probe, wave, a_table, b_table, grads, g * group, group
        )
        real, imag = core_add(at, keep, swapped(send, "core"))
        planes.append(quarters(real, "y") + quarters(imag, "z"))
    top, bot = grads
    far_bot = swapped(bot, "mode")
    far_top = swapped(top, "mode")
    over = along(bot + far_bot, SCAN, 1)
    real, imag = plane_add(at, planes)
    parts = quarters(real, "z") + quarters(imag, "y")
    rows = lax.dynamic_slice_in_dim(probe, lax.axis_index(SCAN) * 8, 8, 2)
    mine, other = row_add(at, parts, rows)
    pairs = [((m, x), (m, 1 - x)) for m in range(2) for x in range(2)]
    flat = lambda m, x: 2 * m + x
    both = ("mode", "x")
    b = lax.ppermute(other, both, [(flat(m, x), flat(m, 1 - x)) for m in range(2) for x in range(2)])
    c = lax.ppermute(mine, both, [(flat(m, x), flat(1 - m, x)) for m in range(2) for x in range(2)])
    d = lax.ppermute(other, both, [(flat(m, x), flat(1 - m, 1 - x)) for m in range(2) for x in range(2)])
    probe_new = mix(at, mixing, mine, b, c, d)
    object_new = object_update(
        jnp.concatenate([place, before]), brightest, object_field, top, far_top, bot, far_bot, over
    )
    return object_new, probe_new


def solution(mesh):
    split = Mesh(mesh.devices.reshape(2, 4, 4, 2, 2), ("mode", *SCAN))
    return jax.shard_map(
        per_device,
        mesh=split,
        in_specs=(P(None, SCAN, None), P(None, "mode", None, None), P(SCAN, None, None), P(SCAN), P(SCAN), P()),
        out_specs=(P(None, SCAN, None), P(None, "mode", SCAN, None)),
        check_vma=False,
    )
```

```python
import functools
import math

import jax
import jax.numpy as jnp
import ml_dtypes
import numpy as np
from jax import lax
from jax.experimental import pallas as pl
from jax.experimental.pallas import tpu as pltpu
from jax.sharding import Mesh
from jax.sharding import PartitionSpec as P

f32, bf16 = jnp.float32, jnp.bfloat16
N = 512
H = 256
CHUNK = 32
VMEM_MIB = 56


def tables():
    i = np.arange(N, dtype=np.int32)
    angle = (i[:, None] * i[None, :] % N).astype(np.float32) * np.float32(2.0 * math.pi / N)
    factor = np.float32(1.0 / math.sqrt(N))
    c = (np.cos(angle) * factor).astype(ml_dtypes.bfloat16)
    s = (np.sin(angle) * factor).astype(ml_dtypes.bfloat16)
    minus = np.block([[c, -s], [s, c]])
    plus = np.block([[c, s], [-s, c]])

    def stacked(table):
        return table.reshape(2 * N, 2, 2, H).swapaxes(1, 2).reshape(2, N, 2 * N)

    wave_rows = stacked(plus).reshape(2, 2, H, 2 * N).swapaxes(0, 1).reshape(2, N, 2 * N)
    back_rows = stacked(minus).reshape(2, 16, 2, 16, 2 * N).transpose(2, 0, 1, 3, 4).reshape(2, N, 2 * N)
    return minus, plus, np.ascontiguousarray(wave_rows), np.ascontiguousarray(back_rows)


def params(mib):
    return pltpu.CompilerParams(vmem_limit_bytes=mib << 20)


def cost(us):
    return pl.CostEstimate(flops=int(us * 1.1e9), transcendentals=0, bytes_accessed=int(us * 3e6))


def shape(*dims, dtype=f32):
    return jax.ShapeDtypeStruct(dims, dtype)


def whole(*dims):
    return pl.BlockSpec(dims, lambda *_: (0,) * len(dims))


def loop(count, fn):
    def body(i, carry):
        fn(i)
        return carry

    lax.fori_loop(0, count, body, 0)


def at(i, size):
    return pl.ds(pl.multiple_of(i * size, size), size)


def exit_rows(p_ref, m, rows, o_r, o_i):
    pr = p_ref[0, m, rows, :].astype(f32)
    pi = p_ref[1, m, rows, :].astype(f32)
    return pr, pi, (pr * o_r - pi * o_i).astype(bf16), (pr * o_i + pi * o_r).astype(bf16)


def exit_half(p_ref, m, patch, x_s):
    def one(i):
        rows = at(i, CHUNK)
        _, _, xr, xi = exit_rows(p_ref, m, rows, patch[0, rows, :], patch[1, rows, :])
        x_s[m, rows, :N] = xr
        x_s[m, rows, N:] = xi

    loop(H // CHUNK, one)


def along_rows(x_s, table, out):
    nm = x_s.shape[0]
    x = x_s[...].reshape(nm * H, 2 * N)
    half = jnp.dot(x, table[...], preferred_element_type=f32).astype(bf16)
    for m in range(nm):
        out[m, :H] = half[m * H : (m + 1) * H, :N]
        out[m, H:] = half[m * H : (m + 1) * H, N:]


def top_body(sc, left, right, p_ref, table, half_ref, patch_ref, x_s):
    @pl.when(pl.program_id(0) == 0)
    def _():
        patch_ref[:, :, :H] = left[...]
        patch_ref[:, :, H:] = right[...]

    for m in range(x_s.shape[0]):
        exit_half(p_ref, m, patch_ref, x_s)
    along_rows(x_s, table, half_ref)


def top_half(sc, obj, probe, table, mb=2):
    nm = probe.shape[1]
    return pl.pallas_call(
        top_body,
        grid_spec=pltpu.PrefetchScalarGridSpec(
            num_scalar_prefetch=1,
            grid=(nm // mb,),
            in_specs=[
                pl.BlockSpec((2, H, H), lambda k, sc: (0, sc[0], sc[1])),
                pl.BlockSpec((2, H, H), lambda k, sc: (0, sc[0], sc[1] + 1)),
                pl.BlockSpec((2, mb, H, N), lambda k, sc: (0, k, 0, 0)),
                whole(2 * N, 2 * N),
            ],
            out_specs=[pl.BlockSpec((mb, N, N), lambda k, sc: (k, 0, 0)), whole(2, H, N)],
            scratch_shapes=[pltpu.VMEM((mb, H, 2 * N), bf16)],
        ),
        out_shape=[shape(nm, N, N, dtype=bf16), shape(2, H, N)],
        compiler_params=params(50),
        name="top_half",
        cost_estimate=cost(6),
    )(sc, obj, obj, probe, table)


def wave_half(wave_ref, sum_ref, wt, top, bot):
    nm = top.shape[0]
    for m in range(nm):
        wave_ref[m] = jnp.dot(wt[0, :, :N], top[m], preferred_element_type=f32) + jnp.dot(
            wt[0, :, N:], bot[m], preferred_element_type=f32
        )

    def one(i):
        rows = at(i, CHUNK)
        low = pl.ds(pl.multiple_of(i * CHUNK + H, CHUNK), CHUNK)
        acc = sum_ref[rows, :]
        for m in range(nm):
            a = wave_ref[m, rows, :]
            b = wave_ref[m, low, :]
            acc = acc + (a * a + b * b)
        sum_ref[rows, :] = acc

    loop(H // CHUNK, one)


def bottom_body(sc, left, right, rim, p_ref, table, wt, top, half_ref, patch_ref, wave_ref, sum_ref, x_s):
    @pl.when(pl.program_id(0) == 0)
    def _():
        @pl.when(sc[0] == 0)
        def _():
            patch_ref[:, :, :H] = left[...]
            patch_ref[:, :, H:] = right[...]

        @pl.when(sc[0] != 0)
        def _():
            patch_ref[...] = rim[...]

        sum_ref[...] = jnp.zeros_like(sum_ref)

    for m in range(x_s.shape[0]):
        exit_half(p_ref, m, patch_ref, x_s)
    along_rows(x_s, table, half_ref)
    wave_half(wave_ref, sum_ref, wt, top, half_ref)


def bottom_half(sc, obj, rim, probe, table, wave_rows, top, mb=2):
    nm = probe.shape[1]
    halves = pl.BlockSpec((mb, N, N), lambda k, sc: (k, 0, 0))
    return pl.pallas_call(
        bottom_body,
        grid_spec=pltpu.PrefetchScalarGridSpec(
            num_scalar_prefetch=1,
            grid=(nm // mb,),
            in_specs=[
                pl.BlockSpec((2, H, H), lambda k, sc: (0, 1, sc[1])),
                pl.BlockSpec((2, H, H), lambda k, sc: (0, 1, sc[1] + 1)),
                whole(2, H, N),
                pl.BlockSpec((2, mb, H, N), lambda k, sc: (0, k, 1, 0)),
                whole(2 * N, 2 * N),
                pl.BlockSpec((1, N, 2 * N), lambda k, sc: (0, 0, 0)),
                halves,
            ],
            out_specs=[halves, whole(2, H, N), halves, whole(H, N)],
            scratch_shapes=[pltpu.VMEM((mb, H, 2 * N), bf16)],
        ),
        out_shape=[shape(nm, N, N, dtype=bf16), shape(2, H, N), shape(nm, N, N), shape(H, N)],
        compiler_params=params(50),
        name="bottom_half",
        cost_estimate=cost(11),
    )(sc, obj, obj, rim, probe, table, wave_rows, top)


def low_wave_body(wt, top, bot, wave_ref, sum_ref):
    @pl.when(pl.program_id(0) == 0)
    def _():
        sum_ref[...] = jnp.zeros_like(sum_ref)

    wave_half(wave_ref, sum_ref, wt, top, bot)


def low_wave(wave_rows, top, bot, mb=2):
    nm = top.shape[0]
    halves = pl.BlockSpec((mb, N, N), lambda k: (k, 0, 0))
    return pl.pallas_call(
        low_wave_body,
        grid=(nm // mb,),
        in_specs=[pl.BlockSpec((1, N, 2 * N), lambda k: (1, 0, 0)), halves, halves],
        out_specs=[halves, whole(H, N)],
        out_shape=[shape(nm, N, N), shape(H, N)],
        compiler_params=params(50),
        name="low_wave",
        cost_estimate=cost(5),
    )(wave_rows, top, bot)


def fixed_half(pat, s0, s1, wave_ref, table, half_ref, scale_s, x_s):
    @pl.when(pl.program_id(0) == 0)
    def _():
        def one(i):
            rows = at(i, CHUNK)
            scale_s[rows, :] = jnp.sqrt(pat[0, rows, :]) / jnp.sqrt(jnp.maximum(s0[rows, :] + s1[rows, :], 1.0))

        loop(H // CHUNK, one)

    for m in range(x_s.shape[0]):

        def one(i):
            rows = at(i, CHUNK)
            low = pl.ds(pl.multiple_of(i * CHUNK + H, CHUNK), CHUNK)
            factor = scale_s[rows, :]
            x_s[m, rows, :N] = (wave_ref[m, rows, :] * factor).astype(bf16)
            x_s[m, rows, N:] = (wave_ref[m, low, :] * factor).astype(bf16)

        loop(H // CHUNK, one)
    along_rows(x_s, table, half_ref)


def fixed_top(pat, s0, s1, wave, table, mb=2):
    nm = wave.shape[0]
    halves = pl.BlockSpec((mb, N, N), lambda k: (k, 0, 0))
    return pl.pallas_call(
        fixed_half,
        grid=(nm // mb,),
        in_specs=[pl.BlockSpec((1, H, N), lambda k: (0, 0, 0)), whole(H, N), whole(H, N), halves, whole(2 * N, 2 * N)],
        out_specs=halves,
        out_shape=shape(nm, N, N, dtype=bf16),
        scratch_shapes=[pltpu.VMEM((H, N), f32), pltpu.VMEM((mb, H, 2 * N), bf16)],
        compiler_params=params(50),
        name="fixed_top",
        cost_estimate=cost(5),
    )(pat, s0, s1, wave, table)


def gradients(sc, block, bt, top, bot, patch_top, patch_bot, p_ref, keep_ref, send_ref, gtop, gbot, back_s):
    core = sc[0]

    @pl.when(pl.program_id(0) == 0)
    def _():
        gtop[...] = jnp.zeros_like(gtop)
        gbot[...] = jnp.zeros_like(gbot)

    for m in range(p_ref.shape[1]):
        back_s[...] = jnp.dot(bt[0, :, :N], top[m], preferred_element_type=f32) + jnp.dot(
            bt[0, :, N:], bot[m], preferred_element_type=f32
        )
        for patch, g_ref, base in ((patch_top, gtop, 0), (patch_bot, gbot, 8)):

            def one(i):
                g = i + base
                rows = pl.ds(pl.multiple_of(i * 32 + block * 16, 16), 16)
                full = pl.ds(pl.multiple_of(g * 32 + block * 16, 16), 16)
                o_r = patch[0, rows, :]
                o_i = patch[1, rows, :]
                pr, pi, xr, xi = exit_rows(p_ref, m, full, o_r, o_i)
                rr = back_s[at(g, 16), :] - xr.astype(f32)
                ri = back_s[pl.ds(pl.multiple_of(g * 16 + H, 16), 16), :] - xi.astype(f32)
                g_ref[0, i] += pr * rr + pi * ri
                g_ref[1, i] += pr * ri - pi * rr
                st0 = o_r * rr + o_i * ri
                st1 = o_r * ri - o_i * rr
                turned_g = (g % 4) * 4 + g // 4
                keep_ref[m, jnp.where(core == 0, g, turned_g)] = jnp.where(core == 0, st0, st1)
                send_ref[m, jnp.where(core == 0, turned_g, g)] = jnp.where(core == 0, st1, st0)

            loop(8, one)


def first_block_body(sc, pat, s0, s1, wave_ref, table, bt, top, ptop, pbot, p_ref, half_ref, keep, send, gtop, gbot, scale_s, x_s, back_s):
    fixed_half(pat, s0, s1, wave_ref, table, half_ref, scale_s, x_s)
    gradients(sc, 0, bt, top, half_ref, ptop, pbot, p_ref, keep, send, gtop, gbot, back_s)


GRADS = [shape(2, 8, 16, N)] * 2


def grad_specs(mb):
    return [pl.BlockSpec((mb, 16, 16, N), lambda k, sc: (k, 0, 0, 0))] * 2 + [whole(2, 8, 16, N)] * 2


def first_block(sc, pat, s0, s1, wave, table, back_rows, top, ptop, pbot, probe, mb=2):
    nm = wave.shape[0]
    halves = pl.BlockSpec((mb, N, N), lambda k, sc: (k, 0, 0))
    return pl.pallas_call(
        first_block_body,
        grid_spec=pltpu.PrefetchScalarGridSpec(
            num_scalar_prefetch=1,
            grid=(nm // mb,),
            in_specs=[
                pl.BlockSpec((1, H, N), lambda k, sc: (0, 1, 0)),
                whole(H, N),
                whole(H, N),
                halves,
                whole(2 * N, 2 * N),
                pl.BlockSpec((1, N, 2 * N), lambda k, sc: (0, 0, 0)),
                halves,
                whole(2, H, N),
                whole(2, H, N),
                pl.BlockSpec((2, mb, N, N), lambda k, sc: (0, k, 0, 0)),
            ],
            out_specs=[halves] + grad_specs(mb),
            scratch_shapes=[pltpu.VMEM((H, N), f32), pltpu.VMEM((mb, H, 2 * N), bf16), pltpu.VMEM((N, N), f32)],
        ),
        out_shape=[shape(nm, N, N, dtype=bf16)] + [shape(nm, 16, 16, N)] * 2 + GRADS,
        compiler_params=params(50),
        name="first_block",
        cost_estimate=cost(16),
    )(sc, pat, s0, s1, wave, table, back_rows, top, ptop, pbot, probe)


def second_block_body(sc, bt, top, bot, ptop, pbot, p_ref, keep, send, gtop, gbot, back_s):
    gradients(sc, 1, bt, top, bot, ptop, pbot, p_ref, keep, send, gtop, gbot, back_s)


def second_block(sc, back_rows, top, bot, ptop, pbot, probe, mb=2):
    nm = top.shape[0]
    halves = pl.BlockSpec((mb, N, N), lambda k, sc: (k, 0, 0))
    return pl.pallas_call(
        second_block_body,
        grid_spec=pltpu.PrefetchScalarGridSpec(
            num_scalar_prefetch=1,
            grid=(nm // mb,),
            in_specs=[
                pl.BlockSpec((1, N, 2 * N), lambda k, sc: (1, 0, 0)),
                halves,
                halves,
                whole(2, H, N),
                whole(2, H, N),
                pl.BlockSpec((2, mb, N, N), lambda k, sc: (0, k, 0, 0)),
            ],
            out_specs=grad_specs(mb),
            scratch_shapes=[pltpu.VMEM((N, N), f32)],
        ),
        out_shape=[shape(nm, 16, 16, N)] * 2 + GRADS,
        compiler_params=params(50),
        name="second_block",
        cost_estimate=cost(9),
    )(sc, back_rows, top, bot, ptop, pbot, probe)


SCAN = ("y", "z", "x", "core")
RING = ("y", "z", "core")


def along(value, steps):
    count = lax.axis_size(SCAN)
    lo, hi = max(0, -steps), min(count, count - steps)
    return lax.ppermute(value, SCAN, [(i, i + steps) for i in range(lo, hi)])


def swapped(value, axis):
    return lax.ppermute(value, axis, [(0, 1), (1, 0)])


def turned(value, steps, first):
    flat = lambda y, z, core: (y * 4 + z) * 2 + core
    pairs = []
    for y in range(4):
        for z in range(4):
            for core in range(2):
                on_y = (core == 0) == first
                to = ((y + steps) % 4, z) if on_y else (y, (z + steps) % 4)
                pairs.append((flat(y, z, core), flat(*to, core)))
    return lax.ppermute(value, RING, pairs)


def across(value, flip_mode, flip_x):
    pairs = [(2 * m + x, 2 * (m ^ flip_mode) + (x ^ flip_x)) for m in range(2) for x in range(2)]
    return lax.ppermute(value, ("mode", "x"), pairs)


def rim_body(sc, a, out):
    out[...] = a[...]


def rim_rows(sc, obj):
    return pl.pallas_call(
        rim_body,
        grid_spec=pltpu.PrefetchScalarGridSpec(
            num_scalar_prefetch=1,
            grid=(2,),
            in_specs=[pl.BlockSpec((2, H, H), lambda k, sc: (0, 0, sc[1] + k))],
            out_specs=pl.BlockSpec((2, H, H), lambda k, sc: (0, 0, k)),
        ),
        out_shape=shape(2, H, N),
        compiler_params=params(8),
        name="rim_rows",
        cost_estimate=cost(2),
    )(sc, obj)


def light_body(p_ref, out_ref):
    @pl.when(pl.program_id(0) == 0)
    def _():
        out_ref[...] = jnp.zeros_like(out_ref)

    def one(i):
        rows = at(i, 16)
        acc = out_ref[rows, :]
        for m in range(p_ref.shape[1]):
            pr = p_ref[0, m, rows, :].astype(f32)
            pi = p_ref[1, m, rows, :].astype(f32)
            acc = acc + (pr * pr + pi * pi)
        out_ref[rows, :] = acc

    loop(N // 16, one)


def light(probe):
    nm = probe.shape[1]
    return pl.pallas_call(
        light_body,
        grid=(3,),
        in_specs=[pl.BlockSpec((2, nm // 3, N, N), lambda k: (0, k, 0, 0))],
        out_specs=whole(N, N),
        out_shape=shape(N, N),
        compiler_params=params(12),
        name="light",
        cost_estimate=cost(3),
    )(probe)


def core_add_body(sc, k0, k1, r0, r1, own, near, back, far0, far1):
    me = sc[0]
    for j, (k, r) in enumerate(((k0, r0), (k1, r1))):
        for out, turn in ((own, 0), (near, 1), (back, 3)):
            a = lax.rem(me + turn, 4)
            out[j, 0] = k[0, a] + r[0, a]
        a = lax.rem(me + 2, 4)
        (far0, far1)[j][0] = k[0, a] + r[0, a]


def core_add(sc, keep, recv):
    nm = keep.shape[0]
    n2 = nm // 2
    keep, recv = (v.reshape(nm, 4, 4, 16, N) for v in (keep, recv))
    low = pl.BlockSpec((1, 4, 4, 16, N), lambda k, sc: (k, 0, 0, 0, 0))
    high = pl.BlockSpec((1, 4, 4, 16, N), lambda k, sc: (k + n2, 0, 0, 0, 0))
    pair = pl.BlockSpec((2, 1, 4, 16, N), lambda k, sc: (0, k, 0, 0, 0))
    one = pl.BlockSpec((1, 4, 16, N), lambda k, sc: (k, 0, 0, 0))
    return pl.pallas_call(
        core_add_body,
        grid_spec=pltpu.PrefetchScalarGridSpec(
            num_scalar_prefetch=1,
            grid=(n2,),
            in_specs=[low, high, low, high],
            out_specs=[pair, pair, pair, one, one],
        ),
        out_shape=[shape(2, n2, 4, 16, N)] * 3 + [shape(n2, 4, 16, N)] * 2,
        compiler_params=params(16),
        name="core_add",
        cost_estimate=cost(4),
    )(sc, keep, keep, recv, recv)


def relay_body(a, b, ra, rb, oa, ob):
    oa[...] = a[...] + ra[...]
    ob[...] = b[...] + rb[...]


def relay_add(near, back, ra, rb):
    n2 = near.shape[1]
    low = pl.BlockSpec((None, 1, 4, 16, N), lambda k: (0, k, 0, 0, 0))
    high = pl.BlockSpec((None, 1, 4, 16, N), lambda k: (1, k, 0, 0, 0))
    one = pl.BlockSpec((1, 4, 16, N), lambda k: (k, 0, 0, 0))
    return pl.pallas_call(
        relay_body,
        grid=(n2,),
        in_specs=[low, high, one, one],
        out_specs=[low, high],
        out_shape=[shape(2, n2, 4, 16, N)] * 2,
        input_output_aliases={0: 0, 1: 1},
        compiler_params=params(8),
        name="relay_add",
        cost_estimate=cost(2),
    )(near, back, ra, rb)


def plane_add_body(sc, *refs):
    me = sc[1]
    for block in range(2):
        own, ra, rb = refs[3 * block : 3 * block + 3]
        for turn in range(4):
            b = lax.rem(me + turn, 4)
            refs[6 + turn][block, :, 0] = own[:, 0, b] + (ra[:, 0, b] + rb[:, 0, b])


def plane_add(sc, blocks):
    n2 = blocks[0][0].shape[1]
    ins = pl.BlockSpec((2, 1, 4, 16, N), lambda k, sc: (0, k, 0, 0, 0))
    outs = pl.BlockSpec((2, 2, 1, 16, N), lambda k, sc: (0, 0, k, 0, 0))
    return pl.pallas_call(
        plane_add_body,
        grid_spec=pltpu.PrefetchScalarGridSpec(
            num_scalar_prefetch=1, grid=(n2,), in_specs=[ins] * 6, out_specs=[outs] * 4
        ),
        out_shape=[shape(2, 2, n2, 16, N)] * 4,
        compiler_params=params(16),
        name="plane_add",
        cost_estimate=cost(3),
    )(sc, *blocks[0], *blocks[1])


def line_add_body(sc, a, b, c, d, keep, send):
    core = sc[2]
    mine = pl.ds(pl.multiple_of(core * 8, 8), 8)
    other = pl.ds(pl.multiple_of((1 - core) * 8, 8), 8)
    for out, rows in ((keep, mine), (send, other)):
        for block in range(2):
            for j in range(2):
                out[block, j] = (a[block, j, :, rows] + b[block, j, :, rows]) + (
                    c[block, j, :, rows] + d[block, j, :, rows]
                )


def line_add(sc, arrays):
    dims = arrays[0].shape
    small = (*dims[:3], 8, N)
    return pl.pallas_call(
        line_add_body,
        grid_spec=pltpu.PrefetchScalarGridSpec(
            num_scalar_prefetch=1, grid=(1,), in_specs=[whole(*dims)] * 4, out_specs=[whole(*small)] * 2
        ),
        out_shape=[shape(*small)] * 2,
        compiler_params=params(16),
        name="line_add",
        cost_estimate=cost(2),
    )(sc, *arrays)


def pixel_body(sc, keep, recv, rows, mine, other):
    core, x = sc[2], sc[3]
    scale = 1.0 / math.sqrt(64)
    nm = mine.shape[1]

    def fill(part, ref):
        mine[part] = ref[x] * scale + rows[part].astype(f32)
        other[part] = ref[1 - x] * scale

    @pl.when(core == 0)
    def _():
        fill(0, keep)
        fill(1, recv)

    @pl.when(core != 0)
    def _():
        fill(0, recv)
        fill(1, keep)


def pixel_step(sc, keep, recv, rows):
    nm = rows.shape[1]
    dims = (2, nm, 8, N)
    return pl.pallas_call(
        pixel_body,
        grid_spec=pltpu.PrefetchScalarGridSpec(
            num_scalar_prefetch=1, grid=(1,), in_specs=[whole(*dims)] * 3, out_specs=[whole(*dims)] * 2
        ),
        out_shape=[shape(*dims)] * 2,
        compiler_params=params(8),
        name="pixel_step",
        cost_estimate=cost(2),
    )(sc, keep.reshape(dims), recv.reshape(dims), rows)


def mix_body(sc, w_ref, mine, b, c, d, out_ref):
    mode = sc[4]
    nm = mine.shape[1]
    for part in range(2):
        own = [mine[part, j] + b[part, j] for j in range(nm)]
        far = [c[part, j] + d[part, j] for j in range(nm)]
        for k in range(nm):
            row = mode * nm + k
            acc = jnp.zeros((8, N), f32)
            for j in range(nm):
                acc += (w_ref[row, mode * nm + j].astype(f32) / 16.0) * own[j]
                acc += (w_ref[row, (1 - mode) * nm + j].astype(f32) / 16.0) * far[j]
            out_ref[part, k] = acc.astype(bf16)


def mix(sc, mixing, mine, b, c, d):
    dims = mine.shape
    return pl.pallas_call(
        mix_body,
        grid_spec=pltpu.PrefetchScalarGridSpec(
            num_scalar_prefetch=2, grid=(1,), in_specs=[whole(*dims)] * 4, out_specs=whole(*dims)
        ),
        out_shape=shape(*dims, dtype=bf16),
        compiler_params=params(8),
        name="mix",
        cost_estimate=cost(2),
    )(sc, mixing, mine, b, c, d)


def object_body(sc, lights, obj, t0, t0f, t1, t1f, b0, b0f, b1, b1f, over0, over1, out_ref):
    i, j = pl.program_id(0), pl.program_id(1)
    own_i, own_j = i - sc[0], j - sc[1]
    over_j = j - sc[3]
    out_ref[...] = obj[...]
    most = lights[0]
    in_cols = jnp.logical_and(own_j >= 0, own_j < 2)

    def add(even, odd):
        for g in range(8):
            for block, values in ((0, even), (1, odd)):
                rows = slice(g * 32 + block * 16, g * 32 + block * 16 + 16)
                total = values[0][:, g]
                for v in values[1:]:
                    total = total + v[:, g]
                out_ref[:, rows, :] += total / most

    @pl.when(jnp.logical_and(in_cols, own_i == 0))
    def _():
        add((t0, t0f), (t1, t1f))

    @pl.when(jnp.logical_and(in_cols, own_i == 1))
    def _():
        add((b0, b0f), (b1, b1f))

    @pl.when(jnp.logical_and(jnp.logical_and(i == 0, sc[2] == 1), jnp.logical_and(over_j >= 0, over_j < 2)))
    def _():
        add((over0,), (over1,))


def object_update(sc, most, obj, pieces, over):
    own = pl.BlockSpec((2, 8, 16, H), lambda i, j, sc, li: (0, 0, 0, jnp.clip(j - sc[1], 0, 1)))
    specs = [
        pl.BlockSpec((None, 2, 8, 16, H), lambda i, j, sc, li, b=b: (b, 0, 0, 0, jnp.clip(j - sc[3], 0, 1)))
        for b in range(2)
    ]
    band = pl.BlockSpec((2, H, H), lambda i, j, sc, li: (0, i, j))
    return pl.pallas_call(
        object_body,
        grid_spec=pltpu.PrefetchScalarGridSpec(
            num_scalar_prefetch=2, grid=(2, 4), in_specs=[band] + [own] * 8 + specs, out_specs=band
        ),
        out_shape=shape(2, N, 4 * H),
        compiler_params=params(24),
        name="object_update",
        cost_estimate=cost(6),
    )(sc, most, obj, *pieces, over, over)


def over_body(b0, b0f, b1, b1f, out):
    out[0] = b0[...] + b0f[...]
    out[1] = b1[...] + b1f[...]


def over_sum(b0, b0f, b1, b1f):
    spec = pl.BlockSpec((2, 2, 16, N), lambda k: (0, k, 0, 0))
    return pl.pallas_call(
        over_body,
        grid=(4,),
        in_specs=[spec] * 4,
        out_specs=pl.BlockSpec((2, 2, 2, 16, N), lambda k: (0, 0, k, 0, 0)),
        out_shape=shape(2, 2, 8, 16, N),
        compiler_params=params(8),
        name="over_sum",
        cost_estimate=cost(2),
    )(b0, b0f, b1, b1f)


def tied(*values):
    return lax.optimization_barrier(values)


def per_device(object_field, probe, patterns, row_shift, col_start, mixing):
    minus, plus, wave_rows, back_rows = tables()
    y, z, x, core = (lax.axis_index(a) for a in SCAN)
    mode = lax.axis_index("mode")
    first = jnp.where(core == 0, y, z)
    second = jnp.where(core == 0, z, y)
    sc = jnp.stack([first, second, core, x, mode])
    core = core[None]
    place = jnp.concatenate([row_shift, col_start])
    before = along(place, 1)
    rim = along(rim_rows(before, object_field), -1)
    half_top, patch_top = top_half(place, object_field, probe, minus)
    own_light = light(probe)
    half_top, own_light = tied(half_top, own_light)
    half_bot, patch_bot, wave_top, sum_top = bottom_half(
        place, object_field, rim, probe, minus, wave_rows, half_top
    )
    far_top = swapped(sum_top, "mode")
    wave_bot, sum_bot = low_wave(wave_rows, half_top, half_bot)
    far_bot = swapped(sum_bot, "mode")
    fixed = fixed_top(patterns, sum_top, far_top, wave_top, plus)
    low, keep0, send0, top0, bot0 = first_block(
        core, patterns, sum_bot, far_bot, wave_bot, plus, back_rows, fixed, patch_top, patch_bot, probe
    )
    recv0 = swapped(send0, "core")
    bot0_far = swapped(bot0, "mode")
    top0_far = swapped(top0, "mode")
    keep1, send1, top1, bot1 = second_block(core, back_rows, fixed, low, patch_top, patch_bot, probe)
    bot1_far = swapped(bot1, "mode")
    top1_far = swapped(top1, "mode")
    far_light = swapped(own_light, "mode")
    recv1 = swapped(send1, "core")
    own0, near0, back0, far0a, far0b = core_add(sc, keep0, recv0)
    ra0, rb0 = turned(far0a, 1, True), turned(far0b, -1, True)
    keep1, recv1, bot0_far = tied(keep1, recv1, bot0_far)
    own1, near1, back1, far1a, far1b = core_add(sc, keep1, recv1)
    near0, back0 = relay_add(near0, back0, ra0, rb0)
    ra1, rb1 = turned(far1a, 1, True), turned(far1b, -1, True)
    plane0 = (own0, turned(near0, 1, True), turned(back0, -1, True))
    ra1, rb1, bot1_far = tied(ra1, rb1, bot1_far)
    over = along(over_sum(bot0, bot0_far, bot1, bot1_far), 1)
    near1, back1 = relay_add(near1, back1, ra1, rb1)
    plane1 = (own1, turned(near1, 1, True), turned(back1, -1, True))
    *plane1, top0_far = tied(*plane1, top0_far)
    line = plane_add(sc, (plane0, plane1))
    line = [line[0]] + [turned(line[r], r, False) for r in (1, 3, 2)]
    *line, top1_far = tied(*line, top1_far)
    keep, send = line_add(sc, line)
    rows = lax.dynamic_slice_in_dim(probe, lax.axis_index(SCAN) * 8, 8, 2)
    keep, far_light = tied(keep, far_light)
    most = jnp.max(own_light + far_light)[None]
    mine, other = pixel_step(sc, keep, swapped(send, "core"), rows)
    probe_new = mix(sc, mixing, mine, across(other, 0, 1), across(mine, 1, 0), across(other, 1, 1))
    pieces = (top0, top0_far, top1, top1_far, bot0, bot0_far, bot1, bot1_far)
    object_new = object_update(jnp.concatenate([place, before]), most, object_field, pieces, over)
    return object_new, probe_new


def solution(mesh):
    split = Mesh(mesh.devices.reshape(2, 4, 4, 2, 2), ("mode", *SCAN))
    return jax.shard_map(
        per_device,
        mesh=split,
        in_specs=(P(None, SCAN, None), P(None, "mode", None, None), P(SCAN, None, None), P(SCAN), P(SCAN), P()),
        out_specs=(P(None, SCAN, None), P(None, "mode", SCAN, None)),
        check_vma=False,
    )
```

```python
import functools
import math

import jax
import jax.numpy as jnp
import ml_dtypes
import numpy as np
from jax import lax
from jax.experimental import pallas as pl
from jax.experimental.pallas import tpu as pltpu
from jax.sharding import Mesh
from jax.sharding import PartitionSpec as P

f32, bf16 = jnp.float32, jnp.bfloat16
N = 512
H = 256
CHUNK = 32
PAIR = 2


def tables():
    i = np.arange(N, dtype=np.int32)
    angle = (i[:, None] * i[None, :] % N).astype(np.float32) * np.float32(2.0 * math.pi / N)
    factor = np.float32(1.0 / math.sqrt(N))
    c = (np.cos(angle) * factor).astype(ml_dtypes.bfloat16)
    s = (np.sin(angle) * factor).astype(ml_dtypes.bfloat16)
    minus = np.block([[c, -s], [s, c]])
    plus = np.block([[c, s], [-s, c]])

    def stacked(table):
        return table.reshape(2 * N, 2, 2, H).swapaxes(1, 2).reshape(2 * N, 2 * N)

    wave_rows = stacked(plus).reshape(2, 2, H, 2 * N).swapaxes(0, 1).reshape(2, N, 2 * N)
    back_rows = stacked(minus).reshape(2, 16, 2, 16, 2 * N).transpose(2, 0, 1, 3, 4).reshape(2, N, 2 * N)
    return minus, plus, wave_rows[0], wave_rows[1], back_rows[0], back_rows[1]


def shape(*dims, dtype=f32):
    return jax.ShapeDtypeStruct(dims, dtype)


def whole(*dims):
    return pl.BlockSpec(dims, lambda *_: (0,) * len(dims))


def params(mib):
    return pltpu.CompilerParams(vmem_limit_bytes=mib << 20)


SCALARS = pl.BlockSpec(memory_space=pltpu.SMEM)
LOCAL = pl.BlockSpec(memory_space=pltpu.VMEM)
FAR = pl.BlockSpec(memory_space=pltpu.HBM)


def local_call(body, name, ins, outs, scratch, mib, alias=None):
    def call(*args):
        return pl.pallas_call(
            body,
            in_specs=ins,
            out_specs=[LOCAL] * len(outs),
            out_shape=outs,
            scratch_shapes=scratch,
            compiler_params=params(mib),
            input_output_aliases=alias or {},
            name=name,
        )(*args)

    return call


def loop(count, fn, unroll=1):
    def body(i, carry):
        fn(i)
        return carry

    lax.fori_loop(0, count, body, 0, unroll=unroll)


def at(i, size, base=0):
    return pl.ds(pl.multiple_of(i * size + base, min(size, base) if base else size), size)


def exit_rows(p_ref, m, rows, o_r, o_i):
    pr = p_ref[0, m, rows, :].astype(f32)
    pi = p_ref[1, m, rows, :].astype(f32)
    return pr, pi, (pr * o_r - pi * o_i).astype(bf16), (pr * o_i + pi * o_r).astype(bf16)


def exit_half(p_ref, m, j, base, patch, x_s):
    def one(i):
        rows = at(i, CHUNK)
        _, _, xr, xi = exit_rows(p_ref, m, at(i, CHUNK, base), patch[0, rows, :], patch[1, rows, :])
        x_s[j, rows, :N] = xr
        x_s[j, rows, N:] = xi

    loop(H // CHUNK, one, 2)


def along_rows(x_s, table, out, m0):
    x = x_s[...].reshape(PAIR * H, 2 * N)
    half = jnp.dot(x, table[...], preferred_element_type=f32).astype(bf16)
    for j in range(PAIR):
        out[m0 + j, :H] = half[j * H : (j + 1) * H, :N]
        out[m0 + j, H:] = half[j * H : (j + 1) * H, N:]


def pairs(p_ref, fn):
    nm = p_ref
    loop(nm // PAIR, lambda k: fn(k * PAIR))


def top_body(sc, patch, p_ref, table, half_ref, own_half, far_half, x_s):
    base = sc[2] * H

    def lit(i):
        rows = pl.ds(pl.multiple_of(base + i * CHUNK, CHUNK), CHUNK)
        acc = jnp.zeros((CHUNK, N), f32)
        for m in range(p_ref.shape[1]):
            pr = p_ref[0, m, rows, :].astype(f32)
            pi = p_ref[1, m, rows, :].astype(f32)
            acc = acc + (pr * pr + pi * pi)
        own_half[at(i, CHUNK), :] = acc
        far_half[at(i, CHUNK), :] = acc

    loop(H // CHUNK, lit)

    def step(m0):
        for j in range(PAIR):
            exit_half(p_ref, m0 + j, j, 0, patch, x_s)
        along_rows(x_s, table, half_ref, m0)

    pairs(p_ref.shape[1], step)


def top_half(sc, patch, probe, table):
    nm = probe.shape[1]
    return local_call(
        top_body,
        "top_half",
        [SCALARS, LOCAL, LOCAL, LOCAL],
        [shape(nm, N, N, dtype=bf16), shape(H, N), shape(H, N)],
        [pltpu.VMEM((PAIR, H, 2 * N), bf16)],
        6,
    )(sc, patch, probe, table)


def wave_half(wave_ref, sum_ref, wt, top, bot, m0):
    for j in range(PAIR):
        m = m0 + j
        wave_ref[m] = jnp.dot(wt[:, :N], top[m], preferred_element_type=f32) + jnp.dot(
            wt[:, N:], bot[m], preferred_element_type=f32
        )

    def one(i):
        rows = at(i, CHUNK)
        low = at(i, CHUNK, H)
        acc = sum_ref[rows, :]
        for j in range(PAIR):
            a = wave_ref[m0 + j, rows, :]
            b = wave_ref[m0 + j, low, :]
            acc = acc + (a * a + b * b)
        sum_ref[rows, :] = acc

    loop(H // CHUNK, one, 2)


def bottom_body(place, own, rim, p_ref, table, wt, top, half_ref, patch_ref, wave_ref, sum_ref, x_s):
    @pl.when(place[0] == 0)
    def _():
        patch_ref[...] = own[...]

    @pl.when(place[0] != 0)
    def _():
        patch_ref[...] = rim[...]

    sum_ref[...] = jnp.zeros_like(sum_ref)

    def step(m0):
        for j in range(PAIR):
            exit_half(p_ref, m0 + j, j, H, patch_ref, x_s)
        along_rows(x_s, table, half_ref, m0)
        wave_half(wave_ref, sum_ref, wt, top, half_ref, m0)

    pairs(p_ref.shape[1], step)


def bottom_half(place, own, rim, probe, table, wave_rows, top):
    nm = probe.shape[1]
    return local_call(
        bottom_body,
        "bottom_half",
        [SCALARS] + [LOCAL] * 6,
        [shape(nm, N, N, dtype=bf16), shape(2, H, N), shape(nm, N, N), shape(H, N)],
        [pltpu.VMEM((PAIR, H, 2 * N), bf16)],
        8,
    )(place, own, rim, probe, table, wave_rows, top)


def low_wave_body(wt, top, bot, wave_ref, sum_ref):
    sum_ref[...] = jnp.zeros_like(sum_ref)
    pairs(top.shape[0], lambda m0: wave_half(wave_ref, sum_ref, wt, top, bot, m0))


def low_wave(wave_rows, top, bot):
    nm = top.shape[0]
    return local_call(
        low_wave_body, "low_wave", [LOCAL] * 3, [shape(nm, N, N), shape(H, N)], [], 5
    )(wave_rows, top, bot)


def set_scale(pat, base, s0, s1, scale_s):
    def one(i):
        rows = at(i, CHUNK)
        total = jnp.maximum(s0[rows, :] + s1[rows, :], 1.0)
        scale_s[rows, :] = jnp.sqrt(pat[0, at(i, CHUNK, base), :]) / jnp.sqrt(total)

    loop(H // CHUNK, one)


def fixed_half(wave_ref, table, half_ref, scale_s, x_s, m0):
    for j in range(PAIR):

        def one(i):
            rows = at(i, CHUNK)
            low = at(i, CHUNK, H)
            factor = scale_s[rows, :]
            x_s[j, rows, :N] = (wave_ref[m0 + j, rows, :] * factor).astype(bf16)
            x_s[j, rows, N:] = (wave_ref[m0 + j, low, :] * factor).astype(bf16)

        loop(H // CHUNK, one, 2)
    along_rows(x_s, table, half_ref, m0)


def fixed_top_body(pat, s0, s1, wave_ref, table, half_ref, scale_s, x_s):
    set_scale(pat, 0, s0, s1, scale_s)
    pairs(wave_ref.shape[0], lambda m0: fixed_half(wave_ref, table, half_ref, scale_s, x_s, m0))


SCALE = [pltpu.VMEM((H, N), f32), pltpu.VMEM((PAIR, H, 2 * N), bf16)]


def fixed_top(pat, s0, s1, wave, table):
    nm = wave.shape[0]
    return local_call(
        fixed_top_body, "fixed_top", [LOCAL] * 5, [shape(nm, N, N, dtype=bf16)], SCALE, 6
    )(pat, s0, s1, wave, table)[0]


def gradients(core, block, bt, top, bot, patch_top, patch_bot, p_ref, keep_ref, send_ref, gtop, gbot, back_s, m):
    back_s[...] = jnp.dot(bt[:, :N], top[m], preferred_element_type=f32) + jnp.dot(
        bt[:, N:], bot[m], preferred_element_type=f32
    )
    for patch, g_ref, base in ((patch_top, gtop, 0), (patch_bot, gbot, 8)):

        def one(i):
            g = i + base
            rows = pl.ds(pl.multiple_of(i * 32 + block * 16, 16), 16)
            full = pl.ds(pl.multiple_of(g * 32 + block * 16, 16), 16)
            o_r = patch[0, rows, :]
            o_i = patch[1, rows, :]
            pr, pi, xr, xi = exit_rows(p_ref, m, full, o_r, o_i)
            rr = back_s[at(g, 16), :] - xr.astype(f32)
            ri = back_s[pl.ds(pl.multiple_of(g * 16 + H, 16), 16), :] - xi.astype(f32)
            g_ref[0, i] += pr * rr + pi * ri
            g_ref[1, i] += pr * ri - pi * rr
            st0 = o_r * rr + o_i * ri
            st1 = o_r * ri - o_i * rr
            turned_g = (g % 4) * 4 + g // 4
            keep_ref[m, jnp.where(core == 0, g, turned_g)] = jnp.where(core == 0, st0, st1)
            send_ref[m, jnp.where(core == 0, turned_g, g)] = jnp.where(core == 0, st1, st0)

        loop(8, one, UNROLL)


UNROLL = 8
LIMIT = 4
GRADS = [shape(2, 8, 16, N)] * 2


def first_block_body(core, pat, s0, s1, wave_ref, table, bt, top, ptop, pbot, p_ref, half_ref, keep, send, gtop, gbot, scale_s, x_s, back_s):
    set_scale(pat, H, s0, s1, scale_s)
    gtop[...] = jnp.zeros_like(gtop)
    gbot[...] = jnp.zeros_like(gbot)

    def step(m0):
        fixed_half(wave_ref, table, half_ref, scale_s, x_s, m0)
        for j in range(PAIR):
            gradients(core[2], 0, bt, top, half_ref, ptop, pbot, p_ref, keep, send, gtop, gbot, back_s, m0 + j)

    pairs(wave_ref.shape[0], step)


def first_block(core, pat, s0, s1, wave, table, back_rows, top, ptop, pbot, probe):
    nm = wave.shape[0]
    return local_call(
        first_block_body,
        "first_block",
        [SCALARS] + [LOCAL] * 10,
        [shape(nm, N, N, dtype=bf16)] + [shape(nm, 16, 16, N)] * 2 + GRADS,
        SCALE + [pltpu.VMEM((N, N), f32)],
        9,
    )(core, pat, s0, s1, wave, table, back_rows, top, ptop, pbot, probe)


def second_block(core, back_rows, top, bot, ptop, pbot, probe, first, count, grads=None):
    nm = top.shape[0]
    half = [shape(2, 8, 16, N)] * 2

    def body(core, bt, top, bot, ptop, pbot, p_ref, *refs):
        if grads is None:
            keep, send, gtop, gbot, back_s = refs
            gtop[...] = jnp.zeros_like(gtop)
            gbot[...] = jnp.zeros_like(gbot)
        else:
            kin, sin, tin, bin_, keep, send, gtop, gbot, back_s = refs
        loop(
            count,
            lambda m: gradients(
                core[2], 1, bt, top, bot, ptop, pbot, p_ref, keep, send, gtop, gbot, back_s, m + first
            ),
        )

    given = [] if grads is None else grads
    return local_call(
        body,
        "second_block",
        [SCALARS] + [LOCAL] * (6 + len(given)),
        [shape(nm, 16, 16, N)] * 2 + half,
        [pltpu.VMEM((N, N), f32)],
        6,
        {7 + i: i for i in range(len(given))},
    )(core, back_rows, top, bot, ptop, pbot, probe, *given)


SCAN = ("y", "z", "x", "core")
RING = ("y", "z", "core")


def along(value, steps):
    count = lax.axis_size(SCAN)
    lo, hi = max(0, -steps), min(count, count - steps)
    return lax.ppermute(value, SCAN, [(i, i + steps) for i in range(lo, hi)])


def swapped(value, axis):
    return lax.ppermute(value, axis, [(0, 1), (1, 0)])


def turned(value, steps, first):
    flat = lambda y, z, core: (y * 4 + z) * 2 + core
    pairs = []
    for y in range(4):
        for z in range(4):
            for core in range(2):
                on_y = (core == 0) == first
                to = ((y + steps) % 4, z) if on_y else (y, (z + steps) % 4)
                pairs.append((flat(y, z, core), flat(*to, core)))
    return lax.ppermute(value, RING, pairs)


def across(value, flip_mode, flip_x):
    pairs = [(2 * m + x, 2 * (m ^ flip_mode) + (x ^ flip_x)) for m in range(2) for x in range(2)]
    return lax.ppermute(value, ("mode", "x"), pairs)


def window(obj, first, place):
    return obj.at[:, pl.ds(pl.multiple_of(first * H, H), H), pl.ds(pl.multiple_of(place[1] * H, H), N)]


def rim_body(place, obj, out, sem):
    copy = pltpu.make_async_copy(window(obj, 0, place), out, sem)
    copy.start()
    copy.wait()


def rim_rows(place, obj):
    return local_call(rim_body, "rim_rows", [SCALARS, FAR], [shape(2, H, N)], [pltpu.SemaphoreType.DMA], 60)(
        place, obj
    )[0]


def own_body(place, obj, top, bot, sems):
    copies = [
        pltpu.make_async_copy(window(obj, place[0], place), top, sems.at[0]),
        pltpu.make_async_copy(window(obj, 1, place), bot, sems.at[1]),
    ]
    for copy in copies:
        copy.start()
    for copy in copies:
        copy.wait()


def own_rows(place, obj):
    outs = [shape(2, H, N)] * 2
    return local_call(own_body, "own_rows", [SCALARS, FAR], outs, [pltpu.SemaphoreType.DMA((2,))], 60)(place, obj)


def brightest_body(own, far, out):
    def one(i, acc):
        return jnp.maximum(acc, own[at(i, 8), :] + far[at(i, 8), :])

    out[...] = lax.fori_loop(0, H // 8, one, jnp.zeros((8, N), f32))


def brightest(own, far):
    return local_call(brightest_body, "brightest", [LOCAL, LOCAL], [shape(8, N)], [], LIMIT)(own, far)[0]


def core_add_body(sc, keep, recv, own, near, back, far0, far1):
    me = sc[0]
    n2 = own.shape[1]
    for m in range(2 * n2):
        j, k = m // n2, m % n2
        for out, turn in ((own, 0), (near, 1), (back, 3)):
            a = at(lax.rem(me + turn, 4), 4)
            out[j, k] = keep[m, a] + recv[m, a]
        a = at(lax.rem(me + 2, 4), 4)
        (far0, far1)[j][k] = keep[m, a] + recv[m, a]


def core_add(sc, keep, recv):
    n2 = keep.shape[0] // 2
    outs = [shape(2, n2, 4, 16, N)] * 3 + [shape(n2, 4, 16, N)] * 2
    return local_call(core_add_body, "core_add", [SCALARS, LOCAL, LOCAL], outs, [], LIMIT)(sc, keep, recv)


def relay_body(a, b, ra, rb, oa, ob):
    oa[0] = a[0] + ra[...]
    ob[1] = b[1] + rb[...]


def relay_add(near, back, ra, rb):
    outs = [shape(*near.shape)] * 2
    return local_call(relay_body, "relay_add", [LOCAL] * 4, outs, [], LIMIT, {0: 0, 1: 1})(near, back, ra, rb)


def plane_add_body(sc, *refs):
    me = sc[1]
    for block in range(2):
        own, ra, rb = refs[3 * block : 3 * block + 3]
        for turn in range(4):
            b = lax.rem(me + turn, 4)
            refs[6 + turn][block] = own[:, :, b] + (ra[:, :, b] + rb[:, :, b])


def plane_add(sc, blocks):
    n2 = blocks[0][0].shape[1]
    outs = [shape(2, 2, n2, 16, N)] * 4
    return local_call(plane_add_body, "plane_add", [SCALARS] + [LOCAL] * 6, outs, [], LIMIT)(
        sc, *blocks[0], *blocks[1]
    )


def line_add_body(sc, a, b, c, d, keep, send):
    core = sc[2]
    for out, side in ((keep, core), (send, 1 - core)):
        rows = at(side, 8)
        for block in range(2):
            for j in range(2):
                out[block, j] = (a[block, j, :, rows] + b[block, j, :, rows]) + (
                    c[block, j, :, rows] + d[block, j, :, rows]
                )


def line_add(sc, arrays):
    dims = arrays[0].shape
    outs = [shape(*dims[:3], 8, N)] * 2
    return local_call(line_add_body, "line_add", [SCALARS] + [LOCAL] * 4, outs, [], LIMIT)(sc, *arrays)


def pixel_body(sc, keep, recv, rows, mine, other):
    core, x = sc[2], sc[3]
    scale = 1.0 / math.sqrt(64)

    def fill(part, ref):
        mine[part] = ref[x] * scale + rows[part].astype(f32)
        other[part] = ref[1 - x] * scale

    @pl.when(core == 0)
    def _():
        fill(0, keep)
        fill(1, recv)

    @pl.when(core != 0)
    def _():
        fill(0, recv)
        fill(1, keep)


def pixel_step(sc, keep, recv, rows):
    dims = rows.shape
    return local_call(pixel_body, "pixel_step", [SCALARS] + [LOCAL] * 3, [shape(*dims)] * 2, [], LIMIT)(
        sc, keep.reshape(dims), recv.reshape(dims), rows
    )


def mix_body(sc, w_ref, mine, b, c, d, out_ref):
    mode = sc[4]
    nm = mine.shape[1]
    for part in range(2):
        own = [mine[part, j] + b[part, j] for j in range(nm)]
        far = [c[part, j] + d[part, j] for j in range(nm)]
        for k in range(nm):
            row = mode * nm + k
            acc = jnp.zeros((8, N), f32)
            for j in range(nm):
                acc += (w_ref[row, mode * nm + j].astype(f32) / 16.0) * own[j]
                acc += (w_ref[row, (1 - mode) * nm + j].astype(f32) / 16.0) * far[j]
            out_ref[part, k] = acc.astype(bf16)


def mix(sc, mixing, mine, b, c, d):
    outs = [shape(*mine.shape, dtype=bf16)]
    return local_call(mix_body, "mix", [SCALARS] * 2 + [LOCAL] * 4, outs, [], LIMIT)(sc, mixing, mine, b, c, d)[0]


def object_body(place, before, near_max, far_max, obj, t0, t0f, t1, t1f, b0, b0f, b1, b1f, over, out, new, sems):
    shift, col = place[0], pl.multiple_of(place[1] * H, H)
    over_shift, over_col = before[0], pl.multiple_of(before[1] * H, H)
    largest = jnp.max(jnp.maximum(near_max[...], far_max[...]))
    copies = []
    for half in range(2):
        base = half * H

        def start(i):
            rows = at(i, CHUNK, base)
            new[:, rows, :] = obj[:, rows, :]

        loop(H // CHUNK, start, 2)

        def add(column, even, odd):
            def one(g):
                for block, values in ((0, even), (1, odd)):
                    rows = pl.ds(pl.multiple_of(g * 32 + base + block * 16, 16), 16)
                    total = values[0][:, g]
                    for v in values[1:]:
                        total = total + v[:, g]
                    new[:, rows, pl.ds(column, N)] += total / largest

            loop(8, one, 2)

        @pl.when(shift == half)
        def _():
            add(col, (t0, t0f), (t1, t1f))

        if half == 1:

            @pl.when(shift == 0)
            def _():
                add(col, (b0, b0f), (b1, b1f))

        else:

            @pl.when(over_shift == 1)
            def _():
                add(over_col, (over.at[0],), (over.at[1],))

        copy = pltpu.make_async_copy(new.at[:, pl.ds(base, H), :], out.at[:, pl.ds(base, H), :], sems.at[half])
        copy.start()
        copies.append(copy)
    for copy in copies:
        copy.wait()


def object_update(place, before, near_max, far_max, obj, pieces, over):
    return pl.pallas_call(
        object_body,
        in_specs=[SCALARS] * 2 + [LOCAL] * 12,
        out_specs=FAR,
        out_shape=shape(2, N, 4 * H),
        scratch_shapes=[pltpu.VMEM((2, N, 4 * H), f32), pltpu.SemaphoreType.DMA((2,))],
        compiler_params=params(10),
        name="object_update",
    )(place, before, near_max, far_max, obj, *pieces, over)


def over_body(b0, b0f, b1, b1f, out):
    out[0] = b0[...] + b0f[...]
    out[1] = b1[...] + b1f[...]


def over_sum(b0, b0f, b1, b1f):
    return local_call(over_body, "over_sum", [LOCAL] * 4, [shape(2, 2, 8, 16, N)], [], LIMIT)(b0, b0f, b1, b1f)[0]


def tied(*values):
    return lax.optimization_barrier(values)


def per_device(object_field, probe, patterns, row_shift, col_start, mixing):
    minus, plus, wave_top_rows, wave_bot_rows, back_rows0, back_rows1 = tables()
    y, z, x, core = (lax.axis_index(a) for a in SCAN)
    mode = lax.axis_index("mode")
    first = jnp.where(core == 0, y, z)
    second = jnp.where(core == 0, z, y)
    sc = jnp.stack([first, second, core, x, mode])
    place = jnp.concatenate([row_shift, col_start])
    before = along(place, 1)
    rows = lax.dynamic_slice_in_dim(probe, lax.axis_index(SCAN) * 8, 8, 2)
    before, place, sc, rows = tied(before, place, sc, rows)
    rim = along(rim_rows(before, object_field), -1)
    patch_top, own_bot = own_rows(place, object_field)
    half_top, own_light, light_out = top_half(sc, patch_top, probe, minus)
    rim, light_out, half_top = tied(rim, light_out, half_top)
    far_light = swapped(light_out, "mode")
    half_bot, patch_bot, wave_top, sum_top = bottom_half(
        place, own_bot, rim, probe, minus, wave_top_rows, half_top
    )
    far_top = swapped(sum_top, "mode")
    half_bot, far_light = tied(half_bot, far_light)
    wave_bot, sum_bot = low_wave(wave_bot_rows, half_top, half_bot)
    far_bot = swapped(sum_bot, "mode")
    fixed = fixed_top(patterns, sum_top, far_top, wave_top, plus)
    half_max = brightest(own_light, far_light)
    low, keep0, send0, top0, bot0 = first_block(
        sc, patterns, sum_bot, far_bot, wave_bot, plus, back_rows0, fixed, patch_top, patch_bot, probe
    )
    recv0 = swapped(send0, "core")
    bot0_far = swapped(bot0, "mode")
    top0_far = swapped(top0, "mode")
    part1 = second_block(sc, back_rows1, fixed, low, patch_top, patch_bot, probe, 0, 3)
    own0, near0, back0, far0a, far0b = core_add(sc, keep0, recv0)
    ra0, rb0 = turned(far0a, 1, True), turned(far0b, -1, True)
    *part1, near0 = tied(*part1, near0)
    keep1, send1, top1, bot1 = second_block(
        sc, back_rows1, fixed, low, patch_top, patch_bot, probe, 3, 3, part1
    )
    bot1_far = swapped(bot1, "mode")
    top1_far = swapped(top1, "mode")
    recv1 = swapped(send1, "core")
    near0, back0 = relay_add(near0, back0, ra0, rb0)
    keep1, near0, back0 = tied(keep1, near0, back0)
    own1, near1, back1, far1a, far1b = core_add(sc, keep1, recv1)
    ra1, rb1 = turned(far1a, 1, True), turned(far1b, -1, True)
    plane0 = (own0, turned(near0, 1, True), turned(back0, -1, True))
    ra1, rb1, bot0_far, *plane0 = tied(ra1, rb1, bot0_far, *plane0)
    near1, back1 = relay_add(near1, back1, ra1, rb1)
    plane1 = (own1, turned(near1, 1, True), turned(back1, -1, True))
    *plane1, bot1_far = tied(*plane1, bot1_far)
    over = along(over_sum(bot0, bot0_far, bot1, bot1_far), 1)
    line = plane_add(sc, (plane0, plane1))
    line = [line[0]] + [turned(line[r], r, False) for r in (1, 3, 2)]
    *line, top0_far = tied(*line, top0_far)
    keep, send = line_add(sc, line)
    far_max = swapped(half_max, "core")
    mine, other = pixel_step(sc, keep, swapped(send, "core"), rows)
    mine, other, over = tied(mine, other, over)
    probe_new = mix(sc, mixing, mine, across(other, 0, 1), across(mine, 1, 0), across(other, 1, 1))
    pieces = (top0, top0_far, top1, top1_far, bot0, bot0_far, bot1, bot1_far)
    object_new = object_update(place, before, half_max, far_max, object_field, pieces, over)
    return object_new, probe_new


def solution(mesh):
    split = Mesh(mesh.devices.reshape(2, 4, 4, 2, 2), ("mode", *SCAN))
    return jax.shard_map(
        per_device,
        mesh=split,
        in_specs=(P(None, SCAN, None), P(None, "mode", None, None), P(SCAN, None, None), P(SCAN), P(SCAN), P()),
        out_specs=(P(None, SCAN, None), P(None, "mode", SCAN, None)),
        check_vma=False,
    )
```

```python
import functools
import math

import jax
import jax.numpy as jnp
import ml_dtypes
import numpy as np
from jax import lax
from jax.experimental import pallas as pl
from jax.experimental.pallas import tpu as pltpu
from jax.sharding import Mesh
from jax.sharding import PartitionSpec as P

f32, bf16 = jnp.float32, jnp.bfloat16
N = 512
H = 256
CHUNK = 32
PAIR = 2


def tables():
    i = np.arange(N, dtype=np.int32)
    angle = (i[:, None] * i[None, :] % N).astype(np.float32) * np.float32(2.0 * math.pi / N)
    factor = np.float32(1.0 / math.sqrt(N))
    c = (np.cos(angle) * factor).astype(ml_dtypes.bfloat16)
    s = (np.sin(angle) * factor).astype(ml_dtypes.bfloat16)
    minus = np.block([[c, -s], [s, c]])
    plus = np.block([[c, s], [-s, c]])

    def stacked(table):
        return table.reshape(2 * N, 2, 2, H).swapaxes(1, 2).reshape(2 * N, 2 * N)

    wave_rows = stacked(plus).reshape(2, 2, H, 2 * N).swapaxes(0, 1).reshape(2, N, 2 * N)
    back_rows = stacked(minus).reshape(2, 16, 2, 16, 2 * N).transpose(2, 0, 1, 3, 4).reshape(2, N, 2 * N)
    return minus, plus, wave_rows[0], wave_rows[1], back_rows[0], back_rows[1]


def shape(*dims, dtype=f32):
    return jax.ShapeDtypeStruct(dims, dtype)


def whole(*dims):
    return pl.BlockSpec(dims, lambda *_: (0,) * len(dims))


def params(mib):
    return pltpu.CompilerParams(vmem_limit_bytes=mib << 20)


SCALARS = pl.BlockSpec(memory_space=pltpu.SMEM)
LOCAL = pl.BlockSpec(memory_space=pltpu.VMEM)
FAR = pl.BlockSpec(memory_space=pltpu.HBM)


def local_call(body, name, ins, outs, scratch, mib, alias=None, cost=None):
    def call(*args):
        return pl.pallas_call(
            body,
            in_specs=ins,
            out_specs=[LOCAL] * len(outs),
            out_shape=outs,
            scratch_shapes=scratch,
            compiler_params=params(mib),
            input_output_aliases=alias or {},
            name=name,
            cost_estimate=cost,
        )(*args)

    return call


def loop(count, fn, unroll=1):
    def body(i, carry):
        fn(i)
        return carry

    lax.fori_loop(0, count, body, 0, unroll=unroll)


def at(i, size, base=0):
    return pl.ds(pl.multiple_of(i * size + base, min(size, base) if base else size), size)


def here():
    y, z, x, core, mode = (lax.axis_index(a) for a in ("y", "z", "x", "core", "mode"))
    return jnp.where(core == 0, y, z), jnp.where(core == 0, z, y), core, x, mode


def exit_rows(p_ref, m, rows, o_r, o_i):
    pr = p_ref[0, m, rows, :].astype(f32)
    pi = p_ref[1, m, rows, :].astype(f32)
    return pr, pi, (pr * o_r - pi * o_i).astype(bf16), (pr * o_i + pi * o_r).astype(bf16)


def exit_half(p_ref, m, j, base, patch, x_s):
    def one(i):
        rows = at(i, CHUNK)
        _, _, xr, xi = exit_rows(p_ref, m, at(i, CHUNK, base), patch[0, rows, :], patch[1, rows, :])
        x_s[j, rows, :N] = xr
        x_s[j, rows, N:] = xi

    loop(H // CHUNK, one, 2)


def along_rows(x_s, table, out, m0):
    x = x_s[...].reshape(PAIR * H, 2 * N)
    half = jnp.dot(x, table[...], preferred_element_type=f32).astype(bf16)
    for j in range(PAIR):
        out[m0 + j, :H] = half[j * H : (j + 1) * H, :N]
        out[m0 + j, H:] = half[j * H : (j + 1) * H, N:]


def pairs(p_ref, fn):
    nm = p_ref
    loop(nm // PAIR, lambda k: fn(k * PAIR))


def window(place):
    return pl.ds(pl.multiple_of(place[1] * H, H), N)


def own_body(place, obj, top_ref, bot_ref, first_ref):
    columns = window(place)
    top = place[0] * H

    def take(i):
        rows = at(i, CHUNK)
        top_ref[:, rows, :] = obj[:, pl.ds(pl.multiple_of(top + i * CHUNK, CHUNK), CHUNK), columns]
        bot_ref[:, rows, :] = obj[:, at(i, CHUNK, H), columns]
        first_ref[:, rows, :] = obj[:, rows, :]

    loop(H // CHUNK, take, 2)


def own_rows(place, obj):
    return local_call(own_body, "own_rows", [SCALARS, LOCAL], [shape(2, H, N)] * 2 + [shape(2, H, 2 * N)], [], LIMIT)(
        place, obj
    )


def top_body(patch_ref, p_ref, table, half_ref, own_half, far_half, rows_ref, x_s):
    def step(m0):
        for j in range(PAIR):
            exit_half(p_ref, m0 + j, j, 0, patch_ref, x_s)
        along_rows(x_s, table, half_ref, m0)

    pairs(p_ref.shape[1], step)
    core = lax.axis_index("core")
    base = core * H

    def lit(i):
        rows = pl.ds(pl.multiple_of(base + i * CHUNK, CHUNK), CHUNK)
        acc = jnp.zeros((CHUNK, N), f32)
        for m in range(p_ref.shape[1]):
            pr = p_ref[0, m, rows, :].astype(f32)
            pi = p_ref[1, m, rows, :].astype(f32)
            acc = acc + (pr * pr + pi * pi)
        own_half[at(i, CHUNK), :] = acc
        far_half[at(i, CHUNK), :] = acc

    loop(H // CHUNK, lit)
    chip = (lax.axis_index("y") * 4 + lax.axis_index("z")) * 2 + lax.axis_index("x")
    for part in range(2):
        for m in range(p_ref.shape[1]):
            both = p_ref[part, m, at(chip, 16), :].astype(f32)
            rows_ref[part, m] = jnp.where(core == 0, both[:8], both[8:])


def top_half(patch, probe, table):
    nm = probe.shape[1]
    return local_call(
        top_body,
        "top_half",
        [LOCAL, LOCAL, LOCAL],
        [shape(nm, N, N, dtype=bf16), shape(H, N), shape(H, N), shape(2, nm, 8, N)],
        [pltpu.VMEM((PAIR, H, 2 * N), bf16)],
        6,
    )(patch, probe, table)


def wave_half(wave_ref, sum_ref, wt, top, bot, m0):
    for j in range(PAIR):
        m = m0 + j
        wave_ref[m] = jnp.dot(wt[:, :N], top[m], preferred_element_type=f32) + jnp.dot(
            wt[:, N:], bot[m], preferred_element_type=f32
        )

    def one(i):
        rows = at(i, CHUNK)
        low = at(i, CHUNK, H)
        acc = sum_ref[rows, :]
        for j in range(PAIR):
            a = wave_ref[m0 + j, rows, :]
            b = wave_ref[m0 + j, low, :]
            acc = acc + (a * a + b * b)
        sum_ref[rows, :] = acc

    loop(H // CHUNK, one, 2)


def bottom_body(place, own, rim, p_ref, table, wt, top, half_ref, patch_ref, wave_ref, sum_ref, x_s):
    @pl.when(place[0] == 0)
    def _():
        patch_ref[...] = own[...]

    @pl.when(place[0] != 0)
    def _():
        patch_ref[...] = rim[...]

    sum_ref[...] = jnp.zeros_like(sum_ref)

    def step(m0):
        for j in range(PAIR):
            exit_half(p_ref, m0 + j, j, H, patch_ref, x_s)
        along_rows(x_s, table, half_ref, m0)
        wave_half(wave_ref, sum_ref, wt, top, half_ref, m0)

    pairs(p_ref.shape[1], step)


def bottom_half(place, own, rim, probe, table, wave_rows, top):
    nm = probe.shape[1]
    return local_call(
        bottom_body,
        "bottom_half",
        [SCALARS] + [LOCAL] * 6,
        [shape(nm, N, N, dtype=bf16), shape(2, H, N), shape(nm, N, N), shape(H, N)],
        [pltpu.VMEM((PAIR, H, 2 * N), bf16)],
        8,
    )(place, own, rim, probe, table, wave_rows, top)


def low_wave_body(wt, top, bot, wave_ref, sum_ref):
    sum_ref[...] = jnp.zeros_like(sum_ref)
    pairs(top.shape[0], lambda m0: wave_half(wave_ref, sum_ref, wt, top, bot, m0))


def low_wave(wave_rows, top, bot):
    nm = top.shape[0]
    return local_call(
        low_wave_body, "low_wave", [LOCAL] * 3, [shape(nm, N, N), shape(H, N)], [], 5
    )(wave_rows, top, bot)


def set_scale(pat, base, s0, s1, scale_s):
    def one(i):
        rows = at(i, CHUNK)
        total = jnp.maximum(s0[rows, :] + s1[rows, :], 1.0)
        scale_s[rows, :] = jnp.sqrt(pat[0, at(i, CHUNK, base), :]) / jnp.sqrt(total)

    loop(H // CHUNK, one)


def fixed_half(wave_ref, table, half_ref, scale_s, x_s, m0):
    for j in range(PAIR):

        def one(i):
            rows = at(i, CHUNK)
            low = at(i, CHUNK, H)
            factor = scale_s[rows, :]
            x_s[j, rows, :N] = (wave_ref[m0 + j, rows, :] * factor).astype(bf16)
            x_s[j, rows, N:] = (wave_ref[m0 + j, low, :] * factor).astype(bf16)

        loop(H // CHUNK, one, 2)
    along_rows(x_s, table, half_ref, m0)


def fixed_top_body(pat, s0, s1, wave_ref, table, half_ref, scale_s, x_s):
    set_scale(pat, 0, s0, s1, scale_s)
    pairs(wave_ref.shape[0], lambda m0: fixed_half(wave_ref, table, half_ref, scale_s, x_s, m0))


SCALE = [pltpu.VMEM((H, N), f32), pltpu.VMEM((PAIR, H, 2 * N), bf16)]


def fixed_top(pat, s0, s1, wave, table):
    nm = wave.shape[0]
    return local_call(
        fixed_top_body, "fixed_top", [LOCAL] * 5, [shape(nm, N, N, dtype=bf16)], SCALE, 6
    )(pat, s0, s1, wave, table)[0]


def gradients(core, block, bt, top, bot, patch_top, patch_bot, p_ref, keep_ref, send_ref, gtop, gbot, back_s, m):
    back_s[...] = jnp.dot(bt[:, :N], top[m], preferred_element_type=f32) + jnp.dot(
        bt[:, N:], bot[m], preferred_element_type=f32
    )
    for patch, g_ref, base in ((patch_top, gtop, 0), (patch_bot, gbot, 8)):

        def one(i):
            g = i + base
            rows = pl.ds(pl.multiple_of(i * 32 + block * 16, 16), 16)
            full = pl.ds(pl.multiple_of(g * 32 + block * 16, 16), 16)
            o_r = patch[0, rows, :]
            o_i = patch[1, rows, :]
            pr, pi, xr, xi = exit_rows(p_ref, m, full, o_r, o_i)
            rr = back_s[at(g, 16), :] - xr.astype(f32)
            ri = back_s[pl.ds(pl.multiple_of(g * 16 + H, 16), 16), :] - xi.astype(f32)
            g_ref[0, i] += pr * rr + pi * ri
            g_ref[1, i] += pr * ri - pi * rr
            st0 = o_r * rr + o_i * ri
            st1 = o_r * ri - o_i * rr
            turned_g = (g % 4) * 4 + g // 4
            keep_ref[m, jnp.where(core == 0, g, turned_g)] = jnp.where(core == 0, st0, st1)
            send_ref[m, jnp.where(core == 0, turned_g, g)] = jnp.where(core == 0, st1, st0)

        loop(8, one, UNROLL)


UNROLL = 8
LIMIT = 4
STAGE = pl.CostEstimate(flops=int(5e9), transcendentals=0, bytes_accessed=int(15e6))
GRADS = [shape(2, 8, 16, N)] * 2


def first_block_body(pat, s0, s1, wave_ref, table, bt, top, ptop, pbot, p_ref, half_ref, keep, send, gtop, gbot, scale_s, x_s, back_s):
    set_scale(pat, H, s0, s1, scale_s)
    gtop[...] = jnp.zeros_like(gtop)
    gbot[...] = jnp.zeros_like(gbot)

    def step(m0):
        fixed_half(wave_ref, table, half_ref, scale_s, x_s, m0)
        for j in range(PAIR):
            gradients(lax.axis_index("core"), 0, bt, top, half_ref, ptop, pbot, p_ref, keep, send, gtop, gbot, back_s, m0 + j)

    pairs(wave_ref.shape[0], step)


def first_block(pat, s0, s1, wave, table, back_rows, top, ptop, pbot, probe):
    nm = wave.shape[0]
    return local_call(
        first_block_body,
        "first_block",
        [LOCAL] * 10,
        [shape(nm, N, N, dtype=bf16)] + [shape(nm, 16, 16, N)] * 2 + GRADS,
        SCALE + [pltpu.VMEM((N, N), f32)],
        9,
    )(pat, s0, s1, wave, table, back_rows, top, ptop, pbot, probe)


def second_block(back_rows, top, bot, ptop, pbot, probe, first, count, grads=None):
    nm = top.shape[0]
    half = [shape(2, 8, 16, N)] * 2

    def body(bt, top, bot, ptop, pbot, p_ref, *refs):
        if grads is None:
            keep, send, gtop, gbot, back_s = refs
            gtop[...] = jnp.zeros_like(gtop)
            gbot[...] = jnp.zeros_like(gbot)
        else:
            kin, sin, tin, bin_, keep, send, gtop, gbot, back_s = refs
        loop(
            count,
            lambda m: gradients(
                lax.axis_index("core"), 1, bt, top, bot, ptop, pbot, p_ref, keep, send, gtop, gbot, back_s, m + first
            ),
        )

    given = [] if grads is None else grads
    return local_call(
        body,
        "second_block",
        [LOCAL] * (6 + len(given)),
        [shape(nm, 16, 16, N)] * 2 + half,
        [pltpu.VMEM((N, N), f32)],
        6,
        {6 + i: i for i in range(len(given))},
    )(back_rows, top, bot, ptop, pbot, probe, *given)


SCAN = ("y", "z", "x", "core")
RING = ("y", "z", "core")


def along(value, steps):
    count = lax.axis_size(SCAN)
    lo, hi = max(0, -steps), min(count, count - steps)
    return lax.ppermute(value, SCAN, [(i, i + steps) for i in range(lo, hi)])


def swapped(value, axis):
    return lax.ppermute(value, axis, [(0, 1), (1, 0)])


def turned(value, steps, first):
    flat = lambda y, z, core: (y * 4 + z) * 2 + core
    pairs = []
    for y in range(4):
        for z in range(4):
            for core in range(2):
                on_y = (core == 0) == first
                to = ((y + steps) % 4, z) if on_y else (y, (z + steps) % 4)
                pairs.append((flat(y, z, core), flat(*to, core)))
    return lax.ppermute(value, RING, pairs)


def across(value, flip_mode, flip_x):
    pairs = [(2 * m + x, 2 * (m ^ flip_mode) + (x ^ flip_x)) for m in range(2) for x in range(2)]
    return lax.ppermute(value, ("mode", "x"), pairs)


def rim_body(place, obj, out):
    columns = window(place)

    def take(i):
        rows = at(i, CHUNK)
        out[:, rows, :] = obj[:, rows, columns]

    loop(H // CHUNK, take, 2)


def rim_rows(place, obj):
    return local_call(rim_body, "rim_rows", [SCALARS, LOCAL], [shape(2, H, N)], [], LIMIT)(place, obj)[0]


def brightest_body(own, far, out):
    def one(i, acc):
        return jnp.maximum(acc, own[at(i, 8), :] + far[at(i, 8), :])

    out[...] = lax.fori_loop(0, H // 8, one, jnp.zeros((8, N), f32))


def brightest(own, far):
    return local_call(brightest_body, "brightest", [LOCAL, LOCAL], [shape(8, N)], [], LIMIT, cost=STAGE)(own, far)[0]


def core_add_body(keep, recv, own, near, back, far0, far1):
    me = here()[0]
    n2 = own.shape[1]
    for m in range(2 * n2):
        j, k = m // n2, m % n2
        for out, turn in ((own, 0), (near, 1), (back, 3)):
            a = at(lax.rem(me + turn, 4), 4)
            out[j, k] = keep[m, a] + recv[m, a]
        a = at(lax.rem(me + 2, 4), 4)
        (far0, far1)[j][k] = keep[m, a] + recv[m, a]


def core_add(keep, recv):
    n2 = keep.shape[0] // 2
    outs = [shape(2, n2, 4, 16, N)] * 3 + [shape(n2, 4, 16, N)] * 2
    return local_call(core_add_body, "core_add", [LOCAL, LOCAL], outs, [], LIMIT, cost=STAGE)(keep, recv)


def relay_body(a, b, ra, rb, oa, ob):
    oa[0] = a[0] + ra[...]
    ob[1] = b[1] + rb[...]


def relay_add(near, back, ra, rb):
    outs = [shape(*near.shape)] * 2
    return local_call(relay_body, "relay_add", [LOCAL] * 4, outs, [], LIMIT, {0: 0, 1: 1}, cost=STAGE)(near, back, ra, rb)


def plane_add_body(*refs):
    me = here()[1]
    for block in range(2):
        own, ra, rb = refs[3 * block : 3 * block + 3]
        for turn in range(4):
            b = lax.rem(me + turn, 4)
            refs[6 + turn][block] = own[:, :, b] + (ra[:, :, b] + rb[:, :, b])


def plane_add(blocks):
    n2 = blocks[0][0].shape[1]
    outs = [shape(2, 2, n2, 16, N)] * 4
    return local_call(plane_add_body, "plane_add", [LOCAL] * 6, outs, [], LIMIT, cost=STAGE)(
        *blocks[0], *blocks[1]
    )


def line_add_body(a, b, c, d, keep, send):
    core = here()[2]
    for out, side in ((keep, core), (send, 1 - core)):
        rows = at(side, 8)
        for block in range(2):
            for j in range(2):
                out[block, j] = (a[block, j, :, rows] + b[block, j, :, rows]) + (
                    c[block, j, :, rows] + d[block, j, :, rows]
                )


def line_add(arrays):
    dims = arrays[0].shape
    outs = [shape(*dims[:3], 8, N)] * 2
    return local_call(line_add_body, "line_add", [LOCAL] * 4, outs, [], LIMIT, cost=STAGE)(*arrays)


def pixel_body(keep, recv, rows, mine, other):
    core, x = here()[2:4]
    scale = 1.0 / math.sqrt(64)

    def fill(part, ref):
        mine[part] = ref[x] * scale + rows[part]
        other[part] = ref[1 - x] * scale

    @pl.when(core == 0)
    def _():
        fill(0, keep)
        fill(1, recv)

    @pl.when(core != 0)
    def _():
        fill(0, recv)
        fill(1, keep)


def pixel_step(keep, recv, rows):
    dims = rows.shape
    return local_call(pixel_body, "pixel_step", [LOCAL] * 3, [shape(*dims)] * 2, [], LIMIT, cost=STAGE)(
        keep.reshape(dims), recv.reshape(dims), rows
    )


def mix_body(w_ref, mine, b, c, d, out_ref):
    mode = here()[4]
    nm = mine.shape[1]
    for part in range(2):
        own = [mine[part, j] + b[part, j] for j in range(nm)]
        far = [c[part, j] + d[part, j] for j in range(nm)]
        for k in range(nm):
            row = mode * nm + k
            acc = jnp.zeros((8, N), f32)
            for j in range(nm):
                acc += (w_ref[row, mode * nm + j].astype(f32) / 16.0) * own[j]
                acc += (w_ref[row, (1 - mode) * nm + j].astype(f32) / 16.0) * far[j]
            out_ref[part, k] = acc.astype(bf16)


def mix(mixing, mine, b, c, d):
    outs = [shape(*mine.shape, dtype=bf16)]
    return local_call(mix_body, "mix", [SCALARS] + [LOCAL] * 4, outs, [], LIMIT)(mixing, mine, b, c, d)[0]


def object_body(place, before, near_max, far_max, obj, t0, t0f, t1, t1f, b0, b0f, b1, b1f, over, out, new, sems):
    shift, col = place[0], pl.multiple_of(place[1] * H, H)
    over_shift, over_col = before[0], pl.multiple_of(before[1] * H, H)
    largest = jnp.max(jnp.maximum(near_max[...], far_max[...]))
    copies = []
    for half in range(2):
        base = half * H

        def start(i):
            rows = at(i, CHUNK, base)
            new[:, rows, :] = obj[:, rows, :]

        loop(H // CHUNK, start, 2)

        def add(column, even, odd):
            def one(g):
                for block, values in ((0, even), (1, odd)):
                    rows = pl.ds(pl.multiple_of(g * 32 + base + block * 16, 16), 16)
                    total = values[0][:, g]
                    for v in values[1:]:
                        total = total + v[:, g]
                    new[:, rows, pl.ds(column, N)] += total / largest

            loop(8, one, 2)

        @pl.when(shift == half)
        def _():
            add(col, (t0, t0f), (t1, t1f))

        if half == 1:

            @pl.when(shift == 0)
            def _():
                add(col, (b0, b0f), (b1, b1f))

        else:

            @pl.when(over_shift == 1)
            def _():
                add(over_col, (over.at[0],), (over.at[1],))

        copy = pltpu.make_async_copy(new.at[:, pl.ds(base, H), :], out.at[:, pl.ds(base, H), :], sems.at[half])
        copy.start()
        copies.append(copy)
    for copy in copies:
        copy.wait()


def object_update(place, before, near_max, far_max, obj, pieces, over):
    return pl.pallas_call(
        object_body,
        in_specs=[SCALARS] * 2 + [LOCAL] * 12,
        out_specs=FAR,
        out_shape=shape(2, N, 4 * H),
        scratch_shapes=[pltpu.VMEM((2, N, 4 * H), f32), pltpu.SemaphoreType.DMA((2,))],
        compiler_params=params(10),
        name="object_update",
    )(place, before, near_max, far_max, obj, *pieces, over)


def over_body(b0, b0f, b1, b1f, out):
    out[0] = b0[...] + b0f[...]
    out[1] = b1[...] + b1f[...]


def over_sum(b0, b0f, b1, b1f):
    return local_call(over_body, "over_sum", [LOCAL] * 4, [shape(2, 2, 8, 16, N)], [], LIMIT, cost=STAGE)(b0, b0f, b1, b1f)[0]


def tied(*values):
    return lax.optimization_barrier(values)


def per_device(object_field, probe, patterns, row_shift, col_start, mixing):
    minus, plus, wave_top_rows, wave_bot_rows, back_rows0, back_rows1 = tables()
    place = jnp.concatenate([row_shift, col_start])
    before = along(place, 1)
    patch_top, own_bot, first_rows = own_rows(place, object_field)
    before, patch_top = tied(before, patch_top)
    rim = along(rim_rows(before, first_rows), -1)
    half_top, own_light, light_out, rows = top_half(patch_top, probe, minus)
    rim, half_top, light_out = tied(rim, half_top, light_out)
    far_light = swapped(light_out, "mode")
    half_bot, patch_bot, wave_top, sum_top = bottom_half(
        place, own_bot, rim, probe, minus, wave_top_rows, half_top
    )
    far_top = swapped(sum_top, "mode")
    wave_bot, sum_bot = low_wave(wave_bot_rows, half_top, half_bot)
    far_bot = swapped(sum_bot, "mode")
    wave_top, far_light = tied(wave_top, far_light)
    fixed = fixed_top(patterns, sum_top, far_top, wave_top, plus)
    low, keep0, send0, top0, bot0 = first_block(
        patterns, sum_bot, far_bot, wave_bot, plus, back_rows0, fixed, patch_top, patch_bot, probe
    )
    recv0 = swapped(send0, "core")
    bot0_far = swapped(bot0, "mode")
    half_max = brightest(own_light, far_light)
    far_max = swapped(half_max, "core")
    part1 = second_block(back_rows1, fixed, low, patch_top, patch_bot, probe, 0, 3)
    own0, near0, back0, far0a, far0b = core_add(keep0, recv0)
    ra0, rb0 = turned(far0a, 1, True), turned(far0b, -1, True)
    *part1, near0 = tied(*part1, near0)
    keep1, send1, top1, bot1 = second_block(back_rows1, fixed, low, patch_top, patch_bot, probe, 3, 3, part1)
    recv1 = swapped(send1, "core")
    near0, back0 = relay_add(near0, back0, ra0, rb0)
    top0_next, bot0_far, _ = tied(top0, bot0_far, near0)
    top0_far = swapped(top0_next, "mode")
    bot1_next, top0_far = tied(bot1, top0_far)
    bot1_far = swapped(bot1_next, "mode")
    keep1, _, bot0_far = tied(keep1, near0, bot0_far)
    own1, near1, back1, far1a, far1b = core_add(keep1, recv1)
    ra1, rb1 = turned(far1a, 1, True), turned(far1b, -1, True)
    plane0 = (own0, turned(near0, 1, True), turned(back0, -1, True))
    ra1, rb1, top0_far, *plane0 = tied(ra1, rb1, top0_far, *plane0)
    near1, back1 = relay_add(near1, back1, ra1, rb1)
    plane1 = (own1, turned(near1, 1, True), turned(back1, -1, True))
    *plane1, bot1_far = tied(*plane1, bot1_far)
    top1_next, _ = tied(top1, plane1[1])
    top1_far = swapped(top1_next, "mode")
    over = along(over_sum(bot0, bot0_far, bot1, bot1_far), 1)
    line = plane_add((plane0, plane1))
    line = [line[0]] + [turned(line[r], r, False) for r in (1, 3, 2)]
    *line, top1_far, far_max = tied(*line, top1_far, far_max)
    keep, send = line_add(line)
    mine, other = pixel_step(keep, swapped(send, "core"), rows)
    mine, other, over = tied(mine, other, over)
    probe_new = mix(mixing, mine, across(other, 0, 1), across(mine, 1, 0), across(other, 1, 1))
    pieces = (top0, top0_far, top1, top1_far, bot0, bot0_far, bot1, bot1_far)
    object_new = object_update(place, before, half_max, far_max, object_field, pieces, over)
    return object_new, probe_new


def solution(mesh):
    split = Mesh(mesh.devices.reshape(2, 4, 4, 2, 2), ("mode", *SCAN))
    return jax.shard_map(
        per_device,
        mesh=split,
        in_specs=(P(None, SCAN, None), P(None, "mode", None, None), P(SCAN, None, None), P(SCAN), P(SCAN), P()),
        out_specs=(P(None, SCAN, None), P(None, "mode", SCAN, None)),
        check_vma=False,
    )
```

```python
import functools
import math

import jax
import jax.numpy as jnp
import ml_dtypes
import numpy as np
from jax import lax
from jax.experimental import pallas as pl
from jax.experimental.pallas import tpu as pltpu
from jax.sharding import Mesh
from jax.sharding import PartitionSpec as P

f32, bf16 = jnp.float32, jnp.bfloat16
N = 512
H = 256
CHUNK = 32
PAIR = 2


def tables():
    i = np.arange(N, dtype=np.int32)
    angle = (i[:, None] * i[None, :] % N).astype(np.float32) * np.float32(2.0 * math.pi / N)
    factor = np.float32(1.0 / math.sqrt(N))
    c = (np.cos(angle) * factor).astype(ml_dtypes.bfloat16)
    s = (np.sin(angle) * factor).astype(ml_dtypes.bfloat16)
    minus = np.block([[c, -s], [s, c]])
    plus = np.block([[c, s], [-s, c]])

    def stacked(table):
        return table.reshape(2 * N, 2, 2, H).swapaxes(1, 2).reshape(2 * N, 2 * N)

    wave_rows = stacked(plus).reshape(2, 2, H, 2 * N).swapaxes(0, 1).reshape(2, N, 2 * N)
    back_rows = stacked(minus).reshape(2, 16, 2, 16, 2 * N).transpose(2, 0, 1, 3, 4).reshape(2, N, 2 * N)
    return minus, plus, wave_rows[0], wave_rows[1], back_rows[0], back_rows[1]


def shape(*dims, dtype=f32):
    return jax.ShapeDtypeStruct(dims, dtype)


def whole(*dims):
    return pl.BlockSpec(dims, lambda *_: (0,) * len(dims))


def params(mib):
    return pltpu.CompilerParams(vmem_limit_bytes=mib << 20)


SCALARS = pl.BlockSpec(memory_space=pltpu.SMEM)
LOCAL = pl.BlockSpec(memory_space=pltpu.VMEM)
FAR = pl.BlockSpec(memory_space=pltpu.HBM)


def local_call(body, name, ins, outs, scratch, mib, alias=None, cost=None):
    def call(*args):
        return pl.pallas_call(
            body,
            in_specs=ins,
            out_specs=[LOCAL] * len(outs),
            out_shape=outs,
            scratch_shapes=scratch,
            compiler_params=params(mib),
            input_output_aliases=alias or {},
            name=name,
            cost_estimate=cost,
        )(*args)

    return call


def loop(count, fn, unroll=1):
    def body(i, carry):
        fn(i)
        return carry

    lax.fori_loop(0, count, body, 0, unroll=unroll)


def at(i, size, base=0):
    return pl.ds(pl.multiple_of(i * size + base, min(size, base) if base else size), size)


def here():
    y, z, x, core, mode = (lax.axis_index(a) for a in ("y", "z", "x", "core", "mode"))
    return jnp.where(core == 0, y, z), jnp.where(core == 0, z, y), core, x, mode


def exit_rows(p_ref, m, rows, o_r, o_i):
    pr = p_ref[0, m, rows, :].astype(f32)
    pi = p_ref[1, m, rows, :].astype(f32)
    return pr, pi, (pr * o_r - pi * o_i).astype(bf16), (pr * o_i + pi * o_r).astype(bf16)


def exit_half(p_ref, m, j, base, patch, x_s):
    def one(i):
        rows = at(i, CHUNK)
        _, _, xr, xi = exit_rows(p_ref, m, at(i, CHUNK, base), patch[0, rows, :], patch[1, rows, :])
        x_s[j, rows, :N] = xr
        x_s[j, rows, N:] = xi

    loop(H // CHUNK, one, 2)


def along_rows(x_s, table, out, m0):
    x = x_s[...].reshape(PAIR * H, 2 * N)
    half = jnp.dot(x, table[...], preferred_element_type=f32).astype(bf16)
    for j in range(PAIR):
        out[m0 + j, :H] = half[j * H : (j + 1) * H, :N]
        out[m0 + j, H:] = half[j * H : (j + 1) * H, N:]


def pairs(p_ref, fn):
    nm = p_ref
    loop(nm // PAIR, lambda k: fn(k * PAIR))


def window(place):
    return pl.ds(pl.multiple_of(place[1] * H, H), N)


def own_body(place, obj, top_ref, bot_ref, first_ref):
    columns = window(place)
    top = place[0] * H

    def take(i):
        rows = at(i, CHUNK)
        top_ref[:, rows, :] = obj[:, pl.ds(pl.multiple_of(top + i * CHUNK, CHUNK), CHUNK), columns]
        bot_ref[:, rows, :] = obj[:, at(i, CHUNK, H), columns]
        first_ref[:, rows, :] = obj[:, rows, :]

    loop(H // CHUNK, take, 2)


def own_rows(place, obj):
    return local_call(own_body, "own_rows", [SCALARS, LOCAL], [shape(2, H, N)] * 2 + [shape(2, H, 2 * N)], [], LIMIT)(
        place, obj
    )


def top_body(patch_ref, p_ref, table, half_ref, own_half, far_half, rows_ref, x_s):
    def step(m0):
        for j in range(PAIR):
            exit_half(p_ref, m0 + j, j, 0, patch_ref, x_s)
        along_rows(x_s, table, half_ref, m0)

    pairs(p_ref.shape[1], step)
    core = lax.axis_index("core")
    base = core * H

    def lit(i):
        rows = pl.ds(pl.multiple_of(base + i * CHUNK, CHUNK), CHUNK)
        acc = jnp.zeros((CHUNK, N), f32)
        for m in range(p_ref.shape[1]):
            pr = p_ref[0, m, rows, :].astype(f32)
            pi = p_ref[1, m, rows, :].astype(f32)
            acc = acc + (pr * pr + pi * pi)
        own_half[at(i, CHUNK), :] = acc
        far_half[at(i, CHUNK), :] = acc

    loop(H // CHUNK, lit)
    chip = (lax.axis_index("y") * 4 + lax.axis_index("z")) * 2 + lax.axis_index("x")
    for part in range(2):
        for m in range(p_ref.shape[1]):
            both = p_ref[part, m, at(chip, 16), :].astype(f32)
            rows_ref[part, m] = jnp.where(core == 0, both[:8], both[8:])


def top_half(patch, probe, table):
    nm = probe.shape[1]
    return local_call(
        top_body,
        "top_half",
        [LOCAL, LOCAL, LOCAL],
        [shape(nm, N, N, dtype=bf16), shape(H, N), shape(H, N), shape(2, nm, 8, N)],
        [pltpu.VMEM((PAIR, H, 2 * N), bf16)],
        6,
    )(patch, probe, table)


def wave_half(wave_ref, sum_ref, wt, top, bot, m0):
    for j in range(PAIR):
        m = m0 + j
        wave_ref[m] = jnp.dot(wt[:, :N], top[m], preferred_element_type=f32) + jnp.dot(
            wt[:, N:], bot[m], preferred_element_type=f32
        )

    def one(i):
        rows = at(i, CHUNK)
        low = at(i, CHUNK, H)
        acc = sum_ref[rows, :]
        for j in range(PAIR):
            a = wave_ref[m0 + j, rows, :]
            b = wave_ref[m0 + j, low, :]
            acc = acc + (a * a + b * b)
        sum_ref[rows, :] = acc

    loop(H // CHUNK, one, 2)


def bottom_body(place, own, rim, p_ref, table, wt, top, half_ref, patch_ref, wave_ref, sum_ref, x_s):
    @pl.when(place[0] == 0)
    def _():
        patch_ref[...] = own[...]

    @pl.when(place[0] != 0)
    def _():
        patch_ref[...] = rim[...]

    sum_ref[...] = jnp.zeros_like(sum_ref)

    def step(m0):
        for j in range(PAIR):
            exit_half(p_ref, m0 + j, j, H, patch_ref, x_s)
        along_rows(x_s, table, half_ref, m0)
        wave_half(wave_ref, sum_ref, wt, top, half_ref, m0)

    pairs(p_ref.shape[1], step)


def bottom_half(place, own, rim, probe, table, wave_rows, top):
    nm = probe.shape[1]
    return local_call(
        bottom_body,
        "bottom_half",
        [SCALARS] + [LOCAL] * 6,
        [shape(nm, N, N, dtype=bf16), shape(2, H, N), shape(nm, N, N), shape(H, N)],
        [pltpu.VMEM((PAIR, H, 2 * N), bf16)],
        8,
    )(place, own, rim, probe, table, wave_rows, top)


def low_wave_body(wt, top, bot, wave_ref, sum_ref):
    sum_ref[...] = jnp.zeros_like(sum_ref)
    pairs(top.shape[0], lambda m0: wave_half(wave_ref, sum_ref, wt, top, bot, m0))


def low_wave(wave_rows, top, bot):
    nm = top.shape[0]
    return local_call(
        low_wave_body, "low_wave", [LOCAL] * 3, [shape(nm, N, N), shape(H, N)], [], 5
    )(wave_rows, top, bot)


def set_scale(pat, base, s0, s1, scale_s):
    def one(i):
        rows = at(i, CHUNK)
        total = jnp.maximum(s0[rows, :] + s1[rows, :], 1.0)
        scale_s[rows, :] = jnp.sqrt(pat[0, at(i, CHUNK, base), :]) / jnp.sqrt(total)

    loop(H // CHUNK, one)


def fixed_half(wave_ref, table, half_ref, scale_s, x_s, m0):
    for j in range(PAIR):

        def one(i):
            rows = at(i, CHUNK)
            low = at(i, CHUNK, H)
            factor = scale_s[rows, :]
            x_s[j, rows, :N] = (wave_ref[m0 + j, rows, :] * factor).astype(bf16)
            x_s[j, rows, N:] = (wave_ref[m0 + j, low, :] * factor).astype(bf16)

        loop(H // CHUNK, one, 2)
    along_rows(x_s, table, half_ref, m0)


def fixed_top_body(pat, s0, s1, wave_ref, table, half_ref, scale_s, x_s):
    set_scale(pat, 0, s0, s1, scale_s)
    pairs(wave_ref.shape[0], lambda m0: fixed_half(wave_ref, table, half_ref, scale_s, x_s, m0))


SCALE = [pltpu.VMEM((H, N), f32), pltpu.VMEM((PAIR, H, 2 * N), bf16)]


def fixed_top(pat, s0, s1, wave, table):
    nm = wave.shape[0]
    return local_call(
        fixed_top_body, "fixed_top", [LOCAL] * 5, [shape(nm, N, N, dtype=bf16)], SCALE, 6
    )(pat, s0, s1, wave, table)[0]


def gradients(core, block, bt, top, bot, patch_top, patch_bot, p_ref, keep_ref, send_ref, grad, back_s, m):
    back_s[...] = jnp.dot(bt[:, :N], top[m], preferred_element_type=f32) + jnp.dot(
        bt[:, N:], bot[m], preferred_element_type=f32
    )
    for patch, side, base in ((patch_top, 0, 0), (patch_bot, 1, 8)):

        def one(i):
            g = i + base
            rows = pl.ds(pl.multiple_of(i * 32 + block * 16, 16), 16)
            full = pl.ds(pl.multiple_of(g * 32 + block * 16, 16), 16)
            o_r = patch[0, rows, :]
            o_i = patch[1, rows, :]
            pr, pi, xr, xi = exit_rows(p_ref, m, full, o_r, o_i)
            rr = back_s[at(g, 16), :] - xr.astype(f32)
            ri = back_s[pl.ds(pl.multiple_of(g * 16 + H, 16), 16), :] - xi.astype(f32)
            grad[side, 0, i] += pr * rr + pi * ri
            grad[side, 1, i] += pr * ri - pi * rr
            st0 = o_r * rr + o_i * ri
            st1 = o_r * ri - o_i * rr
            turned_g = (g % 4) * 4 + g // 4
            keep_ref[m, jnp.where(core == 0, g, turned_g)] = jnp.where(core == 0, st0, st1)
            send_ref[m, jnp.where(core == 0, turned_g, g)] = jnp.where(core == 0, st1, st0)

        loop(8, one, UNROLL)


UNROLL = 8
LIMIT = 4
STAGE = pl.CostEstimate(flops=int(5 * 1e9), transcendentals=0, bytes_accessed=int(5 * 3e6))
GRADS = [shape(2, 2, 8, 16, N)]


def first_block_body(pat, s0, s1, wave_ref, table, bt, top, ptop, pbot, p_ref, half_ref, keep, send, grad, scale_s, x_s, back_s):
    set_scale(pat, H, s0, s1, scale_s)
    grad[...] = jnp.zeros_like(grad)

    def step(m0):
        fixed_half(wave_ref, table, half_ref, scale_s, x_s, m0)
        for j in range(PAIR):
            gradients(lax.axis_index("core"), 0, bt, top, half_ref, ptop, pbot, p_ref, keep, send, grad, back_s, m0 + j)

    pairs(wave_ref.shape[0], step)


def first_block(pat, s0, s1, wave, table, back_rows, top, ptop, pbot, probe):
    nm = wave.shape[0]
    return local_call(
        first_block_body,
        "first_block",
        [LOCAL] * 10,
        [shape(nm, N, N, dtype=bf16)] + [shape(nm, 16, 16, N)] * 2 + GRADS,
        SCALE + [pltpu.VMEM((N, N), f32)],
        9,
    )(pat, s0, s1, wave, table, back_rows, top, ptop, pbot, probe)


def second_block(back_rows, top, bot, ptop, pbot, probe, first, count, grads=None):
    nm = top.shape[0]
    half = GRADS

    def body(bt, top, bot, ptop, pbot, p_ref, *refs):
        if grads is None:
            keep, send, grad, back_s = refs
            grad[...] = jnp.zeros_like(grad)
        else:
            keep, send, grad, back_s = refs[3:]
        loop(
            count,
            lambda m: gradients(
                lax.axis_index("core"), 1, bt, top, bot, ptop, pbot, p_ref, keep, send, grad, back_s, m + first
            ),
        )

    given = [] if grads is None else grads
    return local_call(
        body,
        "second_block",
        [LOCAL] * (6 + len(given)),
        [shape(nm, 16, 16, N)] * 2 + half,
        [pltpu.VMEM((N, N), f32)],
        6,
        {6 + i: i for i in range(len(given))},
    )(back_rows, top, bot, ptop, pbot, probe, *given)


SCAN = ("y", "z", "x", "core")
RING = ("y", "z", "core")


def along(value, steps):
    count = lax.axis_size(SCAN)
    lo, hi = max(0, -steps), min(count, count - steps)
    return lax.ppermute(value, SCAN, [(i, i + steps) for i in range(lo, hi)])


def swapped(value, axis):
    return lax.ppermute(value, axis, [(0, 1), (1, 0)])


def turned(value, steps, first):
    flat = lambda y, z, core: (y * 4 + z) * 2 + core
    pairs = []
    for y in range(4):
        for z in range(4):
            for core in range(2):
                on_y = (core == 0) == first
                to = ((y + steps) % 4, z) if on_y else (y, (z + steps) % 4)
                pairs.append((flat(y, z, core), flat(*to, core)))
    return lax.ppermute(value, RING, pairs)


def across(value, flip_mode, flip_x):
    pairs = [(2 * m + x, 2 * (m ^ flip_mode) + (x ^ flip_x)) for m in range(2) for x in range(2)]
    return lax.ppermute(value, ("mode", "x"), pairs)


def rim_body(place, obj, out):
    columns = window(place)

    def take(i):
        rows = at(i, CHUNK)
        out[:, rows, :] = obj[:, rows, columns]

    loop(H // CHUNK, take, 2)


def rim_rows(place, obj):
    return local_call(rim_body, "rim_rows", [SCALARS, LOCAL], [shape(2, H, N)], [], LIMIT)(place, obj)[0]


def brightest_body(own, far, out):
    def one(i, acc):
        return jnp.maximum(acc, own[at(i, 8), :] + far[at(i, 8), :])

    out[...] = lax.fori_loop(0, H // 8, one, jnp.zeros((8, N), f32))


def brightest(own, far):
    return local_call(brightest_body, "brightest", [LOCAL, LOCAL], [shape(8, N)], [], LIMIT, cost=STAGE)(own, far)[0]


def core_add_body(keep, recv, own, near, back, far0, far1):
    me = here()[0]
    n2 = own.shape[1]
    for m in range(2 * n2):
        j, k = m // n2, m % n2
        for out, turn in ((own, 0), (near, 1), (back, 3)):
            a = at(lax.rem(me + turn, 4), 4)
            out[j, k] = keep[m, a] + recv[m, a]
        a = at(lax.rem(me + 2, 4), 4)
        (far0, far1)[j][k] = keep[m, a] + recv[m, a]


def core_add(keep, recv):
    n2 = keep.shape[0] // 2
    outs = [shape(2, n2, 4, 16, N)] * 3 + [shape(n2, 4, 16, N)] * 2
    return local_call(core_add_body, "core_add", [LOCAL, LOCAL], outs, [], LIMIT, cost=STAGE)(keep, recv)


def relay_body(a, b, ra, rb, oa, ob):
    oa[0] = a[0] + ra[...]
    ob[1] = b[1] + rb[...]


def relay_add(near, back, ra, rb):
    outs = [shape(*near.shape)] * 2
    return local_call(relay_body, "relay_add", [LOCAL] * 4, outs, [], LIMIT, {0: 0, 1: 1}, cost=STAGE)(near, back, ra, rb)


def plane_add_body(*refs):
    me = here()[1]
    for block in range(2):
        own, ra, rb = refs[3 * block : 3 * block + 3]
        for turn in range(4):
            b = lax.rem(me + turn, 4)
            refs[6 + turn][block] = own[:, :, b] + (ra[:, :, b] + rb[:, :, b])


def plane_add(blocks):
    n2 = blocks[0][0].shape[1]
    outs = [shape(2, 2, n2, 16, N)] * 4
    return local_call(plane_add_body, "plane_add", [LOCAL] * 6, outs, [], LIMIT, cost=STAGE)(
        *blocks[0], *blocks[1]
    )


def line_add_body(a, b, c, d, keep, send):
    core = here()[2]
    for out, side in ((keep, core), (send, 1 - core)):
        rows = at(side, 8)
        for block in range(2):
            for j in range(2):
                out[block, j] = (a[block, j, :, rows] + b[block, j, :, rows]) + (
                    c[block, j, :, rows] + d[block, j, :, rows]
                )


def line_add(arrays):
    dims = arrays[0].shape
    outs = [shape(*dims[:3], 8, N)] * 2
    return local_call(line_add_body, "line_add", [LOCAL] * 4, outs, [], LIMIT, cost=STAGE)(*arrays)


def pixel_body(keep, recv, rows, mine, other):
    core, x = here()[2:4]
    scale = 1.0 / math.sqrt(64)

    def fill(part, ref):
        mine[part] = ref[x] * scale + rows[part]
        other[part] = ref[1 - x] * scale

    @pl.when(core == 0)
    def _():
        fill(0, keep)
        fill(1, recv)

    @pl.when(core != 0)
    def _():
        fill(0, recv)
        fill(1, keep)


def pixel_step(keep, recv, rows):
    dims = rows.shape
    return local_call(pixel_body, "pixel_step", [LOCAL] * 3, [shape(*dims)] * 2, [], LIMIT, cost=STAGE)(
        keep.reshape(dims), recv.reshape(dims), rows
    )


def mix_body(w_ref, mine, b, c, d, out_ref):
    mode = here()[4]
    nm = mine.shape[1]
    for part in range(2):
        own = [mine[part, j] + b[part, j] for j in range(nm)]
        far = [c[part, j] + d[part, j] for j in range(nm)]
        for k in range(nm):
            row = mode * nm + k
            acc = jnp.zeros((8, N), f32)
            for j in range(nm):
                acc += (w_ref[row, mode * nm + j].astype(f32) / 16.0) * own[j]
                acc += (w_ref[row, (1 - mode) * nm + j].astype(f32) / 16.0) * far[j]
            out_ref[part, k] = acc.astype(bf16)


def mix(mixing, mine, b, c, d):
    outs = [shape(*mine.shape, dtype=bf16)]
    return local_call(mix_body, "mix", [SCALARS] + [LOCAL] * 4, outs, [], LIMIT)(mixing, mine, b, c, d)[0]


def object_body(place, before, near_max, far_max, obj, g0, g0f, g1, g1f, over, out, new, sems):
    shift, col = place[0], pl.multiple_of(place[1] * H, H)
    over_shift, over_col = before[0], pl.multiple_of(before[1] * H, H)
    largest = jnp.max(jnp.maximum(near_max[...], far_max[...]))
    copies = []
    for half in range(2):
        base = half * H

        def start(i):
            rows = at(i, CHUNK, base)
            new[:, rows, :] = obj[:, rows, :]

        loop(H // CHUNK, start, 2)

        def add(column, even, odd):
            def one(g):
                for block, values in ((0, even), (1, odd)):
                    rows = pl.ds(pl.multiple_of(g * 32 + base + block * 16, 16), 16)
                    total = values[0][:, g]
                    for v in values[1:]:
                        total = total + v[:, g]
                    new[:, rows, pl.ds(column, N)] += total / largest

            loop(8, one, 2)

        @pl.when(shift == half)
        def _():
            add(col, (g0.at[0], g0f.at[0]), (g1.at[0], g1f.at[0]))

        if half == 1:

            @pl.when(shift == 0)
            def _():
                add(col, (g0.at[1], g0f.at[1]), (g1.at[1], g1f.at[1]))

        else:

            @pl.when(over_shift == 1)
            def _():
                add(over_col, (over.at[0],), (over.at[1],))

        copy = pltpu.make_async_copy(new.at[:, pl.ds(base, H), :], out.at[:, pl.ds(base, H), :], sems.at[half])
        copy.start()
        copies.append(copy)
    for copy in copies:
        copy.wait()


def object_update(place, before, near_max, far_max, obj, pieces, over):
    return pl.pallas_call(
        object_body,
        in_specs=[SCALARS] * 2 + [LOCAL] * 8,
        out_specs=FAR,
        out_shape=shape(2, N, 4 * H),
        scratch_shapes=[pltpu.VMEM((2, N, 4 * H), f32), pltpu.SemaphoreType.DMA((2,))],
        compiler_params=params(10),
        name="object_update",
    )(place, before, near_max, far_max, obj, *pieces, over)


def over_body(g0, g0f, g1, g1f, out):
    out[0] = g0[1] + g0f[1]
    out[1] = g1[1] + g1f[1]


def over_sum(*pieces):
    outs = [shape(2, 2, 8, 16, N)]
    return local_call(over_body, "over_sum", [LOCAL] * 4, outs, [], LIMIT, cost=STAGE)(*pieces)[0]


def tied(*values):
    return lax.optimization_barrier(values)


def per_device(object_field, probe, patterns, row_shift, col_start, mixing):
    minus, plus, wave_top_rows, wave_bot_rows, back_rows0, back_rows1 = tables()
    place = jnp.concatenate([row_shift, col_start])
    before = along(place, 1)
    patch_top, own_bot, first_rows = own_rows(place, object_field)
    before, patch_top = tied(before, patch_top)
    rim = along(rim_rows(before, first_rows), -1)
    half_top, own_light, light_out, rows = top_half(patch_top, probe, minus)
    rim, half_top, light_out = tied(rim, half_top, light_out)
    far_light = swapped(light_out, "mode")
    half_bot, patch_bot, wave_top, sum_top = bottom_half(
        place, own_bot, rim, probe, minus, wave_top_rows, half_top
    )
    far_top = swapped(sum_top, "mode")
    wave_bot, sum_bot = low_wave(wave_bot_rows, half_top, half_bot)
    far_bot = swapped(sum_bot, "mode")
    wave_top, far_light = tied(wave_top, far_light)
    fixed = fixed_top(patterns, sum_top, far_top, wave_top, plus)
    low, keep0, send0, grad0 = first_block(
        patterns, sum_bot, far_bot, wave_bot, plus, back_rows0, fixed, patch_top, patch_bot, probe
    )
    recv0 = swapped(send0, "core")
    grad0_far = swapped(grad0, "mode")
    part1 = second_block(back_rows1, fixed, low, patch_top, patch_bot, probe, 0, 3)
    own0, near0, back0, far0a, far0b = core_add(keep0, recv0)
    ra0, rb0 = turned(far0a, 1, True), turned(far0b, -1, True)
    *part1, near0 = tied(*part1, near0)
    keep1, send1, grad1 = second_block(back_rows1, fixed, low, patch_top, patch_bot, probe, 3, 3, part1)
    recv1 = swapped(send1, "core")
    near0, back0 = relay_add(near0, back0, ra0, rb0)
    keep1, _ = tied(keep1, near0)
    own1, near1, back1, far1a, far1b = core_add(keep1, recv1)
    ra1, rb1 = turned(far1a, 1, True), turned(far1b, -1, True)
    plane0 = (own0, turned(near0, 1, True), turned(back0, -1, True))
    ra1, rb1, grad0_far, *plane0 = tied(ra1, rb1, grad0_far, *plane0)
    grad1_next, _ = tied(grad1, grad0_far)
    grad1_far = swapped(grad1_next, "mode")
    near1, back1 = relay_add(near1, back1, ra1, rb1)
    plane1 = (own1, turned(near1, 1, True), turned(back1, -1, True))
    half_max = brightest(own_light, far_light)
    far_max = swapped(half_max, "core")
    line = plane_add((plane0, plane1))
    line = [line[0]] + [turned(line[r], r, False) for r in (1, 3, 2)]
    *line, far_max, grad1_far = tied(*line, far_max, grad1_far)
    over = along(over_sum(grad0, grad0_far, grad1, grad1_far), 1)
    keep, send = line_add(line)
    mine, other = pixel_step(keep, swapped(send, "core"), rows)
    probe_new = mix(mixing, mine, across(other, 0, 1), across(mine, 1, 0), across(other, 1, 1))
    object_new = object_update(
        place, before, half_max, far_max, object_field, (grad0, grad0_far, grad1, grad1_far), over
    )
    return object_new, probe_new


def solution(mesh):
    split = Mesh(mesh.devices.reshape(2, 4, 4, 2, 2), ("mode", *SCAN))
    return jax.shard_map(
        per_device,
        mesh=split,
        in_specs=(P(None, SCAN, None), P(None, "mode", None, None), P(SCAN, None, None), P(SCAN), P(SCAN), P()),
        out_specs=(P(None, SCAN, None), P(None, "mode", SCAN, None)),
        check_vma=False,
    )
```

```python
import functools
import math

import jax
import jax.numpy as jnp
import ml_dtypes
import numpy as np
from jax import lax
from jax.experimental import pallas as pl
from jax.experimental.pallas import tpu as pltpu
from jax.sharding import Mesh
from jax.sharding import PartitionSpec as P

f32, bf16 = jnp.float32, jnp.bfloat16
N = 512
H = 256
CHUNK = 32
QUARTER = 128
PAIR = 2


def tables():
    i = np.arange(N, dtype=np.int32)
    angle = (i[:, None] * i[None, :] % N).astype(np.float32) * np.float32(2.0 * math.pi / N)
    factor = np.float32(1.0 / math.sqrt(N))
    c = (np.cos(angle) * factor).astype(ml_dtypes.bfloat16)
    s = (np.sin(angle) * factor).astype(ml_dtypes.bfloat16)
    minus = np.block([[c, -s], [s, c]])
    plus = np.block([[c, s], [-s, c]])

    def stacked(table):
        return table.reshape(2 * N, 2, 2, H).swapaxes(1, 2).reshape(2 * N, 2 * N)

    wave_rows = stacked(plus).reshape(2, 2, H, 2 * N).swapaxes(0, 1).reshape(2, N, 2 * N)
    back_rows = stacked(minus).reshape(2, 16, 2, 16, 2 * N).transpose(2, 0, 1, 3, 4).reshape(2, N, 2 * N)
    return minus, plus, wave_rows[0], wave_rows[1], back_rows[0], back_rows[1]


def shape(*dims, dtype=f32):
    return jax.ShapeDtypeStruct(dims, dtype)


def whole(*dims):
    return pl.BlockSpec(dims, lambda *_: (0,) * len(dims))


def params(mib):
    return pltpu.CompilerParams(vmem_limit_bytes=mib << 20)


SCALARS = pl.BlockSpec(memory_space=pltpu.SMEM)
LOCAL = pl.BlockSpec(memory_space=pltpu.VMEM)
FAR = pl.BlockSpec(memory_space=pltpu.HBM)


def local_call(body, name, ins, outs, scratch, mib, alias=None, cost=None):
    def call(*args):
        return pl.pallas_call(
            body,
            in_specs=ins,
            out_specs=[LOCAL] * len(outs),
            out_shape=outs,
            scratch_shapes=scratch,
            compiler_params=params(mib),
            input_output_aliases=alias or {},
            name=name,
            cost_estimate=cost,
        )(*args)

    return call


def loop(count, fn, unroll=1):
    def body(i, carry):
        fn(i)
        return carry

    lax.fori_loop(0, count, body, 0, unroll=unroll)


def at(i, size, base=0):
    return pl.ds(pl.multiple_of(i * size + base, min(size, base) if base else size), size)


def here():
    y, z, x, core, mode = (lax.axis_index(a) for a in ("y", "z", "x", "core", "mode"))
    return jnp.where(core == 0, y, z), jnp.where(core == 0, z, y), core, x, mode


def exit_rows(p_ref, m, rows, o_r, o_i):
    pr = p_ref[0, m, rows, :].astype(f32)
    pi = p_ref[1, m, rows, :].astype(f32)
    return pr, pi, (pr * o_r - pi * o_i).astype(bf16), (pr * o_i + pi * o_r).astype(bf16)


def exit_half(p_ref, m, j, base, patch, x_s):
    def one(i):
        rows = at(i, CHUNK)
        _, _, xr, xi = exit_rows(p_ref, m, at(i, CHUNK, base), patch[0, rows, :], patch[1, rows, :])
        x_s[j, rows, :N] = xr
        x_s[j, rows, N:] = xi

    loop(H // CHUNK, one, 2)


def along_rows(x_s, table, out, m0):
    x = x_s[...].reshape(PAIR * H, 2 * N)
    half = jnp.dot(x, table[...], preferred_element_type=f32).astype(bf16)
    for j in range(PAIR):
        out[m0 + j, :H] = half[j * H : (j + 1) * H, :N]
        out[m0 + j, H:] = half[j * H : (j + 1) * H, N:]


def pairs(p_ref, fn):
    nm = p_ref
    loop(nm // PAIR, lambda k: fn(k * PAIR))


def window(place):
    return pl.ds(pl.multiple_of(place[1] * H, H), N)


def own_body(place, obj, top_ref, bot_ref, first_ref):
    columns = window(place)
    top = place[0] * H

    def take(i):
        rows = at(i, CHUNK)
        top_ref[:, rows, :] = obj[:, pl.ds(pl.multiple_of(top + i * CHUNK, CHUNK), CHUNK), columns]
        bot_ref[:, rows, :] = obj[:, at(i, CHUNK, H), columns]
        first_ref[:, rows, :] = obj[:, rows, :]

    loop(H // CHUNK, take, 2)


def own_rows(place, obj):
    return local_call(own_body, "own_rows", [SCALARS, LOCAL], [shape(2, H, N)] * 2 + [shape(2, H, 2 * N)], [], LIMIT)(
        place, obj
    )


def top_body(patch_ref, p_ref, table, half_ref, own_part, far_part, rows_ref, x_s):
    def step(m0):
        for j in range(PAIR):
            exit_half(p_ref, m0 + j, j, 0, patch_ref, x_s)
        along_rows(x_s, table, half_ref, m0)

    pairs(p_ref.shape[1], step)
    core, x = lax.axis_index("core"), lax.axis_index("x")
    base = (core * 2 + x) * QUARTER

    def lit(i):
        rows = pl.ds(pl.multiple_of(base + i * CHUNK, CHUNK), CHUNK)
        acc = jnp.zeros((CHUNK, N), f32)
        for m in range(p_ref.shape[1]):
            pr = p_ref[0, m, rows, :].astype(f32)
            pi = p_ref[1, m, rows, :].astype(f32)
            acc = acc + (pr * pr + pi * pi)
        own_part[at(i, CHUNK), :] = acc
        far_part[at(i, CHUNK), :] = acc

    loop(QUARTER // CHUNK, lit)
    chip = (lax.axis_index("y") * 4 + lax.axis_index("z")) * 2 + lax.axis_index("x")
    for part in range(2):
        for m in range(p_ref.shape[1]):
            both = p_ref[part, m, at(chip, 16), :].astype(f32)
            rows_ref[part, m] = jnp.where(core == 0, both[:8], both[8:])


def top_half(patch, probe, table):
    nm = probe.shape[1]
    return local_call(
        top_body,
        "top_half",
        [LOCAL, LOCAL, LOCAL],
        [shape(nm, N, N, dtype=bf16), shape(QUARTER, N), shape(QUARTER, N), shape(2, nm, 8, N)],
        [pltpu.VMEM((PAIR, H, 2 * N), bf16)],
        6,
    )(patch, probe, table)


def first_terms_body(wt0, wt1, top, wave0, wave1):
    def step(m):
        wave0[m] = jnp.dot(wt0[:, :N], top[m], preferred_element_type=f32)
        wave1[m] = jnp.dot(wt1[:, :N], top[m], preferred_element_type=f32)

    loop(top.shape[0], step)


def first_terms(wt0, wt1, top):
    nm = top.shape[0]
    return local_call(first_terms_body, "first_terms", [LOCAL] * 3, [shape(nm, N, N)] * 2, [], 5)(wt0, wt1, top)


def wave_half(wave_ref, sum_ref, wt, bot, m0):
    for j in range(PAIR):
        m = m0 + j
        wave_ref[m] += jnp.dot(wt[:, N:], bot[m], preferred_element_type=f32)

    def one(i):
        rows = at(i, CHUNK)
        low = at(i, CHUNK, H)
        acc = sum_ref[rows, :]
        for j in range(PAIR):
            a = wave_ref[m0 + j, rows, :]
            b = wave_ref[m0 + j, low, :]
            acc = acc + (a * a + b * b)
        sum_ref[rows, :] = acc

    loop(H // CHUNK, one, 2)


def bottom_body(place, own, rim, p_ref, table, wt, _, half_ref, patch_ref, wave_ref, sum_ref, x_s):
    @pl.when(place[0] == 0)
    def _():
        patch_ref[...] = own[...]

    @pl.when(place[0] != 0)
    def _():
        patch_ref[...] = rim[...]

    sum_ref[...] = jnp.zeros_like(sum_ref)

    def step(m0):
        for j in range(PAIR):
            exit_half(p_ref, m0 + j, j, H, patch_ref, x_s)
        along_rows(x_s, table, half_ref, m0)
        wave_half(wave_ref, sum_ref, wt, half_ref, m0)

    pairs(p_ref.shape[1], step)


def bottom_half(place, own, rim, probe, table, wave_rows, wave):
    nm = probe.shape[1]
    return local_call(
        bottom_body,
        "bottom_half",
        [SCALARS] + [LOCAL] * 6,
        [shape(nm, N, N, dtype=bf16), shape(2, H, N), shape(nm, N, N), shape(H, N)],
        [pltpu.VMEM((PAIR, H, 2 * N), bf16)],
        8,
        {6: 2},
    )(place, own, rim, probe, table, wave_rows, wave)


def low_wave_body(wt, bot, _, wave_ref, sum_ref):
    sum_ref[...] = jnp.zeros_like(sum_ref)
    pairs(bot.shape[0], lambda m0: wave_half(wave_ref, sum_ref, wt, bot, m0))


def low_wave(wave_rows, bot, wave):
    outs = [shape(*wave.shape), shape(H, N)]
    return local_call(low_wave_body, "low_wave", [LOCAL] * 3, outs, [], 5, {2: 0})(wave_rows, bot, wave)


def set_scale(pat, base, s0, s1, scale_s):
    def one(i):
        rows = at(i, CHUNK)
        total = jnp.maximum(s0[rows, :] + s1[rows, :], 1.0)
        scale_s[rows, :] = jnp.sqrt(pat[0, at(i, CHUNK, base), :]) / jnp.sqrt(total)

    loop(H // CHUNK, one)


def fixed_half(wave_ref, table, half_ref, scale_s, x_s, m0):
    for j in range(PAIR):

        def one(i):
            rows = at(i, CHUNK)
            low = at(i, CHUNK, H)
            factor = scale_s[rows, :]
            x_s[j, rows, :N] = (wave_ref[m0 + j, rows, :] * factor).astype(bf16)
            x_s[j, rows, N:] = (wave_ref[m0 + j, low, :] * factor).astype(bf16)

        loop(H // CHUNK, one, 2)
    along_rows(x_s, table, half_ref, m0)


def fixed_top_body(pat, s0, s1, wave_ref, table, half_ref, scale_s, x_s):
    set_scale(pat, 0, s0, s1, scale_s)
    pairs(wave_ref.shape[0], lambda m0: fixed_half(wave_ref, table, half_ref, scale_s, x_s, m0))


SCALE = [pltpu.VMEM((H, N), f32), pltpu.VMEM((PAIR, H, 2 * N), bf16)]


def fixed_top(pat, s0, s1, wave, table):
    nm = wave.shape[0]
    return local_call(
        fixed_top_body, "fixed_top", [LOCAL] * 5, [shape(nm, N, N, dtype=bf16)], SCALE, 6
    )(pat, s0, s1, wave, table)[0]


def gradients(core, block, bt, top, bot, patch_top, patch_bot, p_ref, keep_ref, send_ref, gtop, gbot, back_s, m):
    back_s[...] = jnp.dot(bt[:, :N], top[m], preferred_element_type=f32) + jnp.dot(
        bt[:, N:], bot[m], preferred_element_type=f32
    )
    for patch, g_ref, base in ((patch_top, gtop, 0), (patch_bot, gbot, 8)):

        def one(i):
            g = i + base
            rows = pl.ds(pl.multiple_of(i * 32 + block * 16, 16), 16)
            full = pl.ds(pl.multiple_of(g * 32 + block * 16, 16), 16)
            o_r = patch[0, rows, :]
            o_i = patch[1, rows, :]
            pr, pi, xr, xi = exit_rows(p_ref, m, full, o_r, o_i)
            rr = back_s[at(g, 16), :] - xr.astype(f32)
            ri = back_s[pl.ds(pl.multiple_of(g * 16 + H, 16), 16), :] - xi.astype(f32)
            g_ref[0, i] += pr * rr + pi * ri
            g_ref[1, i] += pr * ri - pi * rr
            st0 = o_r * rr + o_i * ri
            st1 = o_r * ri - o_i * rr
            turned_g = (g % 4) * 4 + g // 4
            keep_ref[m, jnp.where(core == 0, g, turned_g)] = jnp.where(core == 0, st0, st1)
            send_ref[m, jnp.where(core == 0, turned_g, g)] = jnp.where(core == 0, st1, st0)

        loop(8, one, UNROLL)


UNROLL = 8
LIMIT = 4
STAGE = pl.CostEstimate(flops=int(5e9), transcendentals=0, bytes_accessed=int(15e6))
GRADS = [shape(2, 8, 16, N), shape(2, 2, 8, 16, N)]


def first_block_body(pat, s0, s1, wave_ref, table, bt, top, ptop, pbot, p_ref, half_ref, keep, send, gbot, tops, scale_s, x_s, back_s):
    gtop = tops.at[0]
    set_scale(pat, H, s0, s1, scale_s)
    gtop[...] = jnp.zeros_like(gtop)
    gbot[...] = jnp.zeros_like(gbot)

    def step(m0):
        fixed_half(wave_ref, table, half_ref, scale_s, x_s, m0)
        for j in range(PAIR):
            gradients(lax.axis_index("core"), 0, bt, top, half_ref, ptop, pbot, p_ref, keep, send, gtop, gbot, back_s, m0 + j)

    pairs(wave_ref.shape[0], step)


def first_block(pat, s0, s1, wave, table, back_rows, top, ptop, pbot, probe):
    nm = wave.shape[0]
    return local_call(
        first_block_body,
        "first_block",
        [LOCAL] * 10,
        [shape(nm, N, N, dtype=bf16)] + [shape(nm, 16, 16, N)] * 2 + GRADS,
        SCALE + [pltpu.VMEM((N, N), f32)],
        9,
    )(pat, s0, s1, wave, table, back_rows, top, ptop, pbot, probe)


def second_block(back_rows, top, bot, ptop, pbot, probe, first, count, tops, earlier=None):
    nm = top.shape[0]
    given = earlier or []

    def body(bt, top, bot, ptop, pbot, p_ref, *refs):
        keep, send, gbot, tops, back_s = refs[1 + len(given) :]
        gtop = tops.at[1]
        if not given:
            gtop[...] = jnp.zeros_like(gtop)
            gbot[...] = jnp.zeros_like(gbot)
        core = lax.axis_index("core")
        loop(
            count,
            lambda m: gradients(
                core, 1, bt, top, bot, ptop, pbot, p_ref, keep, send, gtop, gbot, back_s, m + first
            ),
        )

    return local_call(
        body,
        "second_block",
        [LOCAL] * (7 + len(given)),
        [shape(nm, 16, 16, N)] * 2 + GRADS,
        [pltpu.VMEM((N, N), f32)],
        6,
        {6: 3, **{7 + i: i for i in range(len(given))}},
    )(back_rows, top, bot, ptop, pbot, probe, tops, *given)


SCAN = ("y", "z", "x", "core")
RING = ("y", "z", "core")


def along(value, steps):
    count = lax.axis_size(SCAN)
    lo, hi = max(0, -steps), min(count, count - steps)
    return lax.ppermute(value, SCAN, [(i, i + steps) for i in range(lo, hi)])


def swapped(value, axis):
    return lax.ppermute(value, axis, [(0, 1), (1, 0)])


def turned(value, steps, first):
    flat = lambda y, z, core: (y * 4 + z) * 2 + core
    pairs = []
    for y in range(4):
        for z in range(4):
            for core in range(2):
                on_y = (core == 0) == first
                to = ((y + steps) % 4, z) if on_y else (y, (z + steps) % 4)
                pairs.append((flat(y, z, core), flat(*to, core)))
    return lax.ppermute(value, RING, pairs)


def across(value, flip_mode, flip_x):
    pairs = [(2 * m + x, 2 * (m ^ flip_mode) + (x ^ flip_x)) for m in range(2) for x in range(2)]
    return lax.ppermute(value, ("mode", "x"), pairs)


def rim_body(place, obj, out):
    columns = window(place)

    def take(i):
        rows = at(i, CHUNK)
        out[:, rows, :] = obj[:, rows, columns]

    loop(H // CHUNK, take, 2)


def rim_rows(place, obj):
    return local_call(rim_body, "rim_rows", [SCALARS, LOCAL], [shape(2, H, N)], [], LIMIT)(place, obj)[0]


def brightest_body(own, far, out):
    def one(i, acc):
        return jnp.maximum(acc, own[at(i, 8), :] + far[at(i, 8), :])

    out[...] = lax.fori_loop(0, QUARTER // 8, one, jnp.zeros((8, N), f32))


def brightest(own, far):
    outs = [shape(8, N)]
    return local_call(brightest_body, "brightest", [LOCAL, LOCAL], outs, [], LIMIT, cost=STAGE)(own, far)[0]


def core_add_body(keep, recv, own, near, back, far0, far1):
    me = here()[0]
    n2 = own.shape[1]
    for m in range(2 * n2):
        j, k = m // n2, m % n2
        for out, turn in ((own, 0), (near, 1), (back, 3)):
            a = at(lax.rem(me + turn, 4), 4)
            out[j, k] = keep[m, a] + recv[m, a]
        a = at(lax.rem(me + 2, 4), 4)
        (far0, far1)[j][k] = keep[m, a] + recv[m, a]


def core_add(keep, recv):
    n2 = keep.shape[0] // 2
    outs = [shape(2, n2, 4, 16, N)] * 3 + [shape(n2, 4, 16, N)] * 2
    return local_call(core_add_body, "core_add", [LOCAL, LOCAL], outs, [], LIMIT, cost=STAGE)(keep, recv)


def relay_body(a, b, ra, rb, oa, ob):
    oa[0] = a[0] + ra[...]
    ob[1] = b[1] + rb[...]


def relay_add(near, back, ra, rb):
    outs = [shape(*near.shape)] * 2
    return local_call(relay_body, "relay_add", [LOCAL] * 4, outs, [], LIMIT, {0: 0, 1: 1}, cost=STAGE)(near, back, ra, rb)


def plane_add_body(*refs):
    me = here()[1]
    for block in range(2):
        own, ra, rb = refs[3 * block : 3 * block + 3]
        for turn in range(4):
            b = lax.rem(me + turn, 4)
            refs[6 + turn][block] = own[:, :, b] + (ra[:, :, b] + rb[:, :, b])


def plane_add(blocks):
    n2 = blocks[0][0].shape[1]
    outs = [shape(2, 2, n2, 16, N)] * 4
    return local_call(plane_add_body, "plane_add", [LOCAL] * 6, outs, [], LIMIT, cost=STAGE)(
        *blocks[0], *blocks[1]
    )


def line_add_body(most, a, b, c, d, keep, send):
    core = here()[2]
    n2 = a.shape[2]
    for side, out in ((core, keep), (1 - core, send)):
        rows = at(side, 8)
        for block in range(2):
            for j in range(2):
                first = (block * 2 + j) * n2
                out[first : first + n2] = (a[block, j, :, rows] + b[block, j, :, rows]) + (
                    c[block, j, :, rows] + d[block, j, :, rows]
                )
    send[4 * n2] = most[...]


def line_add(most, arrays):
    n2 = arrays[0].shape[2]
    outs = [shape(4 * n2, 8, N), shape(4 * n2 + 1, 8, N)]
    return local_call(line_add_body, "line_add", [LOCAL] * 5, outs, [], LIMIT, cost=STAGE)(most, *arrays)


def pixel_body(most, keep, recv, rows, mine, other):
    core, x = here()[2:4]
    scale = 1.0 / math.sqrt(64)
    nm = rows.shape[1]

    def fill(part, ref):
        mine[part] = ref[pl.ds(x * nm, nm)] * scale + rows[part]
        other[pl.ds(part * nm, nm)] = ref[pl.ds((1 - x) * nm, nm)] * scale

    @pl.when(core == 0)
    def _():
        fill(0, keep)
        fill(1, recv)

    @pl.when(core != 0)
    def _():
        fill(0, recv)
        fill(1, keep)

    other[2 * nm] = jnp.maximum(most[...], recv[2 * nm])


def pixel_step(most, keep, recv, rows):
    nm = rows.shape[1]
    outs = [shape(2, nm, 8, N), shape(2 * nm + 1, 8, N)]
    return local_call(pixel_body, "pixel_step", [LOCAL] * 4, outs, [], LIMIT, cost=STAGE)(most, keep, recv, rows)


def mix_body(w_ref, mine, b, c, d, out_ref):
    mode = here()[4]
    nm = mine.shape[1]
    for part in range(2):
        own = [mine[part, j] + b[part * nm + j] for j in range(nm)]
        far = [c[part, j] + d[part * nm + j] for j in range(nm)]
        for k in range(nm):
            row = mode * nm + k
            acc = jnp.zeros((8, N), f32)
            for j in range(nm):
                acc += (w_ref[row, mode * nm + j].astype(f32) / 16.0) * own[j]
                acc += (w_ref[row, (1 - mode) * nm + j].astype(f32) / 16.0) * far[j]
            out_ref[part, k] = acc.astype(bf16)


def mix(mixing, mine, b, c, d):
    outs = [shape(*mine.shape, dtype=bf16)]
    return local_call(mix_body, "mix", [SCALARS] + [LOCAL] * 4, outs, [], LIMIT)(mixing, mine, b, c, d)[0]


def object_body(place, before, near_max, far_max, obj, t, tf, b0, b0f, b1, b1f, over, out, new, sems):
    shift, col = place[0], pl.multiple_of(place[1] * H, H)
    over_shift, over_col = before[0], pl.multiple_of(before[1] * H, H)
    last = near_max.shape[0] - 1
    largest = jnp.max(jnp.maximum(near_max[last], far_max[last]))
    copies = []
    for half in range(2):
        base = half * H

        def start(i):
            rows = at(i, CHUNK, base)
            new[:, rows, :] = obj[:, rows, :]

        loop(H // CHUNK, start, 2)

        def add(column, even, odd):
            def one(g):
                for block, values in ((0, even), (1, odd)):
                    rows = pl.ds(pl.multiple_of(g * 32 + base + block * 16, 16), 16)
                    total = values[0][:, g]
                    for v in values[1:]:
                        total = total + v[:, g]
                    new[:, rows, pl.ds(column, N)] += total / largest

            loop(8, one, 2)

        @pl.when(shift == half)
        def _():
            add(col, (t.at[0], tf.at[0]), (t.at[1], tf.at[1]))

        if half == 1:

            @pl.when(shift == 0)
            def _():
                add(col, (b0, b0f), (b1, b1f))

        else:

            @pl.when(over_shift == 1)
            def _():
                add(over_col, (over.at[0],), (over.at[1],))

        copy = pltpu.make_async_copy(new.at[:, pl.ds(base, H), :], out.at[:, pl.ds(base, H), :], sems.at[half])
        copy.start()
        copies.append(copy)
    for copy in copies:
        copy.wait()


def object_update(place, before, near_max, far_max, obj, pieces, over):
    return pl.pallas_call(
        object_body,
        in_specs=[SCALARS] * 2 + [LOCAL] * 10,
        out_specs=FAR,
        out_shape=shape(2, N, 4 * H),
        scratch_shapes=[pltpu.VMEM((2, N, 4 * H), f32), pltpu.SemaphoreType.DMA((2,))],
        compiler_params=params(10),
        name="object_update",
    )(place, before, near_max, far_max, obj, *pieces, over)


def over_body(b0, b0f, b1, b1f, out):
    out[0] = b0[...] + b0f[...]
    out[1] = b1[...] + b1f[...]


def over_sum(b0, b0f, b1, b1f):
    return local_call(over_body, "over_sum", [LOCAL] * 4, [shape(2, 2, 8, 16, N)], [], LIMIT, cost=STAGE)(b0, b0f, b1, b1f)[0]


def tied(*values):
    return lax.optimization_barrier(values)


def per_device(object_field, probe, patterns, row_shift, col_start, mixing):
    minus, plus, wave_top_rows, wave_bot_rows, back_rows0, back_rows1 = tables()
    place = jnp.concatenate([row_shift, col_start])
    before = along(place, 1)
    patch_top, own_bot, first_rows = own_rows(place, object_field)
    before, patch_top = tied(before, patch_top)
    rim = along(rim_rows(before, first_rows), -1)
    half_top, own_light, light_out, rows = top_half(patch_top, probe, minus)
    wave_top, wave_bot = first_terms(wave_top_rows, wave_bot_rows, half_top)
    rim, wave_top, light_out = tied(rim, wave_top, light_out)
    far_light = swapped(light_out, "mode")
    half_bot, patch_bot, wave_top, sum_top = bottom_half(
        place, own_bot, rim, probe, minus, wave_top_rows, wave_top
    )
    far_top = swapped(sum_top, "mode")
    half_bot, far_light = tied(half_bot, far_light)
    wave_bot, sum_bot = low_wave(wave_bot_rows, half_bot, wave_bot)
    far_bot = swapped(sum_bot, "mode")
    fixed = fixed_top(patterns, sum_top, far_top, wave_top, plus)
    low, keep0, send0, bot0, tops = first_block(
        patterns, sum_bot, far_bot, wave_bot, plus, back_rows0, fixed, patch_top, patch_bot, probe
    )
    most = brightest(own_light, far_light)
    recv0 = swapped(send0, "core")
    bot0_far = swapped(bot0, "mode")
    *part1, tops = second_block(back_rows1, fixed, low, patch_top, patch_bot, probe, 0, 3, tops)
    own0, near0, back0, far0a, far0b = core_add(keep0, recv0)
    ra0, rb0 = turned(far0a, 1, True), turned(far0b, -1, True)
    *part1, near0 = tied(*part1, near0)
    keep1, send1, bot1, tops = second_block(
        back_rows1, fixed, low, patch_top, patch_bot, probe, 3, 3, tops, part1
    )
    recv1 = swapped(send1, "core")
    near0, back0 = relay_add(near0, back0, ra0, rb0)
    keep1, _ = tied(keep1, near0)
    own1, near1, back1, far1a, far1b = core_add(keep1, recv1)
    ra1, rb1 = turned(far1a, 1, True), turned(far1b, -1, True)
    plane0 = (own0, turned(near0, 1, True), turned(back0, -1, True))
    ra1, rb1, bot0_far, *plane0 = tied(ra1, rb1, bot0_far, *plane0)
    bot1_next, _ = tied(bot1, bot0_far)
    bot1_far = swapped(bot1_next, "mode")
    near1, back1 = relay_add(near1, back1, ra1, rb1)
    plane1 = (own1, turned(near1, 1, True), turned(back1, -1, True))
    *plane1, bot1_far = tied(*plane1, bot1_far)
    tops_next, _ = tied(tops, bot1_far)
    tops_far = swapped(tops_next, "mode")
    over = along(over_sum(bot0, bot0_far, bot1, bot1_far), 1)
    line = plane_add((plane0, plane1))
    line = [line[0]] + [turned(line[r], r, False) for r in (1, 3, 2)]
    keep, send = line_add(most, line)
    recv, over, tops_far = tied(swapped(send, "core"), over, tops_far)
    mine, other = pixel_step(most, keep, recv, rows)
    beside = across(other, 0, 1)
    probe_new = mix(mixing, mine, beside, across(mine, 1, 0), across(other, 1, 1))
    pieces = (tops, tops_far, bot0, bot0_far, bot1, bot1_far)
    object_new = object_update(place, before, other, beside, object_field, pieces, over)
    return object_new, probe_new


def solution(mesh):
    split = Mesh(mesh.devices.reshape(2, 4, 4, 2, 2), ("mode", *SCAN))
    return jax.shard_map(
        per_device,
        mesh=split,
        in_specs=(P(None, SCAN, None), P(None, "mode", None, None), P(SCAN, None, None), P(SCAN), P(SCAN), P()),
        out_specs=(P(None, SCAN, None), P(None, "mode", SCAN, None)),
        check_vma=False,
    )
```

```python
import functools
import math

import jax
import jax.numpy as jnp
import ml_dtypes
import numpy as np
from jax import lax
from jax.experimental import pallas as pl
from jax.experimental.pallas import tpu as pltpu
from jax.sharding import Mesh
from jax.sharding import PartitionSpec as P

f32, bf16 = jnp.float32, jnp.bfloat16
N = 512
H = 256
CHUNK = 32
QUARTER = 128
PAIR = 2


def tables():
    i = np.arange(N, dtype=np.int32)
    angle = (i[:, None] * i[None, :] % N).astype(np.float32) * np.float32(2.0 * math.pi / N)
    factor = np.float32(1.0 / math.sqrt(N))
    c = (np.cos(angle) * factor).astype(ml_dtypes.bfloat16)
    s = (np.sin(angle) * factor).astype(ml_dtypes.bfloat16)
    minus = np.block([[c, -s], [s, c]])
    plus = np.block([[c, s], [-s, c]])

    def stacked(table):
        return table.reshape(2 * N, 2, 2, H).swapaxes(1, 2).reshape(2 * N, 2 * N)

    wave_rows = stacked(plus).reshape(2, 2, H, 2 * N).swapaxes(0, 1).reshape(2, N, 2 * N)
    back_rows = stacked(minus).reshape(2, 16, 2, 16, 2 * N).transpose(2, 0, 1, 3, 4).reshape(2, N, 2 * N)
    return minus, plus, wave_rows[0], wave_rows[1], back_rows[0], back_rows[1]


def shape(*dims, dtype=f32):
    return jax.ShapeDtypeStruct(dims, dtype)


def whole(*dims):
    return pl.BlockSpec(dims, lambda *_: (0,) * len(dims))


def params(mib):
    return pltpu.CompilerParams(vmem_limit_bytes=mib << 20)


SCALARS = pl.BlockSpec(memory_space=pltpu.SMEM)
LOCAL = pl.BlockSpec(memory_space=pltpu.VMEM)
FAR = pl.BlockSpec(memory_space=pltpu.HBM)


def local_call(body, name, ins, outs, scratch, mib, alias=None, cost=None):
    def call(*args):
        return pl.pallas_call(
            body,
            in_specs=ins,
            out_specs=[LOCAL] * len(outs),
            out_shape=outs,
            scratch_shapes=scratch,
            compiler_params=params(mib),
            input_output_aliases=alias or {},
            name=name,
            cost_estimate=cost,
        )(*args)

    return call


def loop(count, fn, unroll=1):
    def body(i, carry):
        fn(i)
        return carry

    lax.fori_loop(0, count, body, 0, unroll=unroll)


def at(i, size, base=0):
    return pl.ds(pl.multiple_of(i * size + base, min(size, base) if base else size), size)


def here():
    y, z, x, core, mode = (lax.axis_index(a) for a in ("y", "z", "x", "core", "mode"))
    return jnp.where(core == 0, y, z), jnp.where(core == 0, z, y), core, x, mode


def exit_rows(p_ref, m, rows, o_r, o_i):
    pr = p_ref[0, m, rows, :].astype(f32)
    pi = p_ref[1, m, rows, :].astype(f32)
    return pr, pi, (pr * o_r - pi * o_i).astype(bf16), (pr * o_i + pi * o_r).astype(bf16)


def exit_half(p_ref, m, j, base, patch, x_s):
    def one(i):
        rows = at(i, CHUNK)
        _, _, xr, xi = exit_rows(p_ref, m, at(i, CHUNK, base), patch[0, rows, :], patch[1, rows, :])
        x_s[j, rows, :N] = xr
        x_s[j, rows, N:] = xi

    loop(H // CHUNK, one, 2)


def along_rows(x_s, table, out, m0):
    x = x_s[...].reshape(PAIR * H, 2 * N)
    half = jnp.dot(x, table[...], preferred_element_type=f32).astype(bf16)
    for j in range(PAIR):
        out[m0 + j, :H] = half[j * H : (j + 1) * H, :N]
        out[m0 + j, H:] = half[j * H : (j + 1) * H, N:]


def pairs(p_ref, fn):
    nm = p_ref
    loop(nm // PAIR, lambda k: fn(k * PAIR))


def window(place):
    return pl.ds(pl.multiple_of(place[1] * H, H), N)


def own_body(place, obj, top_ref, bot_ref, first_ref):
    columns = window(place)
    top = place[0] * H

    def take(i):
        rows = at(i, CHUNK)
        top_ref[:, rows, :] = obj[:, pl.ds(pl.multiple_of(top + i * CHUNK, CHUNK), CHUNK), columns]
        bot_ref[:, rows, :] = obj[:, at(i, CHUNK, H), columns]
        first_ref[:, rows, :] = obj[:, rows, :]

    loop(H // CHUNK, take, 2)


def own_rows(place, obj):
    return local_call(own_body, "own_rows", [SCALARS, LOCAL], [shape(2, H, N)] * 2 + [shape(2, H, 2 * N)], [], LIMIT)(
        place, obj
    )


def top_body(patch_ref, p_ref, table, half_ref, own_part, far_part, rows_ref, x_s):
    def step(m0):
        for j in range(PAIR):
            exit_half(p_ref, m0 + j, j, 0, patch_ref, x_s)
        along_rows(x_s, table, half_ref, m0)

    pairs(p_ref.shape[1], step)
    core, x = lax.axis_index("core"), lax.axis_index("x")
    base = (core * 2 + x) * QUARTER

    def lit(i):
        rows = pl.ds(pl.multiple_of(base + i * CHUNK, CHUNK), CHUNK)
        acc = jnp.zeros((CHUNK, N), f32)
        for m in range(p_ref.shape[1]):
            pr = p_ref[0, m, rows, :].astype(f32)
            pi = p_ref[1, m, rows, :].astype(f32)
            acc = acc + (pr * pr + pi * pi)
        own_part[at(i, CHUNK), :] = acc
        far_part[at(i, CHUNK), :] = acc

    loop(QUARTER // CHUNK, lit)
    chip = (lax.axis_index("y") * 4 + lax.axis_index("z")) * 2 + lax.axis_index("x")
    for part in range(2):
        for m in range(p_ref.shape[1]):
            both = p_ref[part, m, at(chip, 16), :].astype(f32)
            rows_ref[part, m] = jnp.where(core == 0, both[:8], both[8:])


def top_half(patch, probe, table):
    nm = probe.shape[1]
    return local_call(
        top_body,
        "top_half",
        [LOCAL, LOCAL, LOCAL],
        [shape(nm, N, N, dtype=bf16), shape(QUARTER, N), shape(QUARTER, N), shape(2, nm, 8, N)],
        [pltpu.VMEM((PAIR, H, 2 * N), bf16)],
        6,
    )(patch, probe, table)


def first_terms_body(wt0, wt1, top, wave0, wave1):
    def step(m):
        wave0[m] = jnp.dot(wt0[:, :N], top[m], preferred_element_type=f32)
        wave1[m] = jnp.dot(wt1[:, :N], top[m], preferred_element_type=f32)

    loop(top.shape[0], step)


def first_terms(wt0, wt1, top):
    nm = top.shape[0]
    return local_call(first_terms_body, "first_terms", [LOCAL] * 3, [shape(nm, N, N)] * 2, [], 5)(wt0, wt1, top)


def wave_half(wave_ref, sum_ref, wt, bot, m0):
    for j in range(PAIR):
        m = m0 + j
        wave_ref[m] += jnp.dot(wt[:, N:], bot[m], preferred_element_type=f32)

    def one(i):
        rows = at(i, CHUNK)
        low = at(i, CHUNK, H)
        acc = sum_ref[rows, :]
        for j in range(PAIR):
            a = wave_ref[m0 + j, rows, :]
            b = wave_ref[m0 + j, low, :]
            acc = acc + (a * a + b * b)
        sum_ref[rows, :] = acc

    loop(H // CHUNK, one, 2)


def bottom_body(place, own, rim, p_ref, table, wt, _, half_ref, patch_ref, wave_ref, sum_ref, x_s):
    @pl.when(place[0] == 0)
    def _():
        patch_ref[...] = own[...]

    @pl.when(place[0] != 0)
    def _():
        patch_ref[...] = rim[...]

    sum_ref[...] = jnp.zeros_like(sum_ref)

    def step(m0):
        for j in range(PAIR):
            exit_half(p_ref, m0 + j, j, H, patch_ref, x_s)
        along_rows(x_s, table, half_ref, m0)
        wave_half(wave_ref, sum_ref, wt, half_ref, m0)

    pairs(p_ref.shape[1], step)


def bottom_half(place, own, rim, probe, table, wave_rows, wave):
    nm = probe.shape[1]
    return local_call(
        bottom_body,
        "bottom_half",
        [SCALARS] + [LOCAL] * 6,
        [shape(nm, N, N, dtype=bf16), shape(2, H, N), shape(nm, N, N), shape(H, N)],
        [pltpu.VMEM((PAIR, H, 2 * N), bf16)],
        8,
        {6: 2},
    )(place, own, rim, probe, table, wave_rows, wave)


def low_wave_body(wt, bot, _, wave_ref, sum_ref):
    sum_ref[...] = jnp.zeros_like(sum_ref)
    pairs(bot.shape[0], lambda m0: wave_half(wave_ref, sum_ref, wt, bot, m0))


def low_wave(wave_rows, bot, wave):
    outs = [shape(*wave.shape), shape(H, N)]
    return local_call(low_wave_body, "low_wave", [LOCAL] * 3, outs, [], 5, {2: 0})(wave_rows, bot, wave)


def set_scale(pat, base, s0, s1, scale_s):
    def one(i):
        rows = at(i, CHUNK)
        total = jnp.maximum(s0[rows, :] + s1[rows, :], 1.0)
        scale_s[rows, :] = jnp.sqrt(pat[0, at(i, CHUNK, base), :]) / jnp.sqrt(total)

    loop(H // CHUNK, one)


def fixed_half(wave_ref, table, half_ref, scale_s, x_s, m0):
    for j in range(PAIR):

        def one(i):
            rows = at(i, CHUNK)
            low = at(i, CHUNK, H)
            factor = scale_s[rows, :]
            x_s[j, rows, :N] = (wave_ref[m0 + j, rows, :] * factor).astype(bf16)
            x_s[j, rows, N:] = (wave_ref[m0 + j, low, :] * factor).astype(bf16)

        loop(H // CHUNK, one, 2)
    along_rows(x_s, table, half_ref, m0)


def fixed_top_body(pat, s0, s1, wave_ref, table, half_ref, scale_s, x_s):
    set_scale(pat, 0, s0, s1, scale_s)
    pairs(wave_ref.shape[0], lambda m0: fixed_half(wave_ref, table, half_ref, scale_s, x_s, m0))


SCALE = [pltpu.VMEM((H, N), f32), pltpu.VMEM((PAIR, H, 2 * N), bf16)]


def fixed_top(pat, s0, s1, wave, table):
    nm = wave.shape[0]
    return local_call(
        fixed_top_body, "fixed_top", [LOCAL] * 5, [shape(nm, N, N, dtype=bf16)], SCALE, 6
    )(pat, s0, s1, wave, table)[0]


def gradients(core, block, bt, top, bot, patch_top, patch_bot, p_ref, keep_ref, send_ref, gtop, gbot, back_s, m):
    back_s[...] = jnp.dot(bt[:, :N], top[m], preferred_element_type=f32) + jnp.dot(
        bt[:, N:], bot[m], preferred_element_type=f32
    )
    for patch, g_ref, base in ((patch_top, gtop, 0), (patch_bot, gbot, 8)):

        def one(i):
            g = i + base
            rows = pl.ds(pl.multiple_of(i * 32 + block * 16, 16), 16)
            full = pl.ds(pl.multiple_of(g * 32 + block * 16, 16), 16)
            o_r = patch[0, rows, :]
            o_i = patch[1, rows, :]
            pr, pi, xr, xi = exit_rows(p_ref, m, full, o_r, o_i)
            rr = back_s[at(g, 16), :] - xr.astype(f32)
            ri = back_s[pl.ds(pl.multiple_of(g * 16 + H, 16), 16), :] - xi.astype(f32)
            g_ref[0, i] += pr * rr + pi * ri
            g_ref[1, i] += pr * ri - pi * rr
            st0 = o_r * rr + o_i * ri
            st1 = o_r * ri - o_i * rr
            turned_g = (g % 4) * 4 + g // 4
            keep_ref[m, jnp.where(core == 0, g, turned_g)] = jnp.where(core == 0, st0, st1)
            send_ref[m, jnp.where(core == 0, turned_g, g)] = jnp.where(core == 0, st1, st0)

        loop(8, one, UNROLL)


UNROLL = 8
LIMIT = 4
STAGE = pl.CostEstimate(flops=int(5e9), transcendentals=0, bytes_accessed=int(15e6))
GRADS = [shape(2, 2, 8, 16, N)] * 2


def first_block_body(pat, s0, s1, wave_ref, table, bt, top, ptop, pbot, p_ref, half_ref, keep, send, bots, tops, scale_s, x_s, back_s):
    gtop, gbot = tops.at[0], bots.at[0]
    set_scale(pat, H, s0, s1, scale_s)
    gtop[...] = jnp.zeros_like(gtop)
    gbot[...] = jnp.zeros_like(gbot)

    def step(m0):
        fixed_half(wave_ref, table, half_ref, scale_s, x_s, m0)
        for j in range(PAIR):
            gradients(lax.axis_index("core"), 0, bt, top, half_ref, ptop, pbot, p_ref, keep, send, gtop, gbot, back_s, m0 + j)

    pairs(wave_ref.shape[0], step)


def first_block(pat, s0, s1, wave, table, back_rows, top, ptop, pbot, probe):
    nm = wave.shape[0]
    return local_call(
        first_block_body,
        "first_block",
        [LOCAL] * 10,
        [shape(nm, N, N, dtype=bf16)] + [shape(nm, 16, 16, N)] * 2 + GRADS,
        SCALE + [pltpu.VMEM((N, N), f32)],
        9,
    )(pat, s0, s1, wave, table, back_rows, top, ptop, pbot, probe)


def second_block(back_rows, top, bot, ptop, pbot, probe, first, count, bots, tops, earlier=None):
    nm = top.shape[0]
    given = earlier or []

    def body(bt, top, bot, ptop, pbot, p_ref, *refs):
        keep, send, bots, tops, back_s = refs[2 + len(given) :]
        gtop, gbot = tops.at[1], bots.at[1]
        if not given:
            gtop[...] = jnp.zeros_like(gtop)
            gbot[...] = jnp.zeros_like(gbot)
        core = lax.axis_index("core")
        loop(
            count,
            lambda m: gradients(
                core, 1, bt, top, bot, ptop, pbot, p_ref, keep, send, gtop, gbot, back_s, m + first
            ),
        )

    return local_call(
        body,
        "second_block",
        [LOCAL] * (8 + len(given)),
        [shape(nm, 16, 16, N)] * 2 + GRADS,
        [pltpu.VMEM((N, N), f32)],
        6,
        {6: 2, 7: 3, **{8 + i: i for i in range(len(given))}},
    )(back_rows, top, bot, ptop, pbot, probe, bots, tops, *given)


SCAN = ("y", "z", "x", "core")
RING = ("y", "z", "core")


def along(value, steps):
    count = lax.axis_size(SCAN)
    lo, hi = max(0, -steps), min(count, count - steps)
    return lax.ppermute(value, SCAN, [(i, i + steps) for i in range(lo, hi)])


def swapped(value, axis):
    return lax.ppermute(value, axis, [(0, 1), (1, 0)])


def turned(value, steps, first):
    flat = lambda y, z, core: (y * 4 + z) * 2 + core
    pairs = []
    for y in range(4):
        for z in range(4):
            for core in range(2):
                on_y = (core == 0) == first
                to = ((y + steps) % 4, z) if on_y else (y, (z + steps) % 4)
                pairs.append((flat(y, z, core), flat(*to, core)))
    return lax.ppermute(value, RING, pairs)


def across(value, flip_mode, flip_x):
    pairs = [(2 * m + x, 2 * (m ^ flip_mode) + (x ^ flip_x)) for m in range(2) for x in range(2)]
    return lax.ppermute(value, ("mode", "x"), pairs)


def rim_body(place, obj, out):
    columns = window(place)

    def take(i):
        rows = at(i, CHUNK)
        out[:, rows, :] = obj[:, rows, columns]

    loop(H // CHUNK, take, 2)


def rim_rows(place, obj):
    return local_call(rim_body, "rim_rows", [SCALARS, LOCAL], [shape(2, H, N)], [], LIMIT)(place, obj)[0]


def brightest_body(own, far, out):
    def one(i, acc):
        return jnp.maximum(acc, own[at(i, 8), :] + far[at(i, 8), :])

    out[...] = lax.fori_loop(0, QUARTER // 8, one, jnp.zeros((8, N), f32))


def brightest(own, far):
    outs = [shape(8, N)]
    return local_call(brightest_body, "brightest", [LOCAL, LOCAL], outs, [], LIMIT, cost=STAGE)(own, far)[0]


def core_add_body(keep, recv, own, near, back, far0, far1):
    me = here()[0]
    n2 = own.shape[1]
    for m in range(2 * n2):
        j, k = m // n2, m % n2
        for out, turn in ((own, 0), (near, 1), (back, 3)):
            a = at(lax.rem(me + turn, 4), 4)
            out[j, k] = keep[m, a] + recv[m, a]
        a = at(lax.rem(me + 2, 4), 4)
        (far0, far1)[j][k] = keep[m, a] + recv[m, a]


def core_add(keep, recv):
    n2 = keep.shape[0] // 2
    outs = [shape(2, n2, 4, 16, N)] * 3 + [shape(n2, 4, 16, N)] * 2
    return local_call(core_add_body, "core_add", [LOCAL, LOCAL], outs, [], LIMIT, cost=STAGE)(keep, recv)


def relay_body(a, b, ra, rb, oa, ob):
    oa[0] = a[0] + ra[...]
    ob[1] = b[1] + rb[...]


def relay_add(near, back, ra, rb):
    outs = [shape(*near.shape)] * 2
    return local_call(relay_body, "relay_add", [LOCAL] * 4, outs, [], LIMIT, {0: 0, 1: 1}, cost=STAGE)(near, back, ra, rb)


def plane_add_body(*refs):
    me = here()[1]
    for block in range(2):
        own, ra, rb = refs[3 * block : 3 * block + 3]
        for turn in range(4):
            b = lax.rem(me + turn, 4)
            refs[6 + turn][block] = own[:, :, b] + (ra[:, :, b] + rb[:, :, b])


def plane_add(blocks):
    n2 = blocks[0][0].shape[1]
    outs = [shape(2, 2, n2, 16, N)] * 4
    return local_call(plane_add_body, "plane_add", [LOCAL] * 6, outs, [], LIMIT, cost=STAGE)(
        *blocks[0], *blocks[1]
    )


def line_add_body(most, a, b, c, d, keep, send):
    core = here()[2]
    n2 = a.shape[2]
    for side, out in ((core, keep), (1 - core, send)):
        rows = at(side, 8)
        for block in range(2):
            for j in range(2):
                first = (block * 2 + j) * n2
                out[first : first + n2] = (a[block, j, :, rows] + b[block, j, :, rows]) + (
                    c[block, j, :, rows] + d[block, j, :, rows]
                )
    send[4 * n2] = most[...]


def line_add(most, arrays):
    n2 = arrays[0].shape[2]
    outs = [shape(4 * n2, 8, N), shape(4 * n2 + 1, 8, N)]
    return local_call(line_add_body, "line_add", [LOCAL] * 5, outs, [], LIMIT, cost=STAGE)(most, *arrays)


def pixel_body(most, keep, recv, rows, mine, other):
    core, x = here()[2:4]
    scale = 1.0 / math.sqrt(64)
    nm = rows.shape[1]

    def fill(part, ref):
        mine[part] = ref[pl.ds(x * nm, nm)] * scale + rows[part]
        other[pl.ds(part * nm, nm)] = ref[pl.ds((1 - x) * nm, nm)] * scale

    @pl.when(core == 0)
    def _():
        fill(0, keep)
        fill(1, recv)

    @pl.when(core != 0)
    def _():
        fill(0, recv)
        fill(1, keep)

    other[2 * nm] = jnp.maximum(most[...], recv[2 * nm])


def pixel_step(most, keep, recv, rows):
    nm = rows.shape[1]
    outs = [shape(2, nm, 8, N), shape(2 * nm + 1, 8, N)]
    return local_call(pixel_body, "pixel_step", [LOCAL] * 4, outs, [], LIMIT, cost=STAGE)(most, keep, recv, rows)


def mix_body(w_ref, mine, b, c, d, out_ref):
    mode = here()[4]
    nm = mine.shape[1]
    for part in range(2):
        own = [mine[part, j] + b[part * nm + j] for j in range(nm)]
        far = [c[part, j] + d[part * nm + j] for j in range(nm)]
        for k in range(nm):
            row = mode * nm + k
            acc = jnp.zeros((8, N), f32)
            for j in range(nm):
                acc += (w_ref[row, mode * nm + j].astype(f32) / 16.0) * own[j]
                acc += (w_ref[row, (1 - mode) * nm + j].astype(f32) / 16.0) * far[j]
            out_ref[part, k] = acc.astype(bf16)


def mix(mixing, mine, b, c, d):
    outs = [shape(*mine.shape, dtype=bf16)]
    return local_call(mix_body, "mix", [SCALARS] + [LOCAL] * 4, outs, [], LIMIT)(mixing, mine, b, c, d)[0]


def object_body(place, before, near_max, far_max, obj, t, tf, b, bf, over, out, new, sems):
    shift, col = place[0], pl.multiple_of(place[1] * H, H)
    over_shift, over_col = before[0], pl.multiple_of(before[1] * H, H)
    last = near_max.shape[0] - 1
    largest = jnp.max(jnp.maximum(near_max[last], far_max[last]))
    copies = []
    for half in range(2):
        base = half * H

        def start(i):
            rows = at(i, CHUNK, base)
            new[:, rows, :] = obj[:, rows, :]

        loop(H // CHUNK, start, 2)

        def add(column, even, odd):
            def one(g):
                for block, values in ((0, even), (1, odd)):
                    rows = pl.ds(pl.multiple_of(g * 32 + base + block * 16, 16), 16)
                    total = values[0][:, g]
                    for v in values[1:]:
                        total = total + v[:, g]
                    new[:, rows, pl.ds(column, N)] += total / largest

            loop(8, one, 2)

        @pl.when(shift == half)
        def _():
            add(col, (t.at[0], tf.at[0]), (t.at[1], tf.at[1]))

        if half == 1:

            @pl.when(shift == 0)
            def _():
                add(col, (b.at[0], bf.at[0]), (b.at[1], bf.at[1]))

        else:

            @pl.when(over_shift == 1)
            def _():
                add(over_col, (over.at[0],), (over.at[1],))

        copy = pltpu.make_async_copy(new.at[:, pl.ds(base, H), :], out.at[:, pl.ds(base, H), :], sems.at[half])
        copy.start()
        copies.append(copy)
    for copy in copies:
        copy.wait()


def object_update(place, before, near_max, far_max, obj, pieces, over):
    return pl.pallas_call(
        object_body,
        in_specs=[SCALARS] * 2 + [LOCAL] * 8,
        out_specs=FAR,
        out_shape=shape(2, N, 4 * H),
        scratch_shapes=[pltpu.VMEM((2, N, 4 * H), f32), pltpu.SemaphoreType.DMA((2,))],
        compiler_params=params(10),
        name="object_update",
    )(place, before, near_max, far_max, obj, *pieces, over)


def over_body(g, gf, out):
    out[...] = g[...] + gf[...]


def over_sum(grads, far):
    outs = [shape(2, 2, 8, 16, N)]
    return local_call(over_body, "over_sum", [LOCAL] * 2, outs, [], LIMIT, cost=STAGE)(grads, far)[0]


def tied(*values):
    return lax.optimization_barrier(values)


def per_device(object_field, probe, patterns, row_shift, col_start, mixing):
    minus, plus, wave_top_rows, wave_bot_rows, back_rows0, back_rows1 = tables()
    place = jnp.concatenate([row_shift, col_start])
    before = along(place, 1)
    patch_top, own_bot, first_rows = own_rows(place, object_field)
    before, patch_top = tied(before, patch_top)
    rim = along(rim_rows(before, first_rows), -1)
    half_top, own_light, light_out, rows = top_half(patch_top, probe, minus)
    wave_top, wave_bot = first_terms(wave_top_rows, wave_bot_rows, half_top)
    rim, wave_top, light_out = tied(rim, wave_top, light_out)
    far_light = swapped(light_out, "mode")
    half_bot, patch_bot, wave_top, sum_top = bottom_half(
        place, own_bot, rim, probe, minus, wave_top_rows, wave_top
    )
    far_top = swapped(sum_top, "mode")
    half_bot, far_light = tied(half_bot, far_light)
    wave_bot, sum_bot = low_wave(wave_bot_rows, half_bot, wave_bot)
    far_bot = swapped(sum_bot, "mode")
    fixed = fixed_top(patterns, sum_top, far_top, wave_top, plus)
    low, keep0, send0, bots, tops = first_block(
        patterns, sum_bot, far_bot, wave_bot, plus, back_rows0, fixed, patch_top, patch_bot, probe
    )
    most = brightest(own_light, far_light)
    recv0 = swapped(send0, "core")
    *part1, bots, tops = second_block(back_rows1, fixed, low, patch_top, patch_bot, probe, 0, 3, bots, tops)
    own0, near0, back0, far0a, far0b = core_add(keep0, recv0)
    ra0, rb0 = turned(far0a, 1, True), turned(far0b, -1, True)
    *part1, near0 = tied(*part1, near0)
    keep1, send1, bots, tops = second_block(
        back_rows1, fixed, low, patch_top, patch_bot, probe, 3, 3, bots, tops, part1
    )
    bots_far = swapped(bots, "mode")
    recv1 = swapped(send1, "core")
    near0, back0 = relay_add(near0, back0, ra0, rb0)
    keep1, _ = tied(keep1, near0)
    own1, near1, back1, far1a, far1b = core_add(keep1, recv1)
    ra1, rb1 = turned(far1a, 1, True), turned(far1b, -1, True)
    plane0 = (own0, turned(near0, 1, True), turned(back0, -1, True))
    ra1, rb1, bots_far, *plane0 = tied(ra1, rb1, bots_far, *plane0)
    near1, back1 = relay_add(near1, back1, ra1, rb1)
    plane1 = (own1, turned(near1, 1, True), turned(back1, -1, True))
    tops_far = swapped(tops, "mode")
    over = along(over_sum(bots, bots_far), 1)
    line = plane_add((plane0, plane1))
    line = [line[0]] + [turned(line[r], r, False) for r in (1, 3, 2)]
    keep, send = line_add(most, line)
    recv, over, tops_far = tied(swapped(send, "core"), over, tops_far)
    mine, other = pixel_step(most, keep, recv, rows)
    beside = across(other, 0, 1)
    probe_new = mix(mixing, mine, beside, across(mine, 1, 0), across(other, 1, 1))
    object_new = object_update(place, before, other, beside, object_field, (tops, tops_far, bots, bots_far), over)
    return object_new, probe_new


def solution(mesh):
    split = Mesh(mesh.devices.reshape(2, 4, 4, 2, 2), ("mode", *SCAN))
    return jax.shard_map(
        per_device,
        mesh=split,
        in_specs=(P(None, SCAN, None), P(None, "mode", None, None), P(SCAN, None, None), P(SCAN), P(SCAN), P()),
        out_specs=(P(None, SCAN, None), P(None, "mode", SCAN, None)),
        check_vma=False,
    )
```

```python
import functools
import math

import jax
import jax.numpy as jnp
import ml_dtypes
import numpy as np
from jax import lax
from jax.experimental import pallas as pl
from jax.experimental.pallas import tpu as pltpu
from jax.sharding import Mesh
from jax.sharding import PartitionSpec as P

f32, bf16 = jnp.float32, jnp.bfloat16
N = 512
H = 256
CHUNK = 32
QUARTER = 128
PAIR = 2


def tables():
    i = np.arange(N, dtype=np.int32)
    angle = (i[:, None] * i[None, :] % N).astype(np.float32) * np.float32(2.0 * math.pi / N)
    factor = np.float32(1.0 / math.sqrt(N))
    c = (np.cos(angle) * factor).astype(ml_dtypes.bfloat16)
    s = (np.sin(angle) * factor).astype(ml_dtypes.bfloat16)
    minus = np.block([[c, -s], [s, c]])
    plus = np.block([[c, s], [-s, c]])

    def stacked(table):
        return table.reshape(2 * N, 2, 2, H).swapaxes(1, 2).reshape(2 * N, 2 * N)

    wave_rows = stacked(plus).reshape(2, 2, H, 2 * N).swapaxes(0, 1).reshape(2, N, 2 * N)
    back_rows = stacked(minus).reshape(2, 16, 2, 16, 2 * N).transpose(2, 0, 1, 3, 4).reshape(2, N, 2 * N)
    return minus, plus, wave_rows[0], wave_rows[1], back_rows[0], back_rows[1]


def shape(*dims, dtype=f32):
    return jax.ShapeDtypeStruct(dims, dtype)


def whole(*dims):
    return pl.BlockSpec(dims, lambda *_: (0,) * len(dims))


def params(mib):
    return pltpu.CompilerParams(vmem_limit_bytes=mib << 20)


SCALARS = pl.BlockSpec(memory_space=pltpu.SMEM)
LOCAL = pl.BlockSpec(memory_space=pltpu.VMEM)
FAR = pl.BlockSpec(memory_space=pltpu.HBM)


def local_call(body, name, ins, outs, scratch, mib, alias=None, cost=None):
    def call(*args):
        return pl.pallas_call(
            body,
            in_specs=ins,
            out_specs=[LOCAL] * len(outs),
            out_shape=outs,
            scratch_shapes=scratch,
            compiler_params=params(mib),
            input_output_aliases=alias or {},
            name=name,
            cost_estimate=cost,
        )(*args)

    return call


def loop(count, fn, unroll=1):
    def body(i, carry):
        fn(i)
        return carry

    lax.fori_loop(0, count, body, 0, unroll=unroll)


def at(i, size, base=0):
    return pl.ds(pl.multiple_of(i * size + base, min(size, base) if base else size), size)


def here():
    y, z, x, core, mode = (lax.axis_index(a) for a in ("y", "z", "x", "core", "mode"))
    return jnp.where(core == 0, y, z), jnp.where(core == 0, z, y), core, x, mode


def exit_rows(p_ref, m, rows, o_r, o_i):
    pr = p_ref[0, m, rows, :].astype(f32)
    pi = p_ref[1, m, rows, :].astype(f32)
    return pr, pi, (pr * o_r - pi * o_i).astype(bf16), (pr * o_i + pi * o_r).astype(bf16)


def exit_half(p_ref, m, j, base, patch, x_s):
    def one(i):
        rows = at(i, CHUNK)
        _, _, xr, xi = exit_rows(p_ref, m, at(i, CHUNK, base), patch[0, rows, :], patch[1, rows, :])
        x_s[j, rows, :N] = xr
        x_s[j, rows, N:] = xi

    loop(H // CHUNK, one, 2)


def along_rows(x_s, table, out, m0):
    x = x_s[...].reshape(PAIR * H, 2 * N)
    half = jnp.dot(x, table[...], preferred_element_type=f32).astype(bf16)
    for j in range(PAIR):
        out[m0 + j, :H] = half[j * H : (j + 1) * H, :N]
        out[m0 + j, H:] = half[j * H : (j + 1) * H, N:]


def pairs(p_ref, fn):
    nm = p_ref
    loop(nm // PAIR, lambda k: fn(k * PAIR))


def window(place):
    return pl.ds(pl.multiple_of(place[1] * H, H), N)


def own_body(place, obj, top_ref, bot_ref, first_ref):
    columns = window(place)
    top = place[0] * H

    def take(i):
        rows = at(i, CHUNK)
        top_ref[:, rows, :] = obj[:, pl.ds(pl.multiple_of(top + i * CHUNK, CHUNK), CHUNK), columns]
        bot_ref[:, rows, :] = obj[:, at(i, CHUNK, H), columns]
        first_ref[:, rows, :] = obj[:, rows, :]

    loop(H // CHUNK, take, 2)


def own_rows(place, obj):
    return local_call(own_body, "own_rows", [SCALARS, LOCAL], [shape(2, H, N)] * 2 + [shape(2, H, 2 * N)], [], LIMIT)(
        place, obj
    )


def top_body(patch_ref, p_ref, table, half_ref, own_part, far_part, rows_ref, x_s):
    def step(m0):
        for j in range(PAIR):
            exit_half(p_ref, m0 + j, j, 0, patch_ref, x_s)
        along_rows(x_s, table, half_ref, m0)

    pairs(p_ref.shape[1], step)
    core, x = lax.axis_index("core"), lax.axis_index("x")
    base = (core * 2 + x) * QUARTER

    def lit(i):
        rows = pl.ds(pl.multiple_of(base + i * CHUNK, CHUNK), CHUNK)
        acc = jnp.zeros((CHUNK, N), f32)
        for m in range(p_ref.shape[1]):
            pr = p_ref[0, m, rows, :].astype(f32)
            pi = p_ref[1, m, rows, :].astype(f32)
            acc = acc + (pr * pr + pi * pi)
        own_part[at(i, CHUNK), :] = acc
        far_part[at(i, CHUNK), :] = acc

    loop(QUARTER // CHUNK, lit)
    chip = (lax.axis_index("y") * 4 + lax.axis_index("z")) * 2 + lax.axis_index("x")
    for part in range(2):
        for m in range(p_ref.shape[1]):
            both = p_ref[part, m, at(chip, 16), :].astype(f32)
            rows_ref[part, m] = jnp.where(core == 0, both[:8], both[8:])


def top_half(patch, probe, table):
    nm = probe.shape[1]
    return local_call(
        top_body,
        "top_half",
        [LOCAL, LOCAL, LOCAL],
        [shape(nm, N, N, dtype=bf16), shape(QUARTER, N), shape(QUARTER, N), shape(2, nm, 8, N)],
        [pltpu.VMEM((PAIR, H, 2 * N), bf16)],
        6,
    )(patch, probe, table)


def first_terms_body(wt0, wt1, top, wave0, wave1):
    def step(m):
        wave0[m] = jnp.dot(wt0[:, :N], top[m], preferred_element_type=f32)
        wave1[m] = jnp.dot(wt1[:, :N], top[m], preferred_element_type=f32)

    loop(top.shape[0], step)


def first_terms(wt0, wt1, top):
    nm = top.shape[0]
    return local_call(first_terms_body, "first_terms", [LOCAL] * 3, [shape(nm, N, N)] * 2, [], 5)(wt0, wt1, top)


def wave_half(wave_ref, sum_ref, wt, bot, m0):
    for j in range(PAIR):
        m = m0 + j
        wave_ref[m] += jnp.dot(wt[:, N:], bot[m], preferred_element_type=f32)

    def one(i):
        rows = at(i, CHUNK)
        low = at(i, CHUNK, H)
        acc = sum_ref[rows, :]
        for j in range(PAIR):
            a = wave_ref[m0 + j, rows, :]
            b = wave_ref[m0 + j, low, :]
            acc = acc + (a * a + b * b)
        sum_ref[rows, :] = acc

    loop(H // CHUNK, one, 2)


def bottom_body(place, own, rim, p_ref, table, wt, _, half_ref, patch_ref, wave_ref, sum_ref, x_s):
    @pl.when(place[0] == 0)
    def _():
        patch_ref[...] = own[...]

    @pl.when(place[0] != 0)
    def _():
        patch_ref[...] = rim[...]

    sum_ref[...] = jnp.zeros_like(sum_ref)

    def step(m0):
        for j in range(PAIR):
            exit_half(p_ref, m0 + j, j, H, patch_ref, x_s)
        along_rows(x_s, table, half_ref, m0)
        wave_half(wave_ref, sum_ref, wt, half_ref, m0)

    pairs(p_ref.shape[1], step)


def bottom_half(place, own, rim, probe, table, wave_rows, wave):
    nm = probe.shape[1]
    return local_call(
        bottom_body,
        "bottom_half",
        [SCALARS] + [LOCAL] * 6,
        [shape(nm, N, N, dtype=bf16), shape(2, H, N), shape(nm, N, N), shape(H, N)],
        [pltpu.VMEM((PAIR, H, 2 * N), bf16)],
        8,
        {6: 2},
    )(place, own, rim, probe, table, wave_rows, wave)


def low_wave_body(wt, bot, _, wave_ref, sum_ref):
    sum_ref[...] = jnp.zeros_like(sum_ref)
    pairs(bot.shape[0], lambda m0: wave_half(wave_ref, sum_ref, wt, bot, m0))


def low_wave(wave_rows, bot, wave):
    outs = [shape(*wave.shape), shape(H, N)]
    return local_call(low_wave_body, "low_wave", [LOCAL] * 3, outs, [], 5, {2: 0})(wave_rows, bot, wave)


def set_scale(pat, base, s0, s1, scale_s):
    def one(i):
        rows = at(i, CHUNK)
        total = jnp.maximum(s0[rows, :] + s1[rows, :], 1.0)
        scale_s[rows, :] = jnp.sqrt(pat[0, at(i, CHUNK, base), :]) / jnp.sqrt(total)

    loop(H // CHUNK, one)


def fixed_half(wave_ref, table, half_ref, scale_s, x_s, m0):
    for j in range(PAIR):

        def one(i):
            rows = at(i, CHUNK)
            low = at(i, CHUNK, H)
            factor = scale_s[rows, :]
            x_s[j, rows, :N] = (wave_ref[m0 + j, rows, :] * factor).astype(bf16)
            x_s[j, rows, N:] = (wave_ref[m0 + j, low, :] * factor).astype(bf16)

        loop(H // CHUNK, one, 2)
    along_rows(x_s, table, half_ref, m0)


def fixed_top_body(pat, s0, s1, wave_ref, table, half_ref, scale_s, x_s):
    set_scale(pat, 0, s0, s1, scale_s)
    pairs(wave_ref.shape[0], lambda m0: fixed_half(wave_ref, table, half_ref, scale_s, x_s, m0))


SCALE = [pltpu.VMEM((H, N), f32), pltpu.VMEM((PAIR, H, 2 * N), bf16)]


def fixed_top(pat, s0, s1, wave, table):
    nm = wave.shape[0]
    return local_call(
        fixed_top_body, "fixed_top", [LOCAL] * 5, [shape(nm, N, N, dtype=bf16)], SCALE, 6
    )(pat, s0, s1, wave, table)[0]


def gradients(core, block, bt, top, bot, patch_top, patch_bot, p_ref, keep_ref, send_ref, gtop, gbot, back_s, m):
    back_s[...] = jnp.dot(bt[:, :N], top[m], preferred_element_type=f32) + jnp.dot(
        bt[:, N:], bot[m], preferred_element_type=f32
    )
    for patch, g_ref, base in ((patch_top, gtop, 0), (patch_bot, gbot, 8)):

        def one(i):
            g = i + base
            rows = pl.ds(pl.multiple_of(i * 32 + block * 16, 16), 16)
            full = pl.ds(pl.multiple_of(g * 32 + block * 16, 16), 16)
            o_r = patch[0, rows, :]
            o_i = patch[1, rows, :]
            pr, pi, xr, xi = exit_rows(p_ref, m, full, o_r, o_i)
            rr = back_s[at(g, 16), :] - xr.astype(f32)
            ri = back_s[pl.ds(pl.multiple_of(g * 16 + H, 16), 16), :] - xi.astype(f32)
            g_ref[0, i] += pr * rr + pi * ri
            g_ref[1, i] += pr * ri - pi * rr
            st0 = o_r * rr + o_i * ri
            st1 = o_r * ri - o_i * rr
            turned_g = (g % 4) * 4 + g // 4
            keep_ref[m, jnp.where(core == 0, g, turned_g)] = jnp.where(core == 0, st0, st1)
            send_ref[m, jnp.where(core == 0, turned_g, g)] = jnp.where(core == 0, st1, st0)

        loop(8, one, UNROLL)


UNROLL = 8
LIMIT = 4
STAGE = pl.CostEstimate(flops=int(5e9), transcendentals=0, bytes_accessed=int(15e6))
GRADS = [shape(2, 2, 8, 16, N)] * 2


def first_block_body(pat, s0, s1, wave_ref, table, bt, top, ptop, pbot, p_ref, half_ref, keep, send, bots, tops, scale_s, x_s, back_s):
    gtop, gbot = tops.at[0], bots.at[0]
    set_scale(pat, H, s0, s1, scale_s)
    gtop[...] = jnp.zeros_like(gtop)
    gbot[...] = jnp.zeros_like(gbot)

    def step(m0):
        fixed_half(wave_ref, table, half_ref, scale_s, x_s, m0)
        for j in range(PAIR):
            gradients(lax.axis_index("core"), 0, bt, top, half_ref, ptop, pbot, p_ref, keep, send, gtop, gbot, back_s, m0 + j)

    pairs(wave_ref.shape[0], step)


def first_block(pat, s0, s1, wave, table, back_rows, top, ptop, pbot, probe):
    nm = wave.shape[0]
    return local_call(
        first_block_body,
        "first_block",
        [LOCAL] * 10,
        [shape(nm, N, N, dtype=bf16)] + [shape(nm, 16, 16, N)] * 2 + GRADS,
        SCALE + [pltpu.VMEM((N, N), f32)],
        9,
    )(pat, s0, s1, wave, table, back_rows, top, ptop, pbot, probe)


def second_block(back_rows, top, bot, ptop, pbot, probe, first, count, bots, tops, earlier=None):
    nm = top.shape[0]
    given = earlier or []

    def body(bt, top, bot, ptop, pbot, p_ref, *refs):
        keep, send, bots, tops, back_s = refs[2 + len(given) :]
        gtop, gbot = tops.at[1], bots.at[1]
        if not given:
            gtop[...] = jnp.zeros_like(gtop)
            gbot[...] = jnp.zeros_like(gbot)
        core = lax.axis_index("core")
        loop(
            count,
            lambda m: gradients(
                core, 1, bt, top, bot, ptop, pbot, p_ref, keep, send, gtop, gbot, back_s, m + first
            ),
        )

    return local_call(
        body,
        "second_block",
        [LOCAL] * (8 + len(given)),
        [shape(nm, 16, 16, N)] * 2 + GRADS,
        [pltpu.VMEM((N, N), f32)],
        6,
        {6: 2, 7: 3, **{8 + i: i for i in range(len(given))}},
    )(back_rows, top, bot, ptop, pbot, probe, bots, tops, *given)


SCAN = ("y", "z", "x", "core")
RING = ("y", "z", "core")


def along(value, steps):
    count = lax.axis_size(SCAN)
    lo, hi = max(0, -steps), min(count, count - steps)
    return lax.ppermute(value, SCAN, [(i, i + steps) for i in range(lo, hi)])


def swapped(value, axis):
    return lax.ppermute(value, axis, [(0, 1), (1, 0)])


def turned(value, steps, first):
    flat = lambda y, z, core: (y * 4 + z) * 2 + core
    pairs = []
    for y in range(4):
        for z in range(4):
            for core in range(2):
                on_y = (core == 0) == first
                to = ((y + steps) % 4, z) if on_y else (y, (z + steps) % 4)
                pairs.append((flat(y, z, core), flat(*to, core)))
    return lax.ppermute(value, RING, pairs)


def across(value, flip_mode, flip_x):
    pairs = [(2 * m + x, 2 * (m ^ flip_mode) + (x ^ flip_x)) for m in range(2) for x in range(2)]
    return lax.ppermute(value, ("mode", "x"), pairs)


def rim_body(place, obj, out):
    columns = window(place)

    def take(i):
        rows = at(i, CHUNK)
        out[:, rows, :] = obj[:, rows, columns]

    loop(H // CHUNK, take, 2)


def rim_rows(place, obj):
    return local_call(rim_body, "rim_rows", [SCALARS, LOCAL], [shape(2, H, N)], [], LIMIT)(place, obj)[0]


def brightest_body(own, far, out):
    def one(i, acc):
        return jnp.maximum(acc, own[at(i, 8), :] + far[at(i, 8), :])

    out[...] = lax.fori_loop(0, QUARTER // 8, one, jnp.zeros((8, N), f32))


def brightest(own, far):
    outs = [shape(8, N)]
    return local_call(brightest_body, "brightest", [LOCAL, LOCAL], outs, [], LIMIT, cost=STAGE)(own, far)[0]


def core_add_body(keep, recv, own, near, back, far0, far1):
    me = here()[0]
    n2 = own.shape[1]
    for m in range(2 * n2):
        j, k = m // n2, m % n2
        for out, turn in ((own, 0), (near, 1), (back, 3)):
            a = at(lax.rem(me + turn, 4), 4)
            out[j, k] = keep[m, a] + recv[m, a]
        a = at(lax.rem(me + 2, 4), 4)
        (far0, far1)[j][k] = keep[m, a] + recv[m, a]


def core_add(keep, recv):
    n2 = keep.shape[0] // 2
    outs = [shape(2, n2, 4, 16, N)] * 3 + [shape(n2, 4, 16, N)] * 2
    return local_call(core_add_body, "core_add", [LOCAL, LOCAL], outs, [], LIMIT, cost=STAGE)(keep, recv)


def relay_body(a, b, ra, rb, oa, ob):
    oa[0] = a[0] + ra[...]
    ob[1] = b[1] + rb[...]


def relay_add(near, back, ra, rb):
    outs = [shape(*near.shape)] * 2
    return local_call(relay_body, "relay_add", [LOCAL] * 4, outs, [], LIMIT, {0: 0, 1: 1}, cost=STAGE)(near, back, ra, rb)


def plane_add_body(*refs):
    me = here()[1]
    for block in range(2):
        own, ra, rb = refs[3 * block : 3 * block + 3]
        for turn in range(4):
            b = lax.rem(me + turn, 4)
            refs[6 + turn][block] = own[:, :, b] + (ra[:, :, b] + rb[:, :, b])


def plane_add(blocks):
    n2 = blocks[0][0].shape[1]
    outs = [shape(2, 2, n2, 16, N)] * 4
    return local_call(plane_add_body, "plane_add", [LOCAL] * 6, outs, [], LIMIT, cost=STAGE)(
        *blocks[0], *blocks[1]
    )


def line_add_body(most, a, b, c, d, keep, send):
    core = here()[2]
    n2 = a.shape[2]
    for side, out in ((core, keep), (1 - core, send)):
        rows = at(side, 8)
        for block in range(2):
            for j in range(2):
                first = (block * 2 + j) * n2
                out[first : first + n2] = (a[block, j, :, rows] + b[block, j, :, rows]) + (
                    c[block, j, :, rows] + d[block, j, :, rows]
                )
    send[4 * n2] = most[...]


def line_add(most, arrays):
    n2 = arrays[0].shape[2]
    outs = [shape(4 * n2, 8, N), shape(4 * n2 + 1, 8, N)]
    return local_call(line_add_body, "line_add", [LOCAL] * 5, outs, [], LIMIT, cost=STAGE)(most, *arrays)


def pixel_body(most, keep, recv, rows, mine, other):
    core, x = here()[2:4]
    scale = 1.0 / math.sqrt(64)
    nm = rows.shape[1]

    def fill(part, ref):
        mine[part] = ref[pl.ds(x * nm, nm)] * scale + rows[part]
        other[pl.ds(part * nm, nm)] = ref[pl.ds((1 - x) * nm, nm)] * scale

    @pl.when(core == 0)
    def _():
        fill(0, keep)
        fill(1, recv)

    @pl.when(core != 0)
    def _():
        fill(0, recv)
        fill(1, keep)

    other[2 * nm] = jnp.maximum(most[...], recv[2 * nm])


def pixel_step(most, keep, recv, rows):
    nm = rows.shape[1]
    outs = [shape(2, nm, 8, N), shape(2 * nm + 1, 8, N)]
    return local_call(pixel_body, "pixel_step", [LOCAL] * 4, outs, [], LIMIT, cost=STAGE)(most, keep, recv, rows)


def mix_body(w_ref, mine, b, c, d, out_ref):
    mode = here()[4]
    nm = mine.shape[1]
    for part in range(2):
        own = [mine[part, j] + b[part * nm + j] for j in range(nm)]
        far = [c[part, j] + d[part * nm + j] for j in range(nm)]
        for k in range(nm):
            row = mode * nm + k
            acc = jnp.zeros((8, N), f32)
            for j in range(nm):
                acc += (w_ref[row, mode * nm + j].astype(f32) / 16.0) * own[j]
                acc += (w_ref[row, (1 - mode) * nm + j].astype(f32) / 16.0) * far[j]
            out_ref[part, k] = acc.astype(bf16)


def mix(mixing, mine, b, c, d):
    outs = [shape(*mine.shape, dtype=bf16)]
    return local_call(mix_body, "mix", [SCALARS] + [LOCAL] * 4, outs, [], LIMIT)(mixing, mine, b, c, d)[0]


def object_body(place, before, near_max, far_max, obj, t, tf, b, bf, over, out, new, sems):
    shift, col = place[0], pl.multiple_of(place[1] * H, H)
    over_shift, over_col = before[0], pl.multiple_of(before[1] * H, H)
    last = near_max.shape[0] - 1
    largest = jnp.max(jnp.maximum(near_max[last], far_max[last]))
    copies = []
    for half in range(2):
        base = half * H

        def start(i):
            rows = at(i, CHUNK, base)
            new[:, rows, :] = obj[:, rows, :]

        loop(H // CHUNK, start, 2)

        def add(column, even, odd):
            def one(g):
                for block, values in ((0, even), (1, odd)):
                    rows = pl.ds(pl.multiple_of(g * 32 + base + block * 16, 16), 16)
                    total = values[0][:, g]
                    for v in values[1:]:
                        total = total + v[:, g]
                    new[:, rows, pl.ds(column, N)] += total / largest

            loop(8, one, 2)

        @pl.when(shift == half)
        def _():
            add(col, (t.at[0], tf.at[0]), (t.at[1], tf.at[1]))

        if half == 1:

            @pl.when(shift == 0)
            def _():
                add(col, (b.at[0], bf.at[0]), (b.at[1], bf.at[1]))

        else:

            @pl.when(over_shift == 1)
            def _():
                add(over_col, (over.at[0],), (over.at[1],))

        copy = pltpu.make_async_copy(new.at[:, pl.ds(base, H), :], out.at[:, pl.ds(base, H), :], sems.at[half])
        copy.start()
        copies.append(copy)
    for copy in copies:
        copy.wait()


def object_update(place, before, near_max, far_max, obj, pieces, over):
    return pl.pallas_call(
        object_body,
        in_specs=[SCALARS] * 2 + [LOCAL] * 8,
        out_specs=FAR,
        out_shape=shape(2, N, 4 * H),
        scratch_shapes=[pltpu.VMEM((2, N, 4 * H), f32), pltpu.SemaphoreType.DMA((2,))],
        compiler_params=params(10),
        name="object_update",
    )(place, before, near_max, far_max, obj, *pieces, over)


def over_body(g, gf, out):
    out[...] = g[...] + gf[...]


def over_sum(grads, far):
    outs = [shape(2, 2, 8, 16, N)]
    return local_call(over_body, "over_sum", [LOCAL] * 2, outs, [], LIMIT, cost=STAGE)(grads, far)[0]


def tied(*values):
    return lax.optimization_barrier(values)


def per_device(object_field, probe, patterns, row_shift, col_start, mixing):
    minus, plus, wave_top_rows, wave_bot_rows, back_rows0, back_rows1 = tables()
    place = jnp.concatenate([row_shift, col_start])
    before = along(place, 1)
    patch_top, own_bot, first_rows = own_rows(place, object_field)
    before, patch_top = tied(before, patch_top)
    rim = along(rim_rows(before, first_rows), -1)
    half_top, own_light, light_out, rows = top_half(patch_top, probe, minus)
    wave_top, wave_bot = first_terms(wave_top_rows, wave_bot_rows, half_top)
    rim, wave_top, light_out = tied(rim, wave_top, light_out)
    far_light = swapped(light_out, "mode")
    half_bot, patch_bot, wave_top, sum_top = bottom_half(
        place, own_bot, rim, probe, minus, wave_top_rows, wave_top
    )
    far_top = swapped(sum_top, "mode")
    half_bot, far_light = tied(half_bot, far_light)
    wave_bot, sum_bot = low_wave(wave_bot_rows, half_bot, wave_bot)
    far_bot = swapped(sum_bot, "mode")
    fixed = fixed_top(patterns, sum_top, far_top, wave_top, plus)
    low, keep0, send0, bots, tops = first_block(
        patterns, sum_bot, far_bot, wave_bot, plus, back_rows0, fixed, patch_top, patch_bot, probe
    )
    most = brightest(own_light, far_light)
    recv0 = swapped(send0, "core")
    *part1, bots, tops = second_block(back_rows1, fixed, low, patch_top, patch_bot, probe, 0, 3, bots, tops)
    own0, near0, back0, far0a, far0b = core_add(keep0, recv0)
    ra0, rb0 = turned(far0a, 1, True), turned(far0b, -1, True)
    *part1, near0 = tied(*part1, near0)
    keep1, send1, bots, tops = second_block(
        back_rows1, fixed, low, patch_top, patch_bot, probe, 3, 3, bots, tops, part1
    )
    bots_far = swapped(bots, "mode")
    recv1 = swapped(send1, "core")
    near0, back0 = relay_add(near0, back0, ra0, rb0)
    keep1, _ = tied(keep1, near0)
    own1, near1, back1, far1a, far1b = core_add(keep1, recv1)
    ra1, rb1 = turned(far1a, 1, True), turned(far1b, -1, True)
    plane0 = (own0, turned(near0, 1, True), turned(back0, -1, True))
    ra1, rb1, bots_far, *plane0 = tied(ra1, rb1, bots_far, *plane0)
    near1, back1 = relay_add(near1, back1, ra1, rb1)
    plane1 = (own1, turned(near1, 1, True), turned(back1, -1, True))
    tops_far = swapped(tops, "mode")
    over = along(over_sum(bots, bots_far), 1)
    line = plane_add((plane0, plane1))
    line = [line[0]] + [turned(line[r], r, False) for r in (1, 3, 2)]
    keep, send = line_add(most, line)
    recv = swapped(send, "core")
    mine, other = pixel_step(most, keep, recv, rows)
    beside = across(other, 0, 1)
    beside, over, tops_far = tied(beside, over, tops_far)
    probe_new = mix(mixing, mine, beside, across(mine, 1, 0), across(other, 1, 1))
    object_new = object_update(place, before, other, beside, object_field, (tops, tops_far, bots, bots_far), over)
    return object_new, probe_new


def solution(mesh):
    split = Mesh(mesh.devices.reshape(2, 4, 4, 2, 2), ("mode", *SCAN))
    return jax.shard_map(
        per_device,
        mesh=split,
        in_specs=(P(None, SCAN, None), P(None, "mode", None, None), P(SCAN, None, None), P(SCAN), P(SCAN), P()),
        out_specs=(P(None, SCAN, None), P(None, "mode", SCAN, None)),
        check_vma=False,
    )
```

```python
import functools
import math

import jax
import jax.numpy as jnp
import ml_dtypes
import numpy as np
from jax import lax
from jax.experimental import pallas as pl
from jax.experimental.pallas import tpu as pltpu
from jax.sharding import Mesh
from jax.sharding import PartitionSpec as P

f32, bf16 = jnp.float32, jnp.bfloat16
N = 512
H = 256
CHUNK = 32
QUARTER = 128
PAIR = 2


def tables():
    i = np.arange(N, dtype=np.int32)
    angle = (i[:, None] * i[None, :] % N).astype(np.float32) * np.float32(2.0 * math.pi / N)
    factor = np.float32(1.0 / math.sqrt(N))
    c = (np.cos(angle) * factor).astype(ml_dtypes.bfloat16)
    s = (np.sin(angle) * factor).astype(ml_dtypes.bfloat16)
    minus = np.block([[c, -s], [s, c]])
    plus = np.block([[c, s], [-s, c]])

    def stacked(table):
        return table.reshape(2 * N, 2, 2, H).swapaxes(1, 2).reshape(2 * N, 2 * N)

    wave_rows = stacked(plus).reshape(2, 2, H, 2 * N).swapaxes(0, 1).reshape(2, N, 2 * N)
    back_rows = stacked(minus).reshape(2, 16, 2, 16, 2 * N).transpose(2, 0, 1, 3, 4).reshape(2, N, 2 * N)
    return minus, plus, wave_rows[0], wave_rows[1], back_rows[0], back_rows[1]


def shape(*dims, dtype=f32):
    return jax.ShapeDtypeStruct(dims, dtype)


def whole(*dims):
    return pl.BlockSpec(dims, lambda *_: (0,) * len(dims))


def params(mib):
    return pltpu.CompilerParams(vmem_limit_bytes=mib << 20)


SCALARS = pl.BlockSpec(memory_space=pltpu.SMEM)
LOCAL = pl.BlockSpec(memory_space=pltpu.VMEM)
FAR = pl.BlockSpec(memory_space=pltpu.HBM)


def local_call(body, name, ins, outs, scratch, mib, alias=None, cost=None):
    def call(*args):
        return pl.pallas_call(
            body,
            in_specs=ins,
            out_specs=[LOCAL] * len(outs),
            out_shape=outs,
            scratch_shapes=scratch,
            compiler_params=params(mib),
            input_output_aliases=alias or {},
            name=name,
            cost_estimate=cost,
        )(*args)

    return call


def loop(count, fn, unroll=1):
    def body(i, carry):
        fn(i)
        return carry

    lax.fori_loop(0, count, body, 0, unroll=unroll)


def at(i, size, base=0):
    return pl.ds(pl.multiple_of(i * size + base, min(size, base) if base else size), size)


def here():
    y, z, x, core, mode = (lax.axis_index(a) for a in ("y", "z", "x", "core", "mode"))
    return jnp.where(core == 0, y, z), jnp.where(core == 0, z, y), core, x, mode


def exit_rows(p_ref, m, rows, o_r, o_i):
    pr = p_ref[0, m, rows, :].astype(f32)
    pi = p_ref[1, m, rows, :].astype(f32)
    return pr, pi, (pr * o_r - pi * o_i).astype(bf16), (pr * o_i + pi * o_r).astype(bf16)


def exit_half(p_ref, m, j, base, patch, x_s):
    def one(i):
        rows = at(i, CHUNK)
        _, _, xr, xi = exit_rows(p_ref, m, at(i, CHUNK, base), patch[0, rows, :], patch[1, rows, :])
        x_s[j, rows, :N] = xr
        x_s[j, rows, N:] = xi

    loop(H // CHUNK, one, 2)


def along_rows(x_s, table, out, m0):
    x = x_s[...].reshape(PAIR * H, 2 * N)
    half = jnp.dot(x, table[...], preferred_element_type=f32).astype(bf16)
    for j in range(PAIR):
        out[m0 + j, :H] = half[j * H : (j + 1) * H, :N]
        out[m0 + j, H:] = half[j * H : (j + 1) * H, N:]


def pairs(p_ref, fn):
    nm = p_ref
    loop(nm // PAIR, lambda k: fn(k * PAIR))


def window(place):
    return pl.ds(pl.multiple_of(place[1] * H, H), N)


def own_body(place, obj, top_ref, bot_ref, first_ref):
    columns = window(place)
    top = place[0] * H

    def take(i):
        rows = at(i, CHUNK)
        top_ref[:, rows, :] = obj[:, pl.ds(pl.multiple_of(top + i * CHUNK, CHUNK), CHUNK), columns]
        bot_ref[:, rows, :] = obj[:, at(i, CHUNK, H), columns]
        first_ref[:, rows, :] = obj[:, rows, :]

    loop(H // CHUNK, take, 2)


def own_rows(place, obj):
    return local_call(own_body, "own_rows", [SCALARS, LOCAL], [shape(2, H, N)] * 2 + [shape(2, H, 2 * N)], [], LIMIT)(
        place, obj
    )


def top_body(patch_ref, p_ref, table, half_ref, own_part, far_part, rows_ref, x_s):
    def step(m0):
        for j in range(PAIR):
            exit_half(p_ref, m0 + j, j, 0, patch_ref, x_s)
        along_rows(x_s, table, half_ref, m0)

    pairs(p_ref.shape[1], step)
    core, x = lax.axis_index("core"), lax.axis_index("x")
    base = (core * 2 + x) * QUARTER

    def lit(i):
        rows = pl.ds(pl.multiple_of(base + i * CHUNK, CHUNK), CHUNK)
        acc = jnp.zeros((CHUNK, N), f32)
        for m in range(p_ref.shape[1]):
            pr = p_ref[0, m, rows, :].astype(f32)
            pi = p_ref[1, m, rows, :].astype(f32)
            acc = acc + (pr * pr + pi * pi)
        own_part[at(i, CHUNK), :] = acc
        far_part[at(i, CHUNK), :] = acc

    loop(QUARTER // CHUNK, lit)
    chip = (lax.axis_index("y") * 4 + lax.axis_index("z")) * 2 + lax.axis_index("x")
    for part in range(2):
        for m in range(p_ref.shape[1]):
            both = p_ref[part, m, at(chip, 16), :].astype(f32)
            rows_ref[part, m] = jnp.where(core == 0, both[:8], both[8:])


def top_half(patch, probe, table):
    nm = probe.shape[1]
    return local_call(
        top_body,
        "top_half",
        [LOCAL, LOCAL, LOCAL],
        [shape(nm, N, N, dtype=bf16), shape(QUARTER, N), shape(QUARTER, N), shape(2, nm, 8, N)],
        [pltpu.VMEM((PAIR, H, 2 * N), bf16)],
        6,
    )(patch, probe, table)


def first_terms_body(wt0, wt1, top, wave0, wave1):
    def step(m):
        wave0[m] = jnp.dot(wt0[:, :N], top[m], preferred_element_type=f32)
        wave1[m] = jnp.dot(wt1[:, :N], top[m], preferred_element_type=f32)

    loop(top.shape[0], step)


def first_terms(wt0, wt1, top):
    nm = top.shape[0]
    return local_call(first_terms_body, "first_terms", [LOCAL] * 3, [shape(nm, N, N)] * 2, [], 5)(wt0, wt1, top)


def wave_half(wave_ref, sum_ref, wt, bot, m0):
    for j in range(PAIR):
        m = m0 + j
        wave_ref[m] += jnp.dot(wt[:, N:], bot[m], preferred_element_type=f32)

    def one(i):
        rows = at(i, CHUNK)
        low = at(i, CHUNK, H)
        acc = sum_ref[rows, :]
        for j in range(PAIR):
            a = wave_ref[m0 + j, rows, :]
            b = wave_ref[m0 + j, low, :]
            acc = acc + (a * a + b * b)
        sum_ref[rows, :] = acc

    loop(H // CHUNK, one, 2)


def bottom_body(place, own, rim, p_ref, table, wt, _, half_ref, patch_ref, wave_ref, sum_ref, x_s):
    @pl.when(place[0] == 0)
    def _():
        patch_ref[...] = own[...]

    @pl.when(place[0] != 0)
    def _():
        patch_ref[...] = rim[...]

    sum_ref[...] = jnp.zeros_like(sum_ref)

    def step(m0):
        for j in range(PAIR):
            exit_half(p_ref, m0 + j, j, H, patch_ref, x_s)
        along_rows(x_s, table, half_ref, m0)
        wave_half(wave_ref, sum_ref, wt, half_ref, m0)

    pairs(p_ref.shape[1], step)


def bottom_half(place, own, rim, probe, table, wave_rows, wave):
    nm = probe.shape[1]
    return local_call(
        bottom_body,
        "bottom_half",
        [SCALARS] + [LOCAL] * 6,
        [shape(nm, N, N, dtype=bf16), shape(2, H, N), shape(nm, N, N), shape(H, N)],
        [pltpu.VMEM((PAIR, H, 2 * N), bf16)],
        8,
        {6: 2},
    )(place, own, rim, probe, table, wave_rows, wave)


def low_wave_body(wt, bot, _, wave_ref, sum_ref):
    sum_ref[...] = jnp.zeros_like(sum_ref)
    pairs(bot.shape[0], lambda m0: wave_half(wave_ref, sum_ref, wt, bot, m0))


def low_wave(wave_rows, bot, wave):
    outs = [shape(*wave.shape), shape(H, N)]
    return local_call(low_wave_body, "low_wave", [LOCAL] * 3, outs, [], 5, {2: 0})(wave_rows, bot, wave)


def set_scale(pat, base, s0, s1, scale_s):
    def one(i):
        rows = at(i, CHUNK)
        total = jnp.maximum(s0[rows, :] + s1[rows, :], 1.0)
        scale_s[rows, :] = jnp.sqrt(pat[0, at(i, CHUNK, base), :]) / jnp.sqrt(total)

    loop(H // CHUNK, one)


def fixed_half(wave_ref, table, half_ref, scale_s, x_s, m0):
    for j in range(PAIR):

        def one(i):
            rows = at(i, CHUNK)
            low = at(i, CHUNK, H)
            factor = scale_s[rows, :]
            x_s[j, rows, :N] = (wave_ref[m0 + j, rows, :] * factor).astype(bf16)
            x_s[j, rows, N:] = (wave_ref[m0 + j, low, :] * factor).astype(bf16)

        loop(H // CHUNK, one, 2)
    along_rows(x_s, table, half_ref, m0)


def fixed_top_body(pat, s0, s1, wave_ref, table, half_ref, scale_s, x_s):
    set_scale(pat, 0, s0, s1, scale_s)
    pairs(wave_ref.shape[0], lambda m0: fixed_half(wave_ref, table, half_ref, scale_s, x_s, m0))


SCALE = [pltpu.VMEM((H, N), f32), pltpu.VMEM((PAIR, H, 2 * N), bf16)]


def fixed_top(pat, s0, s1, wave, table):
    nm = wave.shape[0]
    return local_call(
        fixed_top_body, "fixed_top", [LOCAL] * 5, [shape(nm, N, N, dtype=bf16)], SCALE, 6
    )(pat, s0, s1, wave, table)[0]


def gradients(core, block, bt, top, bot, patch_top, patch_bot, p_ref, keep_ref, send_ref, gtop, gbot, back_s, m):
    back_s[...] = jnp.dot(bt[:, :N], top[m], preferred_element_type=f32) + jnp.dot(
        bt[:, N:], bot[m], preferred_element_type=f32
    )
    for patch, g_ref, base in ((patch_top, gtop, 0), (patch_bot, gbot, 8)):

        def one(i):
            g = i + base
            rows = pl.ds(pl.multiple_of(i * 32 + block * 16, 16), 16)
            full = pl.ds(pl.multiple_of(g * 32 + block * 16, 16), 16)
            o_r = patch[0, rows, :]
            o_i = patch[1, rows, :]
            pr, pi, xr, xi = exit_rows(p_ref, m, full, o_r, o_i)
            rr = back_s[at(g, 16), :] - xr.astype(f32)
            ri = back_s[pl.ds(pl.multiple_of(g * 16 + H, 16), 16), :] - xi.astype(f32)
            g_ref[0, i] += pr * rr + pi * ri
            g_ref[1, i] += pr * ri - pi * rr
            st0 = o_r * rr + o_i * ri
            st1 = o_r * ri - o_i * rr
            turned_g = (g % 4) * 4 + g // 4
            keep_ref[m, jnp.where(core == 0, g, turned_g)] = jnp.where(core == 0, st0, st1)
            send_ref[m, jnp.where(core == 0, turned_g, g)] = jnp.where(core == 0, st1, st0)

        loop(8, one, UNROLL)


UNROLL = 8
LIMIT = 4
STAGE = pl.CostEstimate(flops=int(5e9), transcendentals=0, bytes_accessed=int(15e6))
GRADS = [shape(2, 2, 8, 16, N)] * 2


def first_block_body(pat, s0, s1, wave_ref, table, bt, top, ptop, pbot, p_ref, half_ref, keep, send, bots, tops, scale_s, x_s, back_s):
    gtop, gbot = tops.at[0], bots.at[0]
    set_scale(pat, H, s0, s1, scale_s)
    gtop[...] = jnp.zeros_like(gtop)
    gbot[...] = jnp.zeros_like(gbot)

    def step(m0):
        fixed_half(wave_ref, table, half_ref, scale_s, x_s, m0)
        for j in range(PAIR):
            gradients(lax.axis_index("core"), 0, bt, top, half_ref, ptop, pbot, p_ref, keep, send, gtop, gbot, back_s, m0 + j)

    pairs(wave_ref.shape[0], step)


def first_block(pat, s0, s1, wave, table, back_rows, top, ptop, pbot, probe):
    nm = wave.shape[0]
    return local_call(
        first_block_body,
        "first_block",
        [LOCAL] * 10,
        [shape(nm, N, N, dtype=bf16)] + [shape(nm, 16, 16, N)] * 2 + GRADS,
        SCALE + [pltpu.VMEM((N, N), f32)],
        9,
    )(pat, s0, s1, wave, table, back_rows, top, ptop, pbot, probe)


def second_block(back_rows, top, bot, ptop, pbot, probe, first, count, bots, tops, earlier=None):
    nm = top.shape[0]
    given = earlier or []

    def body(bt, top, bot, ptop, pbot, p_ref, *refs):
        keep, send, bots, tops, back_s = refs[2 + len(given) :]
        gtop, gbot = tops.at[1], bots.at[1]
        if not given:
            gtop[...] = jnp.zeros_like(gtop)
            gbot[...] = jnp.zeros_like(gbot)
        core = lax.axis_index("core")
        loop(
            count,
            lambda m: gradients(
                core, 1, bt, top, bot, ptop, pbot, p_ref, keep, send, gtop, gbot, back_s, m + first
            ),
        )

    return local_call(
        body,
        "second_block",
        [LOCAL] * (8 + len(given)),
        [shape(nm, 16, 16, N)] * 2 + GRADS,
        [pltpu.VMEM((N, N), f32)],
        6,
        {6: 2, 7: 3, **{8 + i: i for i in range(len(given))}},
    )(back_rows, top, bot, ptop, pbot, probe, bots, tops, *given)


SCAN = ("y", "z", "x", "core")
RING = ("y", "z", "core")


def along(value, steps):
    count = lax.axis_size(SCAN)
    lo, hi = max(0, -steps), min(count, count - steps)
    return lax.ppermute(value, SCAN, [(i, i + steps) for i in range(lo, hi)])


def swapped(value, axis):
    return lax.ppermute(value, axis, [(0, 1), (1, 0)])


def turned(value, steps, first):
    flat = lambda y, z, core: (y * 4 + z) * 2 + core
    pairs = []
    for y in range(4):
        for z in range(4):
            for core in range(2):
                on_y = (core == 0) == first
                to = ((y + steps) % 4, z) if on_y else (y, (z + steps) % 4)
                pairs.append((flat(y, z, core), flat(*to, core)))
    return lax.ppermute(value, RING, pairs)


def across(value, flip_mode, flip_x):
    pairs = [(2 * m + x, 2 * (m ^ flip_mode) + (x ^ flip_x)) for m in range(2) for x in range(2)]
    return lax.ppermute(value, ("mode", "x"), pairs)


def rim_body(place, obj, out):
    columns = window(place)

    def take(i):
        rows = at(i, CHUNK)
        out[:, rows, :] = obj[:, rows, columns]

    loop(H // CHUNK, take, 2)


def rim_rows(place, obj):
    return local_call(rim_body, "rim_rows", [SCALARS, LOCAL], [shape(2, H, N)], [], LIMIT)(place, obj)[0]


def brightest_body(own, far, out):
    def one(i, acc):
        return jnp.maximum(acc, own[at(i, 8), :] + far[at(i, 8), :])

    out[...] = lax.fori_loop(0, QUARTER // 8, one, jnp.zeros((8, N), f32))


def brightest(own, far):
    outs = [shape(8, N)]
    return local_call(brightest_body, "brightest", [LOCAL, LOCAL], outs, [], LIMIT, cost=STAGE)(own, far)[0]


def core_add_body(keep, recv, own, near, back, far0, far1):
    me = here()[0]
    n2 = own.shape[1]
    for m in range(2 * n2):
        j, k = m // n2, m % n2
        for out, turn in ((own, 0), (near, 1), (back, 3)):
            a = at(lax.rem(me + turn, 4), 4)
            out[j, k] = keep[m, a] + recv[m, a]
        a = at(lax.rem(me + 2, 4), 4)
        (far0, far1)[j][k] = keep[m, a] + recv[m, a]


def core_add(keep, recv):
    n2 = keep.shape[0] // 2
    outs = [shape(2, n2, 4, 16, N)] * 3 + [shape(n2, 4, 16, N)] * 2
    return local_call(core_add_body, "core_add", [LOCAL, LOCAL], outs, [], LIMIT, cost=STAGE)(keep, recv)


def relay_body(a, b, ra, rb, oa, ob):
    oa[0] = a[0] + ra[...]
    ob[1] = b[1] + rb[...]


def relay_add(near, back, ra, rb):
    outs = [shape(*near.shape)] * 2
    return local_call(relay_body, "relay_add", [LOCAL] * 4, outs, [], LIMIT, {0: 0, 1: 1}, cost=STAGE)(near, back, ra, rb)


def plane_add_body(*refs):
    me = here()[1]
    for block in range(2):
        own, ra, rb = refs[3 * block : 3 * block + 3]
        for turn in range(4):
            b = lax.rem(me + turn, 4)
            refs[6 + turn][block] = own[:, :, b] + (ra[:, :, b] + rb[:, :, b])


def plane_add(blocks):
    n2 = blocks[0][0].shape[1]
    outs = [shape(2, 2, n2, 16, N)] * 4
    return local_call(plane_add_body, "plane_add", [LOCAL] * 6, outs, [], LIMIT, cost=STAGE)(
        *blocks[0], *blocks[1]
    )


def line_add_body(most, a, b, c, d, keep, send):
    core = here()[2]
    n2 = a.shape[2]
    for side, out in ((core, keep), (1 - core, send)):
        rows = at(side, 8)
        for block in range(2):
            for j in range(2):
                first = (block * 2 + j) * n2
                out[first : first + n2] = (a[block, j, :, rows] + b[block, j, :, rows]) + (
                    c[block, j, :, rows] + d[block, j, :, rows]
                )
    send[4 * n2] = most[...]


def line_add(most, arrays):
    n2 = arrays[0].shape[2]
    outs = [shape(4 * n2, 8, N), shape(4 * n2 + 1, 8, N)]
    return local_call(line_add_body, "line_add", [LOCAL] * 5, outs, [], LIMIT, cost=STAGE)(most, *arrays)


def pixel_body(most, keep, recv, rows, mine, other):
    core, x = here()[2:4]
    scale = 1.0 / math.sqrt(64)
    nm = rows.shape[1]

    def fill(part, ref):
        mine[part] = ref[pl.ds(x * nm, nm)] * scale + rows[part]
        other[pl.ds(part * nm, nm)] = ref[pl.ds((1 - x) * nm, nm)] * scale

    @pl.when(core == 0)
    def _():
        fill(0, keep)
        fill(1, recv)

    @pl.when(core != 0)
    def _():
        fill(0, recv)
        fill(1, keep)

    other[2 * nm] = jnp.maximum(most[...], recv[2 * nm])


def pixel_step(most, keep, recv, rows):
    nm = rows.shape[1]
    outs = [shape(2, nm, 8, N), shape(2 * nm + 1, 8, N)]
    return local_call(pixel_body, "pixel_step", [LOCAL] * 4, outs, [], LIMIT, cost=STAGE)(most, keep, recv, rows)


def mix_body(w_ref, mine, b, c, d, out_ref):
    mode = here()[4]
    nm = mine.shape[1]
    for part in range(2):
        own = [mine[part, j] + b[part * nm + j] for j in range(nm)]
        far = [c[part, j] + d[part * nm + j] for j in range(nm)]
        for k in range(nm):
            row = mode * nm + k
            acc = jnp.zeros((8, N), f32)
            for j in range(nm):
                acc += (w_ref[row, mode * nm + j].astype(f32) / 16.0) * own[j]
                acc += (w_ref[row, (1 - mode) * nm + j].astype(f32) / 16.0) * far[j]
            out_ref[part, k] = acc.astype(bf16)


def mix(mixing, mine, b, c, d):
    outs = [shape(*mine.shape, dtype=bf16)]
    return local_call(mix_body, "mix", [SCALARS] + [LOCAL] * 4, outs, [], LIMIT)(mixing, mine, b, c, d)[0]


def object_body(place, before, near_max, far_max, obj, t, tf, b, bf, over, out, new, sems):
    shift, col = place[0], pl.multiple_of(place[1] * H, H)
    over_shift, over_col = before[0], pl.multiple_of(before[1] * H, H)
    last = near_max.shape[0] - 1
    largest = jnp.max(jnp.maximum(near_max[last], far_max[last]))
    copies = []
    for half in range(2):
        base = half * H

        def start(i):
            rows = at(i, CHUNK, base)
            new[:, rows, :] = obj[:, rows, :]

        loop(H // CHUNK, start, 2)

        def add(column, even, odd):
            def one(g):
                for block, values in ((0, even), (1, odd)):
                    rows = pl.ds(pl.multiple_of(g * 32 + base + block * 16, 16), 16)
                    total = values[0][:, g]
                    for v in values[1:]:
                        total = total + v[:, g]
                    new[:, rows, pl.ds(column, N)] += total / largest

            loop(8, one, 2)

        @pl.when(shift == half)
        def _():
            add(col, (t.at[0], tf.at[0]), (t.at[1], tf.at[1]))

        if half == 1:

            @pl.when(shift == 0)
            def _():
                add(col, (b.at[0], bf.at[0]), (b.at[1], bf.at[1]))

        else:

            @pl.when(over_shift == 1)
            def _():
                add(over_col, (over.at[0],), (over.at[1],))

        copy = pltpu.make_async_copy(new.at[:, pl.ds(base, H), :], out.at[:, pl.ds(base, H), :], sems.at[half])
        copy.start()
        copies.append(copy)
    for copy in copies:
        copy.wait()


def object_update(place, before, near_max, far_max, obj, pieces, over):
    return pl.pallas_call(
        object_body,
        in_specs=[SCALARS] * 2 + [LOCAL] * 8,
        out_specs=FAR,
        out_shape=shape(2, N, 4 * H),
        scratch_shapes=[pltpu.VMEM((2, N, 4 * H), f32), pltpu.SemaphoreType.DMA((2,))],
        compiler_params=params(10),
        name="object_update",
    )(place, before, near_max, far_max, obj, *pieces, over)


def over_body(g, gf, out):
    out[...] = g[...] + gf[...]


def over_sum(grads, far):
    outs = [shape(2, 2, 8, 16, N)]
    return local_call(over_body, "over_sum", [LOCAL] * 2, outs, [], LIMIT, cost=STAGE)(grads, far)[0]


def tied(*values):
    return lax.optimization_barrier(values)


def per_device(object_field, probe, patterns, row_shift, col_start, mixing):
    minus, plus, wave_top_rows, wave_bot_rows, back_rows0, back_rows1 = tables()
    place = jnp.concatenate([row_shift, col_start])
    before = along(place, 1)
    patch_top, own_bot, first_rows = own_rows(place, object_field)
    before, patch_top = tied(before, patch_top)
    rim = along(rim_rows(before, first_rows), -1)
    half_top, own_light, light_out, rows = top_half(patch_top, probe, minus)
    wave_top, wave_bot = first_terms(wave_top_rows, wave_bot_rows, half_top)
    rim, wave_top, light_out = tied(rim, wave_top, light_out)
    far_light = swapped(light_out, "mode")
    half_bot, patch_bot, wave_top, sum_top = bottom_half(
        place, own_bot, rim, probe, minus, wave_top_rows, wave_top
    )
    far_top = swapped(sum_top, "mode")
    half_bot, far_light = tied(half_bot, far_light)
    wave_bot, sum_bot = low_wave(wave_bot_rows, half_bot, wave_bot)
    far_bot = swapped(sum_bot, "mode")
    fixed = fixed_top(patterns, sum_top, far_top, wave_top, plus)
    low, keep0, send0, bots, tops = first_block(
        patterns, sum_bot, far_bot, wave_bot, plus, back_rows0, fixed, patch_top, patch_bot, probe
    )
    most = brightest(own_light, far_light)
    recv0 = swapped(send0, "core")
    *part1, bots, tops = second_block(back_rows1, fixed, low, patch_top, patch_bot, probe, 0, 3, bots, tops)
    own0, near0, back0, far0a, far0b = core_add(keep0, recv0)
    ra0, rb0 = turned(far0a, 1, True), turned(far0b, -1, True)
    *part1, near0 = tied(*part1, near0)
    keep1, send1, bots, tops = second_block(
        back_rows1, fixed, low, patch_top, patch_bot, probe, 3, 3, bots, tops, part1
    )
    bots_far = swapped(bots, "mode")
    recv1 = swapped(send1, "core")
    near0, back0 = relay_add(near0, back0, ra0, rb0)
    keep1, _ = tied(keep1, near0)
    own1, near1, back1, far1a, far1b = core_add(keep1, recv1)
    ra1, rb1 = turned(far1a, 1, True), turned(far1b, -1, True)
    plane0 = (own0, turned(near0, 1, True), turned(back0, -1, True))
    ra1, rb1, bots_far, *plane0 = tied(ra1, rb1, bots_far, *plane0)
    near1, back1 = relay_add(near1, back1, ra1, rb1)
    plane1 = (own1, turned(near1, 1, True), turned(back1, -1, True))
    tops_far = swapped(tops, "mode")
    over_out = over_sum(bots, bots_far)
    line = plane_add((plane0, plane1))
    line = [line[0]] + [turned(line[r], r, False) for r in (1, 3, 2)]
    keep, send = line_add(most, line)
    over_out, _ = tied(over_out, keep)
    over = along(over_out, 1)
    recv = swapped(send, "core")
    mine, other = pixel_step(most, keep, recv, rows)
    beside = across(other, 0, 1)
    beside, over, tops_far = tied(beside, over, tops_far)
    probe_new = mix(mixing, mine, beside, across(mine, 1, 0), across(other, 1, 1))
    object_new = object_update(place, before, other, beside, object_field, (tops, tops_far, bots, bots_far), over)
    return object_new, probe_new


def solution(mesh):
    split = Mesh(mesh.devices.reshape(2, 4, 4, 2, 2), ("mode", *SCAN))
    return jax.shard_map(
        per_device,
        mesh=split,
        in_specs=(P(None, SCAN, None), P(None, "mode", None, None), P(SCAN, None, None), P(SCAN), P(SCAN), P()),
        out_specs=(P(None, SCAN, None), P(None, "mode", SCAN, None)),
        check_vma=False,
    )
```

```python
import functools
import math

import jax
import jax.numpy as jnp
import ml_dtypes
import numpy as np
from jax import lax
from jax.experimental import pallas as pl
from jax.experimental.pallas import tpu as pltpu
from jax.sharding import Mesh
from jax.sharding import PartitionSpec as P

f32, bf16 = jnp.float32, jnp.bfloat16
N = 512
H = 256
CHUNK = 32
QUARTER = 128
PAIR = 2


def tables():
    i = np.arange(N, dtype=np.int32)
    angle = (i[:, None] * i[None, :] % N).astype(np.float32) * np.float32(2.0 * math.pi / N)
    factor = np.float32(1.0 / math.sqrt(N))
    c = (np.cos(angle) * factor).astype(ml_dtypes.bfloat16)
    s = (np.sin(angle) * factor).astype(ml_dtypes.bfloat16)
    minus = np.block([[c, -s], [s, c]])
    plus = np.block([[c, s], [-s, c]])

    def stacked(table):
        return table.reshape(2 * N, 2, 2, H).swapaxes(1, 2).reshape(2 * N, 2 * N)

    wave_rows = stacked(plus).reshape(2, 2, H, 2 * N).swapaxes(0, 1).reshape(2, N, 2 * N)
    back_rows = stacked(minus).reshape(2, 16, 2, 16, 2 * N).transpose(2, 0, 1, 3, 4).reshape(2, N, 2 * N)
    return minus, plus, wave_rows[0], wave_rows[1], back_rows[0], back_rows[1]


def shape(*dims, dtype=f32):
    return jax.ShapeDtypeStruct(dims, dtype)


def whole(*dims):
    return pl.BlockSpec(dims, lambda *_: (0,) * len(dims))


def params(mib):
    return pltpu.CompilerParams(vmem_limit_bytes=mib << 20)


SCALARS = pl.BlockSpec(memory_space=pltpu.SMEM)
LOCAL = pl.BlockSpec(memory_space=pltpu.VMEM)
FAR = pl.BlockSpec(memory_space=pltpu.HBM)


def local_call(body, name, ins, outs, scratch, mib, alias=None, cost=None):
    def call(*args):
        return pl.pallas_call(
            body,
            in_specs=ins,
            out_specs=[LOCAL] * len(outs),
            out_shape=outs,
            scratch_shapes=scratch,
            compiler_params=params(mib),
            input_output_aliases=alias or {},
            name=name,
            cost_estimate=cost,
        )(*args)

    return call


def loop(count, fn, unroll=1):
    def body(i, carry):
        fn(i)
        return carry

    lax.fori_loop(0, count, body, 0, unroll=unroll)


def at(i, size, base=0):
    return pl.ds(pl.multiple_of(i * size + base, min(size, base) if base else size), size)


def here():
    y, z, x, core, mode = (lax.axis_index(a) for a in ("y", "z", "x", "core", "mode"))
    return jnp.where(core == 0, y, z), jnp.where(core == 0, z, y), core, x, mode


def exit_rows(p_ref, m, rows, o_r, o_i):
    pr = p_ref[0, m, rows, :].astype(f32)
    pi = p_ref[1, m, rows, :].astype(f32)
    return pr, pi, (pr * o_r - pi * o_i).astype(bf16), (pr * o_i + pi * o_r).astype(bf16)


def exit_half(p_ref, m, j, base, patch, x_s):
    def one(i):
        rows = at(i, CHUNK)
        _, _, xr, xi = exit_rows(p_ref, m, at(i, CHUNK, base), patch[0, rows, :], patch[1, rows, :])
        x_s[j, rows, :N] = xr
        x_s[j, rows, N:] = xi

    loop(H // CHUNK, one, 2)


def along_rows(x_s, table, out, m0):
    x = x_s[...].reshape(PAIR * H, 2 * N)
    half = jnp.dot(x, table[...], preferred_element_type=f32).astype(bf16)
    for j in range(PAIR):
        out[m0 + j, :H] = half[j * H : (j + 1) * H, :N]
        out[m0 + j, H:] = half[j * H : (j + 1) * H, N:]


def pairs(p_ref, fn):
    nm = p_ref
    loop(nm // PAIR, lambda k: fn(k * PAIR))


def window(place):
    return pl.ds(pl.multiple_of(place[1] * H, H), N)


def own_body(place, obj, top_ref, bot_ref, first_ref):
    columns = window(place)
    top = place[0] * H

    def take(i):
        rows = at(i, CHUNK)
        top_ref[:, rows, :] = obj[:, pl.ds(pl.multiple_of(top + i * CHUNK, CHUNK), CHUNK), columns]
        bot_ref[:, rows, :] = obj[:, at(i, CHUNK, H), columns]
        first_ref[:, rows, :] = obj[:, rows, :]

    loop(H // CHUNK, take, 2)


def own_rows(place, obj):
    return local_call(own_body, "own_rows", [SCALARS, LOCAL], [shape(2, H, N)] * 2 + [shape(2, H, 2 * N)], [], LIMIT)(
        place, obj
    )


def top_body(patch_ref, p_ref, table, half_ref, own_part, far_part, rows_ref, x_s):
    def step(m0):
        for j in range(PAIR):
            exit_half(p_ref, m0 + j, j, 0, patch_ref, x_s)
        along_rows(x_s, table, half_ref, m0)

    pairs(p_ref.shape[1], step)
    core, x = lax.axis_index("core"), lax.axis_index("x")
    base = (core * 2 + x) * QUARTER

    def lit(i):
        rows = pl.ds(pl.multiple_of(base + i * CHUNK, CHUNK), CHUNK)
        acc = jnp.zeros((CHUNK, N), f32)
        for m in range(p_ref.shape[1]):
            pr = p_ref[0, m, rows, :].astype(f32)
            pi = p_ref[1, m, rows, :].astype(f32)
            acc = acc + (pr * pr + pi * pi)
        own_part[at(i, CHUNK), :] = acc
        far_part[at(i, CHUNK), :] = acc

    loop(QUARTER // CHUNK, lit)
    chip = (lax.axis_index("y") * 4 + lax.axis_index("z")) * 2 + lax.axis_index("x")
    for part in range(2):
        for m in range(p_ref.shape[1]):
            both = p_ref[part, m, at(chip, 16), :].astype(f32)
            rows_ref[part, m] = jnp.where(core == 0, both[:8], both[8:])


def top_half(patch, probe, table):
    nm = probe.shape[1]
    return local_call(
        top_body,
        "top_half",
        [LOCAL, LOCAL, LOCAL],
        [shape(nm, N, N, dtype=bf16), shape(QUARTER, N), shape(QUARTER, N), shape(2, nm, 8, N)],
        [pltpu.VMEM((PAIR, H, 2 * N), bf16)],
        6,
    )(patch, probe, table)


def first_terms_body(wt0, wt1, top, wave0, wave1):
    def step(m):
        wave0[m] = jnp.dot(wt0[:, :N], top[m], preferred_element_type=f32)
        wave1[m] = jnp.dot(wt1[:, :N], top[m], preferred_element_type=f32)

    loop(top.shape[0], step)


def first_terms(wt0, wt1, top):
    nm = top.shape[0]
    return local_call(first_terms_body, "first_terms", [LOCAL] * 3, [shape(nm, N, N)] * 2, [], 5)(wt0, wt1, top)


def wave_half(wave_ref, sum_ref, wt, bot, m0):
    for j in range(PAIR):
        m = m0 + j
        wave_ref[m] += jnp.dot(wt[:, N:], bot[m], preferred_element_type=f32)

    def one(i):
        rows = at(i, CHUNK)
        low = at(i, CHUNK, H)
        acc = sum_ref[rows, :]
        for j in range(PAIR):
            a = wave_ref[m0 + j, rows, :]
            b = wave_ref[m0 + j, low, :]
            acc = acc + (a * a + b * b)
        sum_ref[rows, :] = acc

    loop(H // CHUNK, one, 2)


def bottom_body(place, own, rim, p_ref, table, wt, _, half_ref, patch_ref, wave_ref, sum_ref, x_s):
    @pl.when(place[0] == 0)
    def _():
        patch_ref[...] = own[...]

    @pl.when(place[0] != 0)
    def _():
        patch_ref[...] = rim[...]

    sum_ref[...] = jnp.zeros_like(sum_ref)

    def step(m0):
        for j in range(PAIR):
            exit_half(p_ref, m0 + j, j, H, patch_ref, x_s)
        along_rows(x_s, table, half_ref, m0)
        wave_half(wave_ref, sum_ref, wt, half_ref, m0)

    pairs(p_ref.shape[1], step)


def bottom_half(place, own, rim, probe, table, wave_rows, wave):
    nm = probe.shape[1]
    return local_call(
        bottom_body,
        "bottom_half",
        [SCALARS] + [LOCAL] * 6,
        [shape(nm, N, N, dtype=bf16), shape(2, H, N), shape(nm, N, N), shape(H, N)],
        [pltpu.VMEM((PAIR, H, 2 * N), bf16)],
        8,
        {6: 2},
    )(place, own, rim, probe, table, wave_rows, wave)


def low_wave_body(wt, bot, _, wave_ref, sum_ref):
    sum_ref[...] = jnp.zeros_like(sum_ref)
    pairs(bot.shape[0], lambda m0: wave_half(wave_ref, sum_ref, wt, bot, m0))


def low_wave(wave_rows, bot, wave):
    outs = [shape(*wave.shape), shape(H, N)]
    return local_call(low_wave_body, "low_wave", [LOCAL] * 3, outs, [], 5, {2: 0})(wave_rows, bot, wave)


def set_scale(pat, base, s0, s1, scale_s):
    def one(i):
        rows = at(i, CHUNK)
        total = jnp.maximum(s0[rows, :] + s1[rows, :], 1.0)
        scale_s[rows, :] = jnp.sqrt(pat[0, at(i, CHUNK, base), :]) / jnp.sqrt(total)

    loop(H // CHUNK, one)


def fixed_half(wave_ref, table, half_ref, scale_s, x_s, m0):
    for j in range(PAIR):

        def one(i):
            rows = at(i, CHUNK)
            low = at(i, CHUNK, H)
            factor = scale_s[rows, :]
            x_s[j, rows, :N] = (wave_ref[m0 + j, rows, :] * factor).astype(bf16)
            x_s[j, rows, N:] = (wave_ref[m0 + j, low, :] * factor).astype(bf16)

        loop(H // CHUNK, one, 2)
    along_rows(x_s, table, half_ref, m0)


def fixed_top_body(pat, s0, s1, wave_ref, table, half_ref, scale_s, x_s):
    set_scale(pat, 0, s0, s1, scale_s)
    pairs(wave_ref.shape[0], lambda m0: fixed_half(wave_ref, table, half_ref, scale_s, x_s, m0))


SCALE = [pltpu.VMEM((H, N), f32), pltpu.VMEM((PAIR, H, 2 * N), bf16)]


def fixed_top(pat, s0, s1, wave, table):
    nm = wave.shape[0]
    return local_call(
        fixed_top_body, "fixed_top", [LOCAL] * 5, [shape(nm, N, N, dtype=bf16)], SCALE, 6
    )(pat, s0, s1, wave, table)[0]


def gradients(core, block, bt, top, bot, patch_top, patch_bot, p_ref, keep_ref, send_ref, gtop, gbot, back_s, m):
    back_s[...] = jnp.dot(bt[:, :N], top[m], preferred_element_type=f32) + jnp.dot(
        bt[:, N:], bot[m], preferred_element_type=f32
    )
    for patch, g_ref, base in ((patch_top, gtop, 0), (patch_bot, gbot, 8)):

        def one(i):
            g = i + base
            rows = pl.ds(pl.multiple_of(i * 32 + block * 16, 16), 16)
            full = pl.ds(pl.multiple_of(g * 32 + block * 16, 16), 16)
            o_r = patch[0, rows, :]
            o_i = patch[1, rows, :]
            pr, pi, xr, xi = exit_rows(p_ref, m, full, o_r, o_i)
            rr = back_s[at(g, 16), :] - xr.astype(f32)
            ri = back_s[pl.ds(pl.multiple_of(g * 16 + H, 16), 16), :] - xi.astype(f32)
            g_ref[0, i] += pr * rr + pi * ri
            g_ref[1, i] += pr * ri - pi * rr
            st0 = o_r * rr + o_i * ri
            st1 = o_r * ri - o_i * rr
            turned_g = (g % 4) * 4 + g // 4
            keep_ref[m, jnp.where(core == 0, g, turned_g)] = jnp.where(core == 0, st0, st1)
            send_ref[m, jnp.where(core == 0, turned_g, g)] = jnp.where(core == 0, st1, st0)

        loop(8, one, UNROLL)


UNROLL = 8
LIMIT = 4
STAGE = pl.CostEstimate(flops=int(5e9), transcendentals=0, bytes_accessed=int(15e6))
GRADS = [shape(2, 2, 8, 16, N)] * 2


def first_block_body(pat, s0, s1, wave_ref, table, bt, top, ptop, pbot, p_ref, half_ref, keep, send, bots, tops, scale_s, x_s, back_s):
    gtop, gbot = tops.at[0], bots.at[0]
    set_scale(pat, H, s0, s1, scale_s)
    gtop[...] = jnp.zeros_like(gtop)
    gbot[...] = jnp.zeros_like(gbot)

    def step(m0):
        fixed_half(wave_ref, table, half_ref, scale_s, x_s, m0)
        for j in range(PAIR):
            gradients(lax.axis_index("core"), 0, bt, top, half_ref, ptop, pbot, p_ref, keep, send, gtop, gbot, back_s, m0 + j)

    pairs(wave_ref.shape[0], step)


def first_block(pat, s0, s1, wave, table, back_rows, top, ptop, pbot, probe):
    nm = wave.shape[0]
    return local_call(
        first_block_body,
        "first_block",
        [LOCAL] * 10,
        [shape(nm, N, N, dtype=bf16)] + [shape(nm, 16, 16, N)] * 2 + GRADS,
        SCALE + [pltpu.VMEM((N, N), f32)],
        9,
    )(pat, s0, s1, wave, table, back_rows, top, ptop, pbot, probe)


def second_block(back_rows, top, bot, ptop, pbot, probe, first, count, bots, tops, earlier=None):
    nm = top.shape[0]
    given = earlier or []

    def body(bt, top, bot, ptop, pbot, p_ref, *refs):
        keep, send, bots, tops, back_s = refs[2 + len(given) :]
        gtop, gbot = tops.at[1], bots.at[1]
        if not given:
            gtop[...] = jnp.zeros_like(gtop)
            gbot[...] = jnp.zeros_like(gbot)
        core = lax.axis_index("core")
        loop(
            count,
            lambda m: gradients(
                core, 1, bt, top, bot, ptop, pbot, p_ref, keep, send, gtop, gbot, back_s, m + first
            ),
        )

    return local_call(
        body,
        "second_block",
        [LOCAL] * (8 + len(given)),
        [shape(nm, 16, 16, N)] * 2 + GRADS,
        [pltpu.VMEM((N, N), f32)],
        6,
        {6: 2, 7: 3, **{8 + i: i for i in range(len(given))}},
    )(back_rows, top, bot, ptop, pbot, probe, bots, tops, *given)


SCAN = ("y", "z", "x", "core")
RING = ("y", "z", "core")


def along(value, steps):
    count = lax.axis_size(SCAN)
    lo, hi = max(0, -steps), min(count, count - steps)
    return lax.ppermute(value, SCAN, [(i, i + steps) for i in range(lo, hi)])


def swapped(value, axis):
    return lax.ppermute(value, axis, [(0, 1), (1, 0)])


def turned(value, steps, first):
    flat = lambda y, z, core: (y * 4 + z) * 2 + core
    pairs = []
    for y in range(4):
        for z in range(4):
            for core in range(2):
                on_y = (core == 0) == first
                to = ((y + steps) % 4, z) if on_y else (y, (z + steps) % 4)
                pairs.append((flat(y, z, core), flat(*to, core)))
    return lax.ppermute(value, RING, pairs)


def across(value, flip_mode, flip_x):
    pairs = [(2 * m + x, 2 * (m ^ flip_mode) + (x ^ flip_x)) for m in range(2) for x in range(2)]
    return lax.ppermute(value, ("mode", "x"), pairs)


def rim_body(place, obj, out):
    columns = window(place)

    def take(i):
        rows = at(i, CHUNK)
        out[:, rows, :] = obj[:, rows, columns]

    loop(H // CHUNK, take, 2)


def rim_rows(place, obj):
    return local_call(rim_body, "rim_rows", [SCALARS, LOCAL], [shape(2, H, N)], [], LIMIT)(place, obj)[0]


def brightest_body(own, far, out):
    def one(i, acc):
        return jnp.maximum(acc, own[at(i, 8), :] + far[at(i, 8), :])

    out[...] = lax.fori_loop(0, QUARTER // 8, one, jnp.zeros((8, N), f32))


def brightest(own, far):
    outs = [shape(8, N)]
    return local_call(brightest_body, "brightest", [LOCAL, LOCAL], outs, [], LIMIT, cost=STAGE)(own, far)[0]


def core_add_body(keep, recv, own, near, back, far0, far1):
    me = here()[0]
    n2 = own.shape[1]
    for m in range(2 * n2):
        j, k = m // n2, m % n2
        for out, turn in ((own, 0), (near, 1), (back, 3)):
            a = at(lax.rem(me + turn, 4), 4)
            out[j, k] = keep[m, a] + recv[m, a]
        a = at(lax.rem(me + 2, 4), 4)
        (far0, far1)[j][k] = keep[m, a] + recv[m, a]


def core_add(keep, recv):
    n2 = keep.shape[0] // 2
    outs = [shape(2, n2, 4, 16, N)] * 3 + [shape(n2, 4, 16, N)] * 2
    return local_call(core_add_body, "core_add", [LOCAL, LOCAL], outs, [], LIMIT, cost=STAGE)(keep, recv)


def relay_body(a, b, ra, rb, oa, ob):
    oa[0] = a[0] + ra[...]
    ob[1] = b[1] + rb[...]


def relay_add(near, back, ra, rb):
    outs = [shape(*near.shape)] * 2
    return local_call(relay_body, "relay_add", [LOCAL] * 4, outs, [], LIMIT, {0: 0, 1: 1}, cost=STAGE)(near, back, ra, rb)


def plane_add_body(*refs):
    me = here()[1]
    for block in range(2):
        own, ra, rb = refs[3 * block : 3 * block + 3]
        for turn in range(4):
            b = lax.rem(me + turn, 4)
            refs[6 + turn][block] = own[:, :, b] + (ra[:, :, b] + rb[:, :, b])


def plane_add(blocks):
    n2 = blocks[0][0].shape[1]
    outs = [shape(2, 2, n2, 16, N)] * 4
    return local_call(plane_add_body, "plane_add", [LOCAL] * 6, outs, [], LIMIT, cost=STAGE)(
        *blocks[0], *blocks[1]
    )


def line_add_body(most, a, b, c, d, keep, send):
    core = here()[2]
    n2 = a.shape[2]
    for side, out in ((core, keep), (1 - core, send)):
        rows = at(side, 8)
        for block in range(2):
            for j in range(2):
                first = (block * 2 + j) * n2
                out[first : first + n2] = (a[block, j, :, rows] + b[block, j, :, rows]) + (
                    c[block, j, :, rows] + d[block, j, :, rows]
                )
    send[4 * n2] = most[...]


def line_add(most, arrays):
    n2 = arrays[0].shape[2]
    outs = [shape(4 * n2, 8, N), shape(4 * n2 + 1, 8, N)]
    return local_call(line_add_body, "line_add", [LOCAL] * 5, outs, [], LIMIT, cost=STAGE)(most, *arrays)


def pixel_body(most, keep, recv, rows, mine, other):
    core, x = here()[2:4]
    scale = 1.0 / math.sqrt(64)
    nm = rows.shape[1]

    def fill(part, ref):
        mine[part] = ref[pl.ds(x * nm, nm)] * scale + rows[part]
        other[pl.ds(part * nm, nm)] = ref[pl.ds((1 - x) * nm, nm)] * scale

    @pl.when(core == 0)
    def _():
        fill(0, keep)
        fill(1, recv)

    @pl.when(core != 0)
    def _():
        fill(0, recv)
        fill(1, keep)

    other[2 * nm] = jnp.maximum(most[...], recv[2 * nm])


def pixel_step(most, keep, recv, rows):
    nm = rows.shape[1]
    outs = [shape(2, nm, 8, N), shape(2 * nm + 1, 8, N)]
    return local_call(pixel_body, "pixel_step", [LOCAL] * 4, outs, [], LIMIT, cost=STAGE)(most, keep, recv, rows)


def mix_body(w_ref, mine, b, c, d, out_ref):
    mode = here()[4]
    nm = mine.shape[1]
    for part in range(2):
        own = [mine[part, j] + b[part * nm + j] for j in range(nm)]
        far = [c[part, j] + d[part * nm + j] for j in range(nm)]
        for k in range(nm):
            row = mode * nm + k
            acc = jnp.zeros((8, N), f32)
            for j in range(nm):
                acc += (w_ref[row, mode * nm + j].astype(f32) / 16.0) * own[j]
                acc += (w_ref[row, (1 - mode) * nm + j].astype(f32) / 16.0) * far[j]
            out_ref[part, k] = acc.astype(bf16)


def mix(mixing, mine, b, c, d):
    outs = [shape(*mine.shape, dtype=bf16)]
    return local_call(mix_body, "mix", [SCALARS] + [LOCAL] * 4, outs, [], LIMIT)(mixing, mine, b, c, d)[0]


def object_body(place, before, near_max, far_max, obj, t, tf, b, bf, over, out, new, sems):
    shift, col = place[0], pl.multiple_of(place[1] * H, H)
    over_shift, over_col = before[0], pl.multiple_of(before[1] * H, H)
    last = near_max.shape[0] - 1
    largest = jnp.max(jnp.maximum(near_max[last], far_max[last]))
    copies = []
    for half in range(2):
        base = half * H

        def start(i):
            rows = at(i, CHUNK, base)
            new[:, rows, :] = obj[:, rows, :]

        loop(H // CHUNK, start, 2)

        def add(column, even, odd):
            def one(g):
                for block, values in ((0, even), (1, odd)):
                    rows = pl.ds(pl.multiple_of(g * 32 + base + block * 16, 16), 16)
                    total = values[0][:, g]
                    for v in values[1:]:
                        total = total + v[:, g]
                    new[:, rows, pl.ds(column, N)] += total / largest

            loop(8, one, 2)

        @pl.when(shift == half)
        def _():
            add(col, (t.at[0], tf.at[0]), (t.at[1], tf.at[1]))

        if half == 1:

            @pl.when(shift == 0)
            def _():
                add(col, (b.at[0], bf.at[0]), (b.at[1], bf.at[1]))

        else:

            @pl.when(over_shift == 1)
            def _():
                add(over_col, (over.at[0],), (over.at[1],))

        copy = pltpu.make_async_copy(new.at[:, pl.ds(base, H), :], out.at[:, pl.ds(base, H), :], sems.at[half])
        copy.start()
        copies.append(copy)
    for copy in copies:
        copy.wait()


def object_update(place, before, near_max, far_max, obj, pieces, over):
    return pl.pallas_call(
        object_body,
        in_specs=[SCALARS] * 2 + [LOCAL] * 8,
        out_specs=FAR,
        out_shape=shape(2, N, 4 * H),
        scratch_shapes=[pltpu.VMEM((2, N, 4 * H), f32), pltpu.SemaphoreType.DMA((2,))],
        compiler_params=params(10),
        name="object_update",
    )(place, before, near_max, far_max, obj, *pieces, over)


def over_body(g, gf, out):
    out[...] = g[...] + gf[...]


def over_sum(grads, far):
    outs = [shape(2, 2, 8, 16, N)]
    return local_call(over_body, "over_sum", [LOCAL] * 2, outs, [], LIMIT, cost=STAGE)(grads, far)[0]


def tied(*values):
    return lax.optimization_barrier(values)


def per_device(object_field, probe, patterns, row_shift, col_start, mixing):
    minus, plus, wave_top_rows, wave_bot_rows, back_rows0, back_rows1 = tables()
    place = jnp.concatenate([row_shift, col_start])
    before = along(place, 1)
    patch_top, own_bot, first_rows = own_rows(place, object_field)
    before, patch_top = tied(before, patch_top)
    rim = along(rim_rows(before, first_rows), -1)
    half_top, own_light, light_out, rows = top_half(patch_top, probe, minus)
    wave_top, wave_bot = first_terms(wave_top_rows, wave_bot_rows, half_top)
    rim, wave_top, light_out = tied(rim, wave_top, light_out)
    far_light = swapped(light_out, "mode")
    half_bot, patch_bot, wave_top, sum_top = bottom_half(
        place, own_bot, rim, probe, minus, wave_top_rows, wave_top
    )
    far_top = swapped(sum_top, "mode")
    half_bot, far_light = tied(half_bot, far_light)
    wave_bot, sum_bot = low_wave(wave_bot_rows, half_bot, wave_bot)
    far_bot = swapped(sum_bot, "mode")
    fixed = fixed_top(patterns, sum_top, far_top, wave_top, plus)
    low, keep0, send0, bots, tops = first_block(
        patterns, sum_bot, far_bot, wave_bot, plus, back_rows0, fixed, patch_top, patch_bot, probe
    )
    most = brightest(own_light, far_light)
    recv0 = swapped(send0, "core")
    *part1, bots, tops = second_block(back_rows1, fixed, low, patch_top, patch_bot, probe, 0, 3, bots, tops)
    own0, near0, back0, far0a, far0b = core_add(keep0, recv0)
    ra0, rb0 = turned(far0a, 1, True), turned(far0b, -1, True)
    *part1, near0 = tied(*part1, near0)
    keep1, send1, bots, tops = second_block(
        back_rows1, fixed, low, patch_top, patch_bot, probe, 3, 3, bots, tops, part1
    )
    bots_far = swapped(bots, "mode")
    recv1 = swapped(send1, "core")
    near0, back0 = relay_add(near0, back0, ra0, rb0)
    keep1, _ = tied(keep1, near0)
    own1, near1, back1, far1a, far1b = core_add(keep1, recv1)
    ra1, rb1 = turned(far1a, 1, True), turned(far1b, -1, True)
    plane0 = (own0, turned(near0, 1, True), turned(back0, -1, True))
    ra1, rb1, bots_far, *plane0 = tied(ra1, rb1, bots_far, *plane0)
    near1, back1 = relay_add(near1, back1, ra1, rb1)
    plane1 = (own1, turned(near1, 1, True), turned(back1, -1, True))
    over = along(over_sum(bots, bots_far), 1)
    *plane1, over = tied(*plane1, over)
    tops_next, _ = tied(tops, over)
    tops_far = swapped(tops_next, "mode")
    line = plane_add((plane0, plane1))
    line = [line[0]] + [turned(line[r], r, False) for r in (1, 3, 2)]
    keep, send = line_add(most, line)
    recv = swapped(send, "core")
    mine, other = pixel_step(most, keep, recv, rows)
    beside = across(other, 0, 1)
    beside, tops_far = tied(beside, tops_far)
    probe_new = mix(mixing, mine, beside, across(mine, 1, 0), across(other, 1, 1))
    object_new = object_update(place, before, other, beside, object_field, (tops, tops_far, bots, bots_far), over)
    return object_new, probe_new


def solution(mesh):
    split = Mesh(mesh.devices.reshape(2, 4, 4, 2, 2), ("mode", *SCAN))
    return jax.shard_map(
        per_device,
        mesh=split,
        in_specs=(P(None, SCAN, None), P(None, "mode", None, None), P(SCAN, None, None), P(SCAN), P(SCAN), P()),
        out_specs=(P(None, SCAN, None), P(None, "mode", SCAN, None)),
        check_vma=False,
    )
```
